256 devices in a mesh: req: 32 (over z, y), head: 8 (over x, core).
Axes of the slice: x: 4, y: 4, z: 8, core: 2. Of those that a mesh axis runs over, the one named last changes fastest.
Arguments:
- hidden: bfloat16 [512, 2048], P('req'), may hold values from -6 to 6
- deal_order: int32 [512], replicated, may hold values from 0 to 511, each once
- lengths: int32 [512], replicated, may hold values from 1 to 8192, as said below
- page_table: int32 [512, 64], replicated, may hold values from 0 to 2047, as said below
- key_cache: bfloat16 [2048, 128, 8, 128], P('req', None, 'head'), as said below
- value_cache: bfloat16 [2048, 128, 8, 128], P('req', None, 'head'), may hold values from -12 to 12
- attn_gain: float32 [2048], replicated, may hold values from 0.1 to 1.9
- w_query: bfloat16 [2048, 2048], P(None, 'head'), may hold values from -0.125 to 0.125
- w_key: bfloat16 [2048, 1024], P(None, 'head'), may hold values from -0.125 to 0.125
- w_value: bfloat16 [2048, 1024], P(None, 'head'), may hold values from -0.125 to 0.125
- w_gate: bfloat16 [2048, 2048], P(None, 'head'), may hold values from -0.125 to 0.125
- w_out: bfloat16 [2048, 2048], P('head'), may hold values from -1.5 to 1.5
- query_gain: float32 [128], replicated, may hold values from 0.5 to 2
- key_gain: float32 [128], replicated, may hold values from 0.5 to 2
- mlp_gain: float32 [2048], replicated, may hold values from 0.1 to 1.9
- mlp_gate: bfloat16 [2048, 3072], P(None, 'head'), may hold values from -0.125 to 0.125
- mlp_up: bfloat16 [2048, 3072], P(None, 'head'), may hold values from -0.125 to 0.125
- mlp_down: bfloat16 [3072, 2048], P('head'), may hold values from -0.109375 to 0.109375
Outputs:
- output: bfloat16 [512, 2048], P('req')
The draws below stay inside these ranges and needn't reach their ends.
Inputs may be any that keep to these rules, and one draw needn't show every extreme that they name: `lengths`: one request holds exactly 8192 cached tokens, and all requests together fill at most 2048 pages of 128 tokens. `page_table`: for request r the first ceil(lengths[r] / 128) entries of row r name, in order, the pages that hold its cached tokens; no page is named by two such entries; the other entries are arbitrary page numbers. `key_cache`: cached keys; entries lie within -402 and 402.
All inputs are finite; a program needn't handle non-finite values.
Results may differ from the reference program's by a relative error of at most 0.022.
Values may be sent and summed in bfloat16 or wider, within the bound.
A program may use at most 64 MiB of HBM per device.

```python
import math
import jax
import jax.numpy as jnp
from jax import lax

D = 2048
HD = 128
KVH = 8
GROUP = 2
QH = 16
FF = 3072
PAGE = 128
MAXP = 64
MAXLEN = 8192
POOL_DEV = 64
B = 512
POOL = 2048


def allocation(key):
    base_key = jax.random.fold_in(key, 7)
    keys_list = jax.random.split(base_key, 7)
    exponent = jnp.minimum(jax.random.randint(keys_list[0], (B,), 4, 14), jax.random.randint(keys_list[1], (B,), 4, 14)).astype(jnp.int32)
    span_top = jnp.minimum(jnp.left_shift(jnp.ones((B,), jnp.int32), exponent), MAXLEN)
    raw_length = jax.random.randint(keys_list[2], (B,), 1, span_top + 1).astype(jnp.int32)
    forced = jax.random.randint(keys_list[3], (), 0, B)
    is_forced = jnp.arange(B, dtype=jnp.int32) == forced
    raw_length = jnp.where(is_forced, MAXLEN, raw_length)
    extra_pages = (raw_length + PAGE - 1) // PAGE - 1
    others = jnp.where(is_forced, 0, extra_pages)
    before = jnp.cumsum(others) - others + (MAXP - 1)
    allowed = jnp.clip(POOL - B - before, 0, others)
    allowed = jnp.where(is_forced, MAXP - 1, allowed)
    length_final = jnp.minimum(raw_length, (allowed + 1) * PAGE).astype(jnp.int32)
    page_counts = (allowed + 1).astype(jnp.int32)
    first_page = jnp.cumsum(page_counts) - page_counts
    device_bias = jax.random.randint(keys_list[4], (POOL // POOL_DEV,), 0, 16).astype(jnp.int32)
    noise_rank = jax.random.randint(keys_list[5], (POOL,), 0, 256).astype(jnp.int32)
    page_ids = jnp.arange(POOL, dtype=jnp.int32)
    ranking = (device_bias[page_ids // POOL_DEV] * 256 + noise_rank) * POOL + page_ids
    free_list = jnp.argsort(ranking).astype(jnp.int32)
    slot_ids = jnp.arange(MAXP, dtype=jnp.int32)
    used_slots = slot_ids[None, :] < page_counts[:, None]
    position_list = jnp.minimum(first_page[:, None] + slot_ids[None, :], POOL - 1)
    filler = jax.random.randint(keys_list[6], (B, MAXP), 0, POOL).astype(jnp.int32)
    table = jnp.where(used_slots, free_list[position_list], filler).astype(jnp.int32)
    return (length_final, table)


def draw_lengths(key, part):
    return allocation(key)[0]


def draw_page_table(key, part):
    return allocation(key)[1]


def draw_key_cache(key, part):
    keys_list = jax.random.split(jax.random.fold_in(key, 11), 1)
    entries = jnp.clip(jax.random.normal(keys_list[0], (POOL, PAGE, KVH, HD), jnp.float32), -6.0, 6.0)
    return entries.astype(jnp.bfloat16)


def block_scale(key, extent, pieces, smallest, high):
    factor_of, own = 1.0, jax.random.fold_in(key, 6)
    for dim, blocks in pieces:
        heights = jnp.exp(jax.random.uniform(jax.random.fold_in(own, dim), (blocks,), jnp.float32, smallest / len(pieces), high / len(pieces)))
        factor_of = factor_of * jnp.repeat(heights, extent[dim] // blocks).reshape([-1 if axis == dim else 1 for axis in range(len(extent))])
    return factor_of


def noise(stream_key, shape, scale, limit, cuts=(), held_as=jnp.bfloat16):
    level = block_scale(stream_key, shape, cuts, -0.22, 0.18) if cuts else 1.0
    array = jax.random.normal(stream_key, shape, jnp.float32) * scale * level
    return jnp.minimum(jnp.maximum(array, -limit), limit).astype(held_as)


def setup_inputs(seed: int = 0) -> dict:
    arg_keys = jax.random.split(jax.random.key(seed), 19)
    hidden = noise(arg_keys[0], (B, D), 1.0, 6.0, ((0, 32),))
    deal_order = jax.random.permutation(arg_keys[1], B).astype(jnp.int32)
    lengths = draw_lengths(jax.random.fold_in(arg_keys[18], 71), 0)
    page_table = draw_page_table(jax.random.fold_in(arg_keys[18], 71), 0)
    key_cache = draw_key_cache(jax.random.fold_in(arg_keys[18], 71), 0)
    value_cache = noise(arg_keys[5], (POOL, PAGE, KVH, HD), 2.0, 12.0, ((0, 32), (2, 8)))
    attn_gain = jnp.clip(1.0 + 0.18 * jax.random.normal(arg_keys[6], (D,), jnp.float32), 0.1, 1.9)
    w_query = noise(arg_keys[7], (D, QH * HD), D ** -0.5, 0.125, ((1, 8),))
    w_key = noise(arg_keys[8], (D, KVH * HD), D ** -0.5, 0.125, ((1, 8),))
    w_value = noise(arg_keys[9], (D, KVH * HD), D ** -0.5, 0.125, ((1, 8),))
    w_gate = noise(arg_keys[10], (D, QH * HD), D ** -0.5, 0.125, ((1, 8),))
    w_out = noise(arg_keys[11], (QH * HD, D), 16 ** -0.5, 1.5, ((0, 8),))
    query_gain = jnp.clip(jnp.exp(jax.random.uniform(arg_keys[12], (HD,), jnp.float32, math.log(0.5), math.log(2.0))), 0.5, 2.0)
    key_gain = jnp.clip(jnp.exp(jax.random.uniform(arg_keys[13], (HD,), jnp.float32, math.log(0.5), math.log(2.0))), 0.5, 2.0)
    mlp_gain = jnp.clip(1.0 + 0.18 * jax.random.normal(arg_keys[14], (D,), jnp.float32), 0.1, 1.9)
    mlp_gate = noise(arg_keys[15], (D, FF), D ** -0.5, 0.125, ((1, 8),))
    mlp_up = noise(arg_keys[16], (D, FF), D ** -0.5, 0.125, ((1, 8),))
    mlp_down = noise(arg_keys[17], (FF, D), FF ** -0.5, 0.109375, ((0, 8),))
    return dict(hidden=hidden, deal_order=deal_order, lengths=lengths, page_table=page_table, key_cache=key_cache, value_cache=value_cache, attn_gain=attn_gain, w_query=w_query, w_key=w_key, w_value=w_value, w_gate=w_gate, w_out=w_out, query_gain=query_gain, key_gain=key_gain, mlp_gain=mlp_gain, mlp_gate=mlp_gate, mlp_up=mlp_up, mlp_down=mlp_down)


EPSILON = 1e-06
ROPE_BASE = 1000000.0
LOW_SCORE = -1e+30
LOG_TWO = math.log(2.0)

def rms_inv(values):
    return lax.rsqrt(lax.optimization_barrier(jnp.mean(values * values, axis=-1, keepdims=True)) + EPSILON)

def rotate(values, position):
    half_dim = values.shape[-1] // 2
    exponent = jnp.arange(half_dim, dtype=jnp.float32) * (2.0 / values.shape[-1])
    frequency = ROPE_BASE ** (-exponent)
    angles = position[:, None] * frequency[None, :]
    ones_tail = (1,) * (values.ndim - 2)
    angles = angles.reshape((angles.shape[0],) + ones_tail + (half_dim,))
    cosine = jnp.cos(angles)
    sine_vals = jnp.sin(angles)
    front_half = values[..., :half_dim]
    back_half = values[..., half_dim:]
    return jnp.concatenate([front_half * cosine - back_half * sine_vals, back_half * cosine + front_half * sine_vals], axis=-1)

def norm_rotate(values, gain_vec, position):
    return rotate(values * rms_inv(values) * gain_vec, position)

def reference(hidden, deal_order, lengths, page_table, key_cache, value_cache, attn_gain, w_query, w_key, w_value, w_gate, w_out, query_gain, key_gain, mlp_gain, mlp_gate, mlp_up, mlp_down):
    scale_factor = 1.0 / math.sqrt(HD)
    hidden_f = hidden.astype(jnp.float32)
    normed = (hidden_f * rms_inv(hidden_f) * attn_gain).astype(jnp.bfloat16)
    dealt_lengths = lengths[deal_order]
    position = dealt_lengths.astype(jnp.float32)
    queries = jnp.dot(normed, w_query, preferred_element_type=jnp.float32).reshape(B, KVH, GROUP, HD)
    queries = norm_rotate(queries, query_gain, position).astype(jnp.bfloat16)
    new_keys = jnp.dot(normed, w_key, preferred_element_type=jnp.float32).reshape(B, KVH, HD)
    new_keys = norm_rotate(new_keys, key_gain, position).astype(jnp.bfloat16)
    new_values = jnp.dot(normed, w_value, preferred_element_type=jnp.float32).astype(jnp.bfloat16).reshape(B, KVH, HD)
    gate_logits = jnp.dot(normed, w_gate, preferred_element_type=jnp.float32)
    dealt_tables = page_table[deal_order]

    def attend(items):
        query_row, key_new, value_new, table_row, length_row = items
        keys_all = key_cache[table_row].reshape(MAXP * PAGE, KVH, HD).astype(jnp.float32)
        values_all = value_cache[table_row].reshape(MAXP * PAGE, KVH, HD).astype(jnp.float32)
        query_f = query_row.astype(jnp.float32)
        scores = jnp.einsum('kgd,tkd->kgt', query_f, keys_all, precision=lax.Precision.HIGHEST) * scale_factor
        live_mask = jnp.arange(MAXP * PAGE, dtype=jnp.int32) < length_row
        scores = jnp.where(live_mask, scores, LOW_SCORE)
        self_score = jnp.einsum('kgd,kd->kg', query_f, key_new.astype(jnp.float32), precision=lax.Precision.HIGHEST) * scale_factor
        peak_score = jnp.maximum(lax.optimization_barrier(jnp.max(scores, axis=-1)), self_score)
        shift = LOG_TWO * jnp.ceil(peak_score / LOG_TWO)
        weights = jnp.where(live_mask, jnp.exp(scores - shift[..., None]), 0.0)
        self_weight = jnp.exp(self_score - shift)
        totals = lax.optimization_barrier(jnp.sum(weights, axis=-1)) + self_weight
        rounded = lax.optimization_barrier(weights.astype(jnp.bfloat16)).astype(jnp.float32)
        self_rounded = lax.optimization_barrier(self_weight.astype(jnp.bfloat16)).astype(jnp.float32)
        numerators = jnp.einsum('kgt,tkd->kgd', rounded, values_all, precision=lax.Precision.HIGHEST)
        numerators = numerators + self_rounded[..., None] * value_new.astype(jnp.float32)[:, None, :]
        return numerators / totals[..., None]
    heads_out = lax.map(attend, (queries, new_keys, new_values, dealt_tables, dealt_lengths))
    attended = (heads_out.reshape(B, QH * HD) * jax.nn.sigmoid(gate_logits)).astype(jnp.bfloat16)
    mixed_rows = (hidden_f + jnp.dot(attended, w_out, preferred_element_type=jnp.float32)).astype(jnp.bfloat16)
    mixed_f = mixed_rows.astype(jnp.float32)
    normed_two = (mixed_f * rms_inv(mixed_f) * mlp_gain).astype(jnp.bfloat16)
    gate_part = jnp.dot(normed_two, mlp_gate, preferred_element_type=jnp.float32)
    up_part = jnp.dot(normed_two, mlp_up, preferred_element_type=jnp.float32)
    inner_act = (jax.nn.silu(gate_part) * up_part).astype(jnp.bfloat16)
    result = (mixed_f + jnp.dot(inner_act, mlp_down, preferred_element_type=jnp.float32)).astype(jnp.bfloat16)
    return jnp.zeros_like(result).at[deal_order].set(result)
```

```python
import functools
import math

import jax
import jax.numpy as jnp
from jax import lax
from jax.experimental import pallas as pl
from jax.experimental.pallas import tpu as pltpu
from jax.sharding import PartitionSpec as P

EPSILON = 1e-06
ROPE_BASE = 1000000.0
LOW_SCORE = -1e30
LOG_TWO = math.log(2.0)
MESH_IDS = pl.DeviceIdType.MESH


def rms_inv(values):
    return lax.rsqrt(jnp.mean(values * values, axis=-1, keepdims=True) + EPSILON)


def rotate(values, position):
    half_dim = values.shape[-1] // 2
    exponent = jnp.arange(half_dim, dtype=jnp.float32) * (2.0 / values.shape[-1])
    frequency = ROPE_BASE ** (-exponent)
    angles = position[:, None] * frequency[None, :]
    ones_tail = (1,) * (values.ndim - 2)
    angles = angles.reshape((angles.shape[0],) + ones_tail + (half_dim,))
    cosine = jnp.cos(angles)
    sine_vals = jnp.sin(angles)
    front_half = values[..., :half_dim]
    back_half = values[..., half_dim:]
    return jnp.concatenate(
        [front_half * cosine - back_half * sine_vals, back_half * cosine + front_half * sine_vals],
        axis=-1,
    )


def norm_rotate(values, gain_vec, position):
    return rotate(values * rms_inv(values) * gain_vec, position)


def exchange_kernel(axis, count, spread, src_ref, out_ref, send_sems, recv_sems):
    me = lax.axis_index(axis)
    barrier = pltpu.get_barrier_semaphore()
    for offset in range(1, count):
        peer = lax.rem(me + offset, count)
        pl.semaphore_signal(barrier, inc=1, device_id={axis: peer}, device_id_type=MESH_IDS)
    pl.semaphore_wait(barrier, count - 1)
    copies = []
    for offset in range(1, count):
        peer = lax.rem(me + offset, count)
        copy = pltpu.make_async_remote_copy(
            src_ref=src_ref.at[peer] if spread else src_ref,
            dst_ref=out_ref.at[me],
            send_sem=send_sems.at[offset],
            recv_sem=recv_sems.at[offset],
            device_id={axis: peer},
            device_id_type=MESH_IDS,
        )
        copy.start()
        copies.append(copy)
    out_ref[me] = src_ref[me] if spread else src_ref[...]
    for copy in copies:
        copy.wait()


def exchange(values, axis, count, spread, ident):
    block = values.shape[1:] if spread else values.shape
    return pl.pallas_call(
        functools.partial(exchange_kernel, axis, count, spread),
        out_shape=jax.ShapeDtypeStruct((count,) + tuple(block), values.dtype),
        in_specs=[pl.BlockSpec(memory_space=pltpu.VMEM)],
        out_specs=pl.BlockSpec(memory_space=pltpu.VMEM),
        scratch_shapes=[pltpu.SemaphoreType.DMA((count,)), pltpu.SemaphoreType.DMA((count,))],
        compiler_params=pltpu.CompilerParams(collective_id=ident, has_side_effects=True),
    )(values)


def body(
    req_count,
    head_count,
    hidden,
    deal_order,
    lengths,
    page_table,
    key_cache,
    value_cache,
    attn_gain,
    w_query,
    w_key,
    w_value,
    w_gate,
    w_out,
    query_gain,
    key_gain,
    mlp_gain,
    mlp_gate,
    mlp_up,
    mlp_down,
):
    local_rows, model_width = hidden.shape
    req_index = lax.axis_index("req")
    head_index = lax.axis_index("head")
    all_rows = local_rows * req_count
    head_width = query_gain.shape[0]
    pool_pages, page_size, local_kv = key_cache.shape[:3]
    group_size = w_query.shape[1] // (local_kv * head_width)
    head_cols = local_kv * group_size * head_width
    pairs = local_kv * group_size
    chunk = model_width // head_count
    scale_factor = 1.0 / math.sqrt(head_width)
    first_own = req_index * local_rows

    with jax.named_scope("projections"):
        hidden_f = hidden.astype(jnp.float32)
        normed = (hidden_f * rms_inv(hidden_f) * attn_gain).astype(jnp.bfloat16)
        own_requests = lax.dynamic_slice_in_dim(deal_order, first_own, local_rows)
        position = lengths[own_requests].astype(jnp.float32)
        queries = jnp.dot(normed, w_query, preferred_element_type=jnp.float32).reshape(
            local_rows, local_kv, group_size, head_width
        )
        queries = norm_rotate(queries, query_gain, position).astype(jnp.bfloat16)
        new_keys = jnp.dot(normed, w_key, preferred_element_type=jnp.float32).reshape(
            local_rows, local_kv, head_width
        )
        new_keys = norm_rotate(new_keys, key_gain, position).astype(jnp.bfloat16)
        new_values = (
            jnp.dot(normed, w_value, preferred_element_type=jnp.float32)
            .astype(jnp.bfloat16)
            .reshape(local_rows, local_kv, head_width)
        )
        gate_logits = jnp.dot(normed, w_gate, preferred_element_type=jnp.float32)

    all_queries = exchange(queries.reshape(local_rows, head_cols), "req", req_count, False, 0)
    all_queries = all_queries.reshape(all_rows, head_cols)

    with jax.named_scope("page_owners"):
        dealt_lengths = lengths[deal_order]
        dealt_tables = page_table[deal_order]
        page_counts = (dealt_lengths + page_size - 1) // page_size
        slot_ids = jnp.arange(dealt_tables.shape[1], dtype=jnp.int32)
        local_ids = dealt_tables - req_index * pool_pages
        usable = (
            (slot_ids[None, :] < page_counts[:, None]) & (local_ids >= 0) & (local_ids < pool_pages)
        )
        keyed = jnp.where(usable, local_ids, pool_pages)
        page_ids = jnp.arange(pool_pages, dtype=jnp.int32)
        match = keyed[None, :, :] == page_ids[:, None, None]
        owned = jnp.any(match, axis=2)
        owner_slot = jnp.sum(jnp.where(match, slot_ids[None, None, :], 0), axis=(1, 2))
        owner_length = jnp.sum(jnp.where(owned, dealt_lengths[None, :], 0), axis=1)
        filled = jnp.clip(owner_length - owner_slot * page_size, 0, page_size)
        filled = jnp.where(jnp.any(owned, axis=1), filled, 0)
        page_queries = (
            jnp.dot(owned.astype(jnp.bfloat16), all_queries, preferred_element_type=jnp.float32)
            .astype(jnp.bfloat16)
            .reshape(pool_pages, local_kv, group_size, head_width)
        )

    with jax.named_scope("page_attention"):
        scores = (
            jnp.einsum("pkgd,ptkd->pkgt", page_queries, key_cache, preferred_element_type=jnp.float32)
            * scale_factor
        )
        live_mask = (
            jnp.arange(page_size, dtype=jnp.int32)[None, None, None, :] < filled[:, None, None, None]
        )
        scores = jnp.where(live_mask, scores, LOW_SCORE)
        page_peaks = jnp.max(scores, axis=-1)
        owned_b = owned[:, :, None, None]
        row_peaks = jnp.max(jnp.where(owned_b, page_peaks[:, None], LOW_SCORE), axis=0)
        row_shift = LOG_TWO * jnp.ceil(row_peaks / LOG_TWO)
        page_shift = jnp.max(jnp.where(owned_b, row_shift[None], LOW_SCORE), axis=1)
        weights = jnp.where(live_mask, jnp.exp(scores - page_shift[..., None]), 0.0)
        page_totals = jnp.sum(weights, axis=-1)
        page_numerators = jnp.einsum(
            "pkgt,ptkd->pkgd",
            weights.astype(jnp.bfloat16),
            value_cache,
            preferred_element_type=jnp.float32,
        )
        owned_f = owned.astype(jnp.float32)
        row_totals = jnp.dot(
            owned_f.T, page_totals.reshape(pool_pages, pairs), precision=lax.Precision.HIGHEST
        )
        row_numerators = jnp.dot(
            owned_f.T,
            page_numerators.reshape(pool_pages, head_cols),
            precision=lax.Precision.HIGHEST,
        )
        pad = (-(head_cols + 2 * pairs)) % 128
        message = jnp.concatenate(
            [
                row_numerators,
                row_shift.reshape(all_rows, pairs),
                row_totals,
                jnp.zeros((all_rows, pad), jnp.float32),
            ],
            axis=1,
        ).reshape(req_count, local_rows, -1)

    arrived = exchange(message, "req", req_count, True, 1)

    with jax.named_scope("combine"):
        got_numerators = arrived[:, :, :head_cols].reshape(
            req_count, local_rows, local_kv, group_size, head_width
        )
        got_shift = arrived[:, :, head_cols : head_cols + pairs].reshape(
            req_count, local_rows, local_kv, group_size
        )
        got_totals = arrived[:, :, head_cols + pairs : head_cols + 2 * pairs].reshape(
            req_count, local_rows, local_kv, group_size
        )
        self_scores = (
            jnp.einsum("rkgd,rkd->rkg", queries, new_keys, preferred_element_type=jnp.float32)
            * scale_factor
        )
        self_shift = LOG_TWO * jnp.ceil(self_scores / LOG_TWO)
        shift = jnp.maximum(jnp.max(got_shift, axis=0), self_shift)
        factor = jnp.exp(got_shift - shift[None])
        self_weight = jnp.exp(self_scores - shift)
        totals = jnp.sum(got_totals * factor, axis=0) + self_weight
        self_rounded = self_weight.astype(jnp.bfloat16).astype(jnp.float32)
        numerators = (
            jnp.sum(got_numerators * factor[..., None], axis=0)
            + self_rounded[..., None] * new_values.astype(jnp.float32)[:, :, None, :]
        )
        heads_out = (numerators / totals[..., None]).reshape(local_rows, head_cols)
        attended = (heads_out * jax.nn.sigmoid(gate_logits)).astype(jnp.bfloat16)
        projected = jnp.dot(attended, w_out, preferred_element_type=jnp.float32)
        projected = projected.reshape(local_rows, head_count, chunk).transpose(1, 0, 2)

    attn_parts = exchange(projected, "head", head_count, True, 2)

    with jax.named_scope("residual"):
        hidden_chunk = lax.dynamic_slice_in_dim(hidden_f, head_index * chunk, chunk, axis=1)
        mixed_chunk = (hidden_chunk + jnp.sum(attn_parts, axis=0)).astype(jnp.bfloat16)

    mixed_all = exchange(mixed_chunk, "head", head_count, False, 3)

    with jax.named_scope("mlp"):
        mixed_rows = mixed_all.transpose(1, 0, 2).reshape(local_rows, model_width)
        mixed_f = mixed_rows.astype(jnp.float32)
        normed_two = (mixed_f * rms_inv(mixed_f) * mlp_gain).astype(jnp.bfloat16)
        gate_part = jnp.dot(normed_two, mlp_gate, preferred_element_type=jnp.float32)
        up_part = jnp.dot(normed_two, mlp_up, preferred_element_type=jnp.float32)
        inner_act = (jax.nn.silu(gate_part) * up_part).astype(jnp.bfloat16)
        down_part = jnp.dot(inner_act, mlp_down, preferred_element_type=jnp.float32)
        down_part = down_part.reshape(local_rows, head_count, chunk).transpose(1, 0, 2)

    mlp_parts = exchange(down_part, "head", head_count, True, 4)

    with jax.named_scope("result"):
        result_chunk = (mixed_chunk.astype(jnp.float32) + jnp.sum(mlp_parts, axis=0)).astype(
            jnp.bfloat16
        )

    result_all = exchange(result_chunk, "req", req_count, False, 5).reshape(all_rows, chunk)

    with jax.named_scope("reorder"):
        wanted = first_own + jnp.arange(local_rows, dtype=jnp.int32)
        selector = (deal_order[None, :] == wanted[:, None]).astype(jnp.bfloat16)
        picked = jnp.dot(selector, result_all, preferred_element_type=jnp.float32).astype(
            jnp.bfloat16
        )

    output_parts = exchange(picked, "head", head_count, False, 6)
    return output_parts.transpose(1, 0, 2).reshape(local_rows, model_width)


def solution(mesh):
    return jax.shard_map(
        functools.partial(body, mesh.shape["req"], mesh.shape["head"]),
        mesh=mesh,
        in_specs=(
            P("req", None),
            P(),
            P(),
            P(),
            P("req", None, "head", None),
            P("req", None, "head", None),
            P(),
            P(None, "head"),
            P(None, "head"),
            P(None, "head"),
            P(None, "head"),
            P("head", None),
            P(),
            P(),
            P(),
            P(None, "head"),
            P(None, "head"),
            P("head", None),
        ),
        out_specs=P("req", None),
        check_vma=False,
    )
```

```python
import functools
import math

import jax
import jax.numpy as jnp
from jax import lax
from jax.experimental import pallas as pl
from jax.experimental.pallas import tpu as pltpu
from jax.sharding import PartitionSpec as P

EPSILON = 1e-06
ROPE_BASE = 1000000.0
LOW_SCORE = -1e30
LOG_TWO = math.log(2.0)
MESH_IDS = pl.DeviceIdType.MESH


def rms_inv(values):
    return lax.rsqrt(jnp.mean(values * values, axis=-1, keepdims=True) + EPSILON)


def rotate(values, position):
    half_dim = values.shape[-1] // 2
    exponent = jnp.arange(half_dim, dtype=jnp.float32) * (2.0 / values.shape[-1])
    frequency = ROPE_BASE ** (-exponent)
    angles = position[:, None] * frequency[None, :]
    ones_tail = (1,) * (values.ndim - 2)
    angles = angles.reshape((angles.shape[0],) + ones_tail + (half_dim,))
    cosine = jnp.cos(angles)
    sine_vals = jnp.sin(angles)
    front_half = values[..., :half_dim]
    back_half = values[..., half_dim:]
    return jnp.concatenate(
        [front_half * cosine - back_half * sine_vals, back_half * cosine + front_half * sine_vals],
        axis=-1,
    )


def norm_rotate(values, gain_vec, position):
    return rotate(values * rms_inv(values) * gain_vec, position)


def exchange_kernel(axis, count, spreads, *refs):
    arrays = len(spreads)
    sources, outputs = refs[:arrays], refs[arrays : 2 * arrays]
    send_sems, recv_sems = refs[2 * arrays], refs[2 * arrays + 1]
    me = lax.axis_index(axis)
    barrier = pltpu.get_barrier_semaphore()
    for offset in range(1, count):
        peer = lax.rem(me + offset, count)
        pl.semaphore_signal(barrier, inc=1, device_id={axis: peer}, device_id_type=MESH_IDS)
    pl.semaphore_wait(barrier, count - 1)
    copies = []
    for offset in range(1, count):
        peer = lax.rem(me + offset, count)
        for which in range(arrays):
            src_ref, out_ref = sources[which], outputs[which]
            copy = pltpu.make_async_remote_copy(
                src_ref=src_ref.at[peer] if spreads[which] else src_ref,
                dst_ref=out_ref.at[me],
                send_sem=send_sems.at[which, offset],
                recv_sem=recv_sems.at[which, offset],
                device_id={axis: peer},
                device_id_type=MESH_IDS,
            )
            copy.start()
            copies.append(copy)
    for which in range(arrays):
        src_ref, out_ref = sources[which], outputs[which]
        out_ref[me] = src_ref[me] if spreads[which] else src_ref[...]
    for copy in copies:
        copy.wait()


def exchange_many(arrays, spreads, axis, count, ident):
    shapes = []
    for values, spread in zip(arrays, spreads):
        block = values.shape[1:] if spread else values.shape
        shapes.append(jax.ShapeDtypeStruct((count,) + tuple(block), values.dtype))
    return pl.pallas_call(
        functools.partial(exchange_kernel, axis, count, tuple(spreads)),
        out_shape=tuple(shapes),
        in_specs=[pl.BlockSpec(memory_space=pltpu.VMEM)] * len(arrays),
        out_specs=tuple(pl.BlockSpec(memory_space=pltpu.VMEM) for _ in arrays),
        scratch_shapes=[
            pltpu.SemaphoreType.DMA((len(arrays), count)),
            pltpu.SemaphoreType.DMA((len(arrays), count)),
        ],
        compiler_params=pltpu.CompilerParams(collective_id=ident, has_side_effects=True),
    )(*arrays)


def exchange(values, axis, count, spread, ident):
    return exchange_many((values,), (spread,), axis, count, ident)[0]


def body(
    req_count,
    head_count,
    hidden,
    deal_order,
    lengths,
    page_table,
    key_cache,
    value_cache,
    attn_gain,
    w_query,
    w_key,
    w_value,
    w_gate,
    w_out,
    query_gain,
    key_gain,
    mlp_gain,
    mlp_gate,
    mlp_up,
    mlp_down,
):
    local_rows, model_width = hidden.shape
    req_index = lax.axis_index("req")
    head_index = lax.axis_index("head")
    all_rows = local_rows * req_count
    head_width = query_gain.shape[0]
    pool_pages, page_size, local_kv = key_cache.shape[:3]
    group_size = w_query.shape[1] // (local_kv * head_width)
    head_cols = local_kv * group_size * head_width
    pairs = local_kv * group_size
    chunk = model_width // head_count
    scale_factor = 1.0 / math.sqrt(head_width)
    first_own = req_index * local_rows

    with jax.named_scope("projections"):
        hidden_f = hidden.astype(jnp.float32)
        normed = (hidden_f * rms_inv(hidden_f) * attn_gain).astype(jnp.bfloat16)
        own_requests = lax.dynamic_slice_in_dim(deal_order, first_own, local_rows)
        request_ids = jnp.arange(all_rows, dtype=jnp.int32)
        own_pick = own_requests[:, None] == request_ids[None, :]
        position = jnp.sum(jnp.where(own_pick, lengths[None, :], 0), axis=1).astype(jnp.float32)
        queries = jnp.dot(normed, w_query, preferred_element_type=jnp.float32).reshape(
            local_rows, local_kv, group_size, head_width
        )
        queries = norm_rotate(queries, query_gain, position).astype(jnp.bfloat16)
        new_keys = jnp.dot(normed, w_key, preferred_element_type=jnp.float32).reshape(
            local_rows, local_kv, head_width
        )
        new_keys = norm_rotate(new_keys, key_gain, position).astype(jnp.bfloat16)
        new_values = (
            jnp.dot(normed, w_value, preferred_element_type=jnp.float32)
            .astype(jnp.bfloat16)
            .reshape(local_rows, local_kv, head_width)
        )
        gate_logits = jnp.dot(normed, w_gate, preferred_element_type=jnp.float32)

    all_queries = exchange(queries.reshape(local_rows, head_cols), "req", req_count, False, 0)
    all_queries = all_queries.reshape(all_rows, head_cols)

    with jax.named_scope("page_owners"):
        page_counts = (lengths + page_size - 1) // page_size
        slot_ids = jnp.arange(page_table.shape[1], dtype=jnp.int32)
        local_ids = page_table - req_index * pool_pages
        usable = (
            (slot_ids[None, :] < page_counts[:, None]) & (local_ids >= 0) & (local_ids < pool_pages)
        )
        keyed = jnp.where(usable, local_ids, pool_pages)
        page_ids = jnp.arange(pool_pages, dtype=jnp.int32)
        match = keyed[None, :, :] == page_ids[:, None, None]
        owned_requests = jnp.any(match, axis=2)
        owner_slot = jnp.sum(jnp.where(match, slot_ids[None, None, :], 0), axis=(1, 2))
        owner_length = jnp.sum(jnp.where(owned_requests, lengths[None, :], 0), axis=1)
        filled = jnp.clip(owner_length - owner_slot * page_size, 0, page_size)
        filled = jnp.where(jnp.any(owned_requests, axis=1), filled, 0)
        dealing = (request_ids[:, None] == deal_order[None, :]).astype(jnp.bfloat16)
        owned = (
            jnp.dot(owned_requests.astype(jnp.bfloat16), dealing, preferred_element_type=jnp.float32)
            > 0.5
        )
        page_queries = (
            jnp.dot(owned.astype(jnp.bfloat16), all_queries, preferred_element_type=jnp.float32)
            .astype(jnp.bfloat16)
            .reshape(pool_pages, local_kv, group_size, head_width)
        )

    with jax.named_scope("page_attention"):
        scores = (
            jnp.einsum("pkgd,ptkd->pkgt", page_queries, key_cache, preferred_element_type=jnp.float32)
            * scale_factor
        )
        live_mask = (
            jnp.arange(page_size, dtype=jnp.int32)[None, None, None, :] < filled[:, None, None, None]
        )
        scores = jnp.where(live_mask, scores, LOW_SCORE)
        page_peaks = jnp.max(scores, axis=-1)
        owned_b = owned[:, :, None, None]
        row_peaks = jnp.max(jnp.where(owned_b, page_peaks[:, None], LOW_SCORE), axis=0)
        row_shift = LOG_TWO * jnp.ceil(row_peaks / LOG_TWO)
        page_shift = jnp.max(jnp.where(owned_b, row_shift[None], LOW_SCORE), axis=1)
        weights = jnp.where(live_mask, jnp.exp(scores - page_shift[..., None]), 0.0)
        page_totals = jnp.sum(weights, axis=-1)
        page_numerators = jnp.einsum(
            "pkgt,ptkd->pkgd",
            weights.astype(jnp.bfloat16),
            value_cache,
            preferred_element_type=jnp.float32,
        )
        owned_f = owned.astype(jnp.float32)
        row_totals = jnp.dot(
            owned_f.T, page_totals.reshape(pool_pages, pairs), precision=lax.Precision.HIGHEST
        )
        row_numerators = jnp.dot(
            owned_f.T,
            page_numerators.reshape(pool_pages, head_cols),
            precision=lax.Precision.HIGHEST,
        )
        numerator_message = row_numerators.astype(jnp.bfloat16).reshape(req_count, local_rows, head_cols)
        stats_message = jnp.concatenate(
            [row_shift.reshape(req_count, local_rows, pairs), row_totals.reshape(req_count, local_rows, pairs)],
            axis=2,
        ).transpose(0, 2, 1)

    got_numerators, got_stats = exchange_many(
        (numerator_message, stats_message), (True, True), "req", req_count, 1
    )

    with jax.named_scope("combine"):
        got_numerators = got_numerators.astype(jnp.float32).reshape(
            req_count, local_rows, local_kv, group_size, head_width
        )
        got_stats = got_stats.transpose(0, 2, 1)
        got_shift = got_stats[:, :, :pairs].reshape(req_count, local_rows, local_kv, group_size)
        got_totals = got_stats[:, :, pairs:].reshape(req_count, local_rows, local_kv, group_size)
        self_scores = (
            jnp.einsum("rkgd,rkd->rkg", queries, new_keys, preferred_element_type=jnp.float32)
            * scale_factor
        )
        self_shift = LOG_TWO * jnp.ceil(self_scores / LOG_TWO)
        shift = jnp.maximum(jnp.max(got_shift, axis=0), self_shift)
        factor = jnp.exp(got_shift - shift[None])
        self_weight = jnp.exp(self_scores - shift)
        totals = jnp.sum(got_totals * factor, axis=0) + self_weight
        self_rounded = self_weight.astype(jnp.bfloat16).astype(jnp.float32)
        numerators = (
            jnp.sum(got_numerators * factor[..., None], axis=0)
            + self_rounded[..., None] * new_values.astype(jnp.float32)[:, :, None, :]
        )
        heads_out = (numerators / totals[..., None]).reshape(local_rows, head_cols)
        attended = (heads_out * jax.nn.sigmoid(gate_logits)).astype(jnp.bfloat16)
        projected = jnp.dot(attended, w_out, preferred_element_type=jnp.float32)
        projected = projected.reshape(local_rows, head_count, chunk).transpose(1, 0, 2)

    attn_parts = exchange(projected, "head", head_count, True, 2)

    with jax.named_scope("residual"):
        hidden_chunk = lax.dynamic_slice_in_dim(hidden_f, head_index * chunk, chunk, axis=1)
        mixed_chunk = (hidden_chunk + jnp.sum(attn_parts, axis=0)).astype(jnp.bfloat16)

    mixed_all = exchange(mixed_chunk, "head", head_count, False, 3)

    with jax.named_scope("mlp"):
        mixed_rows = mixed_all.transpose(1, 0, 2).reshape(local_rows, model_width)
        mixed_f = mixed_rows.astype(jnp.float32)
        normed_two = (mixed_f * rms_inv(mixed_f) * mlp_gain).astype(jnp.bfloat16)
        gate_part = jnp.dot(normed_two, mlp_gate, preferred_element_type=jnp.float32)
        up_part = jnp.dot(normed_two, mlp_up, preferred_element_type=jnp.float32)
        inner_act = (jax.nn.silu(gate_part) * up_part).astype(jnp.bfloat16)
        down_part = jnp.dot(inner_act, mlp_down, preferred_element_type=jnp.float32)
        down_part = down_part.reshape(local_rows, head_count, chunk).transpose(1, 0, 2)

    mlp_parts = exchange(down_part, "head", head_count, True, 4)

    with jax.named_scope("result"):
        result_chunk = (mixed_chunk.astype(jnp.float32) + jnp.sum(mlp_parts, axis=0)).astype(
            jnp.bfloat16
        )

    result_all = exchange(result_chunk, "req", req_count, False, 5).reshape(all_rows, chunk)

    with jax.named_scope("reorder"):
        wanted = first_own + jnp.arange(local_rows, dtype=jnp.int32)
        selector = (deal_order[None, :] == wanted[:, None]).astype(jnp.bfloat16)
        picked = jnp.dot(selector, result_all, preferred_element_type=jnp.float32).astype(
            jnp.bfloat16
        )

    output_parts = exchange(picked, "head", head_count, False, 6)
    return output_parts.transpose(1, 0, 2).reshape(local_rows, model_width)


def solution(mesh):
    return jax.shard_map(
        functools.partial(body, mesh.shape["req"], mesh.shape["head"]),
        mesh=mesh,
        in_specs=(
            P("req", None),
            P(),
            P(),
            P(),
            P("req", None, "head", None),
            P("req", None, "head", None),
            P(),
            P(None, "head"),
            P(None, "head"),
            P(None, "head"),
            P(None, "head"),
            P("head", None),
            P(),
            P(),
            P(),
            P(None, "head"),
            P(None, "head"),
            P("head", None),
        ),
        out_specs=P("req", None),
        check_vma=False,
    )
```

```python
import functools
import math

import jax
import jax.numpy as jnp
from jax import lax
from jax.experimental import pallas as pl
from jax.experimental.pallas import tpu as pltpu
from jax.sharding import PartitionSpec as P

EPSILON = 1e-06
ROPE_BASE = 1000000.0
LOW_SCORE = -1e30
LOG_TWO = math.log(2.0)
MESH_IDS = pl.DeviceIdType.MESH


def rms_inv(values):
    return lax.rsqrt(jnp.mean(values * values, axis=-1, keepdims=True) + EPSILON)


def rotate(values, position):
    half_dim = values.shape[-1] // 2
    exponent = jnp.arange(half_dim, dtype=jnp.float32) * (2.0 / values.shape[-1])
    frequency = ROPE_BASE ** (-exponent)
    angles = position[:, None] * frequency[None, :]
    ones_tail = (1,) * (values.ndim - 2)
    angles = angles.reshape((angles.shape[0],) + ones_tail + (half_dim,))
    cosine = jnp.cos(angles)
    sine_vals = jnp.sin(angles)
    front_half = values[..., :half_dim]
    back_half = values[..., half_dim:]
    return jnp.concatenate(
        [front_half * cosine - back_half * sine_vals, back_half * cosine + front_half * sine_vals],
        axis=-1,
    )


def norm_rotate(values, gain_vec, position):
    return rotate(values * rms_inv(values) * gain_vec, position)


def exchange_kernel(axis, count, spreads, *refs):
    arrays = len(spreads)
    sources, outputs = refs[:arrays], refs[arrays : 2 * arrays]
    send_sems, recv_sems = refs[2 * arrays], refs[2 * arrays + 1]
    me = lax.axis_index(axis)
    barrier = pltpu.get_barrier_semaphore()
    for offset in range(1, count):
        peer = lax.rem(me + offset, count)
        pl.semaphore_signal(barrier, inc=1, device_id={axis: peer}, device_id_type=MESH_IDS)
    pl.semaphore_wait(barrier, count - 1)
    copies = []
    for offset in range(1, count):
        peer = lax.rem(me + offset, count)
        for which in range(arrays):
            src_ref, out_ref = sources[which], outputs[which]
            copy = pltpu.make_async_remote_copy(
                src_ref=src_ref.at[peer] if spreads[which] else src_ref,
                dst_ref=out_ref.at[me],
                send_sem=send_sems.at[which, offset],
                recv_sem=recv_sems.at[which, offset],
                device_id={axis: peer},
                device_id_type=MESH_IDS,
            )
            copy.start()
            copies.append(copy)
    for which in range(arrays):
        src_ref, out_ref = sources[which], outputs[which]
        out_ref[me] = src_ref[me] if spreads[which] else src_ref[...]
    for copy in copies:
        copy.wait()


def exchange_many(arrays, spreads, axis, count, ident):
    shapes = []
    for values, spread in zip(arrays, spreads):
        block = values.shape[1:] if spread else values.shape
        shapes.append(jax.ShapeDtypeStruct((count,) + tuple(block), values.dtype))
    return pl.pallas_call(
        functools.partial(exchange_kernel, axis, count, tuple(spreads)),
        out_shape=tuple(shapes),
        in_specs=[pl.BlockSpec(memory_space=pltpu.VMEM)] * len(arrays),
        out_specs=tuple(pl.BlockSpec(memory_space=pltpu.VMEM) for _ in arrays),
        scratch_shapes=[
            pltpu.SemaphoreType.DMA((len(arrays), count)),
            pltpu.SemaphoreType.DMA((len(arrays), count)),
        ],
        compiler_params=pltpu.CompilerParams(collective_id=ident, has_side_effects=True),
    )(*arrays)


def exchange(values, axis, count, spread, ident):
    return exchange_many((values,), (spread,), axis, count, ident)[0]


def greet(peers):
    barrier = pltpu.get_barrier_semaphore()
    for axis, peer in peers:
        pl.semaphore_signal(barrier, inc=1, device_id={axis: peer}, device_id_type=MESH_IDS)
    pl.semaphore_wait(barrier, len(peers))


def peers_of(axis, count):
    me = lax.axis_index(axis)
    return me, [(offset, lax.rem(me + offset, count)) for offset in range(1, count)]


def send_all(axis, peers, src_of, dst, send_sems, recv_sems, phase):
    copies = []
    for offset, peer in peers:
        copy = pltpu.make_async_remote_copy(
            src_ref=src_of(peer),
            dst_ref=dst,
            send_sem=send_sems.at[phase, offset],
            recv_sem=recv_sems.at[phase, offset],
            device_id={axis: peer},
            device_id_type=MESH_IDS,
        )
        copy.start()
        copies.append(copy)
    for copy in copies:
        copy.wait()


def residual_kernel(count, parts_ref, base_ref, out_ref, summed, send_sems, recv_sems):
    me, peers = peers_of("head", count)
    greet([("head", peer) for _, peer in peers])
    summed[me] = parts_ref[me]
    send_all("head", peers, lambda peer: parts_ref.at[peer], summed.at[me], send_sems, recv_sems, 0)
    out_ref[me] = (base_ref[...] + jnp.sum(summed[...], axis=0)).astype(out_ref.dtype)
    send_all("head", peers, lambda peer: out_ref.at[me], out_ref.at[me], send_sems, recv_sems, 1)


def residual_exchange(parts, base, count, ident):
    return pl.pallas_call(
        functools.partial(residual_kernel, count),
        out_shape=jax.ShapeDtypeStruct(parts.shape, jnp.bfloat16),
        in_specs=[pl.BlockSpec(memory_space=pltpu.VMEM)] * 2,
        out_specs=pl.BlockSpec(memory_space=pltpu.VMEM),
        scratch_shapes=[
            pltpu.VMEM(parts.shape, jnp.float32),
            pltpu.SemaphoreType.DMA((2, count)),
            pltpu.SemaphoreType.DMA((2, count)),
        ],
        compiler_params=pltpu.CompilerParams(collective_id=ident, has_side_effects=True),
    )(parts, base)


def tail_kernel(
    head_count, req_count, parts_ref, base_ref, picker_ref, out_ref, summed, results, send_sems, recv_sems
):
    head_me, head_peers = peers_of("head", head_count)
    req_me, req_peers = peers_of("req", req_count)
    greet([("head", peer) for _, peer in head_peers] + [("req", peer) for _, peer in req_peers])
    summed[head_me] = parts_ref[head_me]
    send_all("head", head_peers, lambda peer: parts_ref.at[peer], summed.at[head_me], send_sems, recv_sems, 0)
    results[req_me] = (base_ref[...].astype(jnp.float32) + jnp.sum(summed[...], axis=0)).astype(
        results.dtype
    )
    send_all("req", req_peers, lambda peer: results.at[req_me], results.at[req_me], send_sems, recv_sems, 1)
    rows, cols = base_ref.shape
    out_ref[head_me] = jnp.dot(
        picker_ref[...], results[...].reshape(req_count * rows, cols), preferred_element_type=jnp.float32
    ).astype(out_ref.dtype)
    send_all("head", head_peers, lambda peer: out_ref.at[head_me], out_ref.at[head_me], send_sems, recv_sems, 2)


def tail_exchange(parts, base, picker, head_count, req_count, ident):
    rows, cols = base.shape
    most = max(head_count, req_count)
    return pl.pallas_call(
        functools.partial(tail_kernel, head_count, req_count),
        out_shape=jax.ShapeDtypeStruct((head_count, rows, cols), jnp.bfloat16),
        in_specs=[pl.BlockSpec(memory_space=pltpu.VMEM)] * 3,
        out_specs=pl.BlockSpec(memory_space=pltpu.VMEM),
        scratch_shapes=[
            pltpu.VMEM(parts.shape, jnp.float32),
            pltpu.VMEM((req_count, rows, cols), jnp.bfloat16),
            pltpu.SemaphoreType.DMA((3, most)),
            pltpu.SemaphoreType.DMA((3, most)),
        ],
        compiler_params=pltpu.CompilerParams(collective_id=ident, has_side_effects=True),
    )(parts, base, picker)


def body(
    req_count,
    head_count,
    hidden,
    deal_order,
    lengths,
    page_table,
    key_cache,
    value_cache,
    attn_gain,
    w_query,
    w_key,
    w_value,
    w_gate,
    w_out,
    query_gain,
    key_gain,
    mlp_gain,
    mlp_gate,
    mlp_up,
    mlp_down,
):
    local_rows, model_width = hidden.shape
    req_index = lax.axis_index("req")
    head_index = lax.axis_index("head")
    all_rows = local_rows * req_count
    head_width = query_gain.shape[0]
    pool_pages, page_size, local_kv = key_cache.shape[:3]
    group_size = w_query.shape[1] // (local_kv * head_width)
    head_cols = local_kv * group_size * head_width
    pairs = local_kv * group_size
    chunk = model_width // head_count
    scale_factor = 1.0 / math.sqrt(head_width)
    first_own = req_index * local_rows

    with jax.named_scope("projections"):
        hidden_f = hidden.astype(jnp.float32)
        normed = (hidden_f * rms_inv(hidden_f) * attn_gain).astype(jnp.bfloat16)
        own_requests = lax.dynamic_slice_in_dim(deal_order, first_own, local_rows)
        request_ids = jnp.arange(all_rows, dtype=jnp.int32)
        own_pick = own_requests[:, None] == request_ids[None, :]
        position = jnp.sum(jnp.where(own_pick, lengths[None, :], 0), axis=1).astype(jnp.float32)
        queries = jnp.dot(normed, w_query, preferred_element_type=jnp.float32).reshape(
            local_rows, local_kv, group_size, head_width
        )
        queries = norm_rotate(queries, query_gain, position).astype(jnp.bfloat16)
        new_keys = jnp.dot(normed, w_key, preferred_element_type=jnp.float32).reshape(
            local_rows, local_kv, head_width
        )
        new_keys = norm_rotate(new_keys, key_gain, position).astype(jnp.bfloat16)
        new_values = (
            jnp.dot(normed, w_value, preferred_element_type=jnp.float32)
            .astype(jnp.bfloat16)
            .reshape(local_rows, local_kv, head_width)
        )
        gate_logits = jnp.dot(normed, w_gate, preferred_element_type=jnp.float32)

    all_queries = exchange(queries.reshape(local_rows, head_cols), "req", req_count, False, 0)
    all_queries = all_queries.reshape(all_rows, head_cols)

    with jax.named_scope("page_owners"):
        page_counts = (lengths + page_size - 1) // page_size
        slot_ids = jnp.arange(page_table.shape[1], dtype=jnp.int32)
        local_ids = page_table - req_index * pool_pages
        usable = (
            (slot_ids[None, :] < page_counts[:, None]) & (local_ids >= 0) & (local_ids < pool_pages)
        )
        keyed = jnp.where(usable, local_ids, pool_pages)
        page_ids = jnp.arange(pool_pages, dtype=jnp.int32)
        match = keyed[None, :, :] == page_ids[:, None, None]
        owned_requests = jnp.any(match, axis=2)
        owner_slot = jnp.sum(jnp.where(match, slot_ids[None, None, :], 0), axis=(1, 2))
        owner_length = jnp.sum(jnp.where(owned_requests, lengths[None, :], 0), axis=1)
        filled = jnp.clip(owner_length - owner_slot * page_size, 0, page_size)
        filled = jnp.where(jnp.any(owned_requests, axis=1), filled, 0)
        dealing = (request_ids[:, None] == deal_order[None, :]).astype(jnp.bfloat16)
        owned = (
            jnp.dot(owned_requests.astype(jnp.bfloat16), dealing, preferred_element_type=jnp.float32)
            > 0.5
        )
        page_queries = (
            jnp.dot(owned.astype(jnp.bfloat16), all_queries, preferred_element_type=jnp.float32)
            .astype(jnp.bfloat16)
            .reshape(pool_pages, local_kv, group_size, head_width)
        )

    with jax.named_scope("page_attention"):
        scores = (
            jnp.einsum("pkgd,ptkd->pkgt", page_queries, key_cache, preferred_element_type=jnp.float32)
            * scale_factor
        )
        live_mask = (
            jnp.arange(page_size, dtype=jnp.int32)[None, None, None, :] < filled[:, None, None, None]
        )
        scores = jnp.where(live_mask, scores, LOW_SCORE)
        page_peaks = jnp.max(scores, axis=-1)
        owned_b = owned[:, :, None, None]
        row_peaks = jnp.max(jnp.where(owned_b, page_peaks[:, None], LOW_SCORE), axis=0)
        row_shift = LOG_TWO * jnp.ceil(row_peaks / LOG_TWO)
        page_shift = jnp.max(jnp.where(owned_b, row_shift[None], LOW_SCORE), axis=1)
        weights = jnp.where(live_mask, jnp.exp(scores - page_shift[..., None]), 0.0)
        page_totals = jnp.sum(weights, axis=-1)
        page_numerators = jnp.einsum(
            "pkgt,ptkd->pkgd",
            weights.astype(jnp.bfloat16),
            value_cache,
            preferred_element_type=jnp.float32,
        )
        owned_f = owned.astype(jnp.float32)
        row_totals = jnp.dot(
            owned_f.T, page_totals.reshape(pool_pages, pairs), precision=lax.Precision.HIGHEST
        )
        row_numerators = jnp.dot(
            owned_f.T,
            page_numerators.reshape(pool_pages, head_cols),
            precision=lax.Precision.HIGHEST,
        )
        numerator_message = row_numerators.astype(jnp.bfloat16).reshape(req_count, local_rows, head_cols)
        stats_message = jnp.concatenate(
            [row_shift.reshape(req_count, local_rows, pairs), row_totals.reshape(req_count, local_rows, pairs)],
            axis=2,
        ).transpose(0, 2, 1)

    got_numerators, got_stats = exchange_many(
        (numerator_message, stats_message), (True, True), "req", req_count, 1
    )

    with jax.named_scope("combine"):
        got_numerators = got_numerators.astype(jnp.float32).reshape(
            req_count, local_rows, local_kv, group_size, head_width
        )
        got_stats = got_stats.transpose(0, 2, 1)
        got_shift = got_stats[:, :, :pairs].reshape(req_count, local_rows, local_kv, group_size)
        got_totals = got_stats[:, :, pairs:].reshape(req_count, local_rows, local_kv, group_size)
        self_scores = (
            jnp.einsum("rkgd,rkd->rkg", queries, new_keys, preferred_element_type=jnp.float32)
            * scale_factor
        )
        self_shift = LOG_TWO * jnp.ceil(self_scores / LOG_TWO)
        shift = jnp.maximum(jnp.max(got_shift, axis=0), self_shift)
        factor = jnp.exp(got_shift - shift[None])
        self_weight = jnp.exp(self_scores - shift)
        totals = jnp.sum(got_totals * factor, axis=0) + self_weight
        self_rounded = self_weight.astype(jnp.bfloat16).astype(jnp.float32)
        numerators = (
            jnp.sum(got_numerators * factor[..., None], axis=0)
            + self_rounded[..., None] * new_values.astype(jnp.float32)[:, :, None, :]
        )
        heads_out = (numerators / totals[..., None]).reshape(local_rows, head_cols)
        attended = (heads_out * jax.nn.sigmoid(gate_logits)).astype(jnp.bfloat16)
        projected = jnp.dot(attended, w_out, preferred_element_type=jnp.float32)
        projected = projected.reshape(local_rows, head_count, chunk).transpose(1, 0, 2)

    hidden_chunk = lax.dynamic_slice_in_dim(hidden_f, head_index * chunk, chunk, axis=1)
    mixed_all = residual_exchange(projected, hidden_chunk, head_count, 2)
    mixed_chunk = lax.dynamic_index_in_dim(mixed_all, head_index, axis=0, keepdims=False)

    with jax.named_scope("mlp"):
        mixed_rows = mixed_all.transpose(1, 0, 2).reshape(local_rows, model_width)
        mixed_f = mixed_rows.astype(jnp.float32)
        normed_two = (mixed_f * rms_inv(mixed_f) * mlp_gain).astype(jnp.bfloat16)
        gate_part = jnp.dot(normed_two, mlp_gate, preferred_element_type=jnp.float32)
        up_part = jnp.dot(normed_two, mlp_up, preferred_element_type=jnp.float32)
        inner_act = (jax.nn.silu(gate_part) * up_part).astype(jnp.bfloat16)
        down_part = jnp.dot(inner_act, mlp_down, preferred_element_type=jnp.float32)
        down_part = down_part.reshape(local_rows, head_count, chunk).transpose(1, 0, 2)

    with jax.named_scope("reorder"):
        wanted = first_own + jnp.arange(local_rows, dtype=jnp.int32)
        picker = (deal_order[None, :] == wanted[:, None]).astype(jnp.bfloat16)

    output_parts = tail_exchange(down_part, mixed_chunk, picker, head_count, req_count, 3)
    return output_parts.transpose(1, 0, 2).reshape(local_rows, model_width)


def solution(mesh):
    return jax.shard_map(
        functools.partial(body, mesh.shape["req"], mesh.shape["head"]),
        mesh=mesh,
        in_specs=(
            P("req", None),
            P(),
            P(),
            P(),
            P("req", None, "head", None),
            P("req", None, "head", None),
            P(),
            P(None, "head"),
            P(None, "head"),
            P(None, "head"),
            P(None, "head"),
            P("head", None),
            P(),
            P(),
            P(),
            P(None, "head"),
            P(None, "head"),
            P("head", None),
        ),
        out_specs=P("req", None),
        check_vma=False,
    )
```

```python
import functools
import math

import jax
import jax.numpy as jnp
from jax import lax
from jax.experimental import pallas as pl
from jax.experimental.pallas import tpu as pltpu
from jax.sharding import PartitionSpec as P

EPSILON = 1e-06
ROPE_BASE = 1000000.0
LOW_SCORE = -1e30
LOG_TWO = math.log(2.0)
MESH_IDS = pl.DeviceIdType.MESH


def rms_inv(values):
    return lax.rsqrt(jnp.mean(values * values, axis=-1, keepdims=True) + EPSILON)


def rotate(values, position):
    half_dim = values.shape[-1] // 2
    exponent = jnp.arange(half_dim, dtype=jnp.float32) * (2.0 / values.shape[-1])
    frequency = ROPE_BASE ** (-exponent)
    angles = position[:, None] * frequency[None, :]
    ones_tail = (1,) * (values.ndim - 2)
    angles = angles.reshape((angles.shape[0],) + ones_tail + (half_dim,))
    cosine = jnp.cos(angles)
    sine_vals = jnp.sin(angles)
    front_half = values[..., :half_dim]
    back_half = values[..., half_dim:]
    return jnp.concatenate(
        [front_half * cosine - back_half * sine_vals, back_half * cosine + front_half * sine_vals],
        axis=-1,
    )


def norm_rotate(values, gain_vec, position):
    return rotate(values * rms_inv(values) * gain_vec, position)


def exchange_kernel(axis, count, spreads, *refs):
    arrays = len(spreads)
    sources, outputs = refs[:arrays], refs[arrays : 2 * arrays]
    send_sems, recv_sems = refs[2 * arrays], refs[2 * arrays + 1]
    me = lax.axis_index(axis)
    barrier = pltpu.get_barrier_semaphore()
    for offset in range(1, count):
        peer = lax.rem(me + offset, count)
        pl.semaphore_signal(barrier, inc=1, device_id={axis: peer}, device_id_type=MESH_IDS)
    pl.semaphore_wait(barrier, count - 1)
    copies = []
    for offset in range(1, count):
        peer = lax.rem(me + offset, count)
        for which in range(arrays):
            src_ref, out_ref = sources[which], outputs[which]
            copy = pltpu.make_async_remote_copy(
                src_ref=src_ref.at[peer] if spreads[which] else src_ref,
                dst_ref=out_ref.at[me],
                send_sem=send_sems.at[which, offset],
                recv_sem=recv_sems.at[which, offset],
                device_id={axis: peer},
                device_id_type=MESH_IDS,
            )
            copy.start()
            copies.append(copy)
    for which in range(arrays):
        src_ref, out_ref = sources[which], outputs[which]
        out_ref[me] = src_ref[me] if spreads[which] else src_ref[...]
    for copy in copies:
        copy.wait()


def exchange_many(arrays, spreads, axis, count, ident):
    shapes = []
    for values, spread in zip(arrays, spreads):
        block = values.shape[1:] if spread else values.shape
        shapes.append(jax.ShapeDtypeStruct((count,) + tuple(block), values.dtype))
    return pl.pallas_call(
        functools.partial(exchange_kernel, axis, count, tuple(spreads)),
        out_shape=tuple(shapes),
        in_specs=[pl.BlockSpec(memory_space=pltpu.VMEM)] * len(arrays),
        out_specs=tuple(pl.BlockSpec(memory_space=pltpu.VMEM) for _ in arrays),
        scratch_shapes=[
            pltpu.SemaphoreType.DMA((len(arrays), count)),
            pltpu.SemaphoreType.DMA((len(arrays), count)),
        ],
        compiler_params=pltpu.CompilerParams(collective_id=ident, has_side_effects=True),
    )(*arrays)


def exchange(values, axis, count, spread, ident):
    return exchange_many((values,), (spread,), axis, count, ident)[0]


def greet(peers):
    barrier = pltpu.get_barrier_semaphore()
    for axis, peer in peers:
        pl.semaphore_signal(barrier, inc=1, device_id={axis: peer}, device_id_type=MESH_IDS)
    pl.semaphore_wait(barrier, len(peers))


def peers_of(axis, count):
    me = lax.axis_index(axis)
    return me, [(offset, lax.rem(me + offset, count)) for offset in range(1, count)]


def send_all(axis, peers, src_of, dst, send_sems, recv_sems, phase):
    copies = []
    for offset, peer in peers:
        copy = pltpu.make_async_remote_copy(
            src_ref=src_of(peer),
            dst_ref=dst,
            send_sem=send_sems.at[phase, offset],
            recv_sem=recv_sems.at[phase, offset],
            device_id={axis: peer},
            device_id_type=MESH_IDS,
        )
        copy.start()
        copies.append(copy)
    for copy in copies:
        copy.wait()


def two_level_peers(count, inner):
    me = lax.axis_index("req")
    outer_index, inner_index = me // inner, me % inner
    near = [(k, outer_index * inner + lax.rem(inner_index + k, inner)) for k in range(1, inner)]
    far = [(k, lax.rem(outer_index + k, count // inner) * inner + inner_index) for k in range(1, count // inner)]
    return me, outer_index, near, far


def two_level_gather(count, inner, me, outer_index, near, far, own_ref, out_ref, local_sem, send_sems, recv_sems, phase):
    local = pltpu.make_async_copy(own_ref, out_ref.at[me], local_sem)
    local.start()
    send_all("req", near, lambda peer: own_ref, out_ref.at[me], send_sems, recv_sems, phase)
    local.wait()
    group = pl.ds(outer_index * inner, inner)
    send_all("req", far, lambda peer: out_ref.at[group], out_ref.at[group], send_sems, recv_sems, phase + 1)


def gather_kernel(count, inner, src_ref, out_ref, local_sem, send_sems, recv_sems):
    me, outer_index, near, far = two_level_peers(count, inner)
    greet([("req", peer) for _, peer in near + far])
    two_level_gather(count, inner, me, outer_index, near, far, src_ref, out_ref, local_sem, send_sems, recv_sems, 0)


def req_gather(values, count, inner, ident):
    return pl.pallas_call(
        functools.partial(gather_kernel, count, inner),
        out_shape=jax.ShapeDtypeStruct((count,) + values.shape, values.dtype),
        in_specs=[pl.BlockSpec(memory_space=pltpu.VMEM)],
        out_specs=pl.BlockSpec(memory_space=pltpu.VMEM),
        scratch_shapes=[
            pltpu.SemaphoreType.DMA(()),
            pltpu.SemaphoreType.DMA((2, count)),
            pltpu.SemaphoreType.DMA((2, count)),
        ],
        compiler_params=pltpu.CompilerParams(collective_id=ident, has_side_effects=True),
    )(values)


def residual_kernel(count, parts_ref, base_ref, out_ref, summed, send_sems, recv_sems):
    me, peers = peers_of("head", count)
    greet([("head", peer) for _, peer in peers])
    summed[me] = parts_ref[me]
    send_all("head", peers, lambda peer: parts_ref.at[peer], summed.at[me], send_sems, recv_sems, 0)
    out_ref[me] = (base_ref[...] + jnp.sum(summed[...], axis=0)).astype(out_ref.dtype)
    send_all("head", peers, lambda peer: out_ref.at[me], out_ref.at[me], send_sems, recv_sems, 1)


def residual_exchange(parts, base, count, ident):
    return pl.pallas_call(
        functools.partial(residual_kernel, count),
        out_shape=jax.ShapeDtypeStruct(parts.shape, jnp.bfloat16),
        in_specs=[pl.BlockSpec(memory_space=pltpu.VMEM)] * 2,
        out_specs=pl.BlockSpec(memory_space=pltpu.VMEM),
        scratch_shapes=[
            pltpu.VMEM(parts.shape, jnp.float32),
            pltpu.SemaphoreType.DMA((2, count)),
            pltpu.SemaphoreType.DMA((2, count)),
        ],
        compiler_params=pltpu.CompilerParams(collective_id=ident, has_side_effects=True),
    )(parts, base)


def tail_kernel(
    head_count, req_count, inner, parts_ref, base_ref, picker_ref, out_ref, summed, own, results, local_sem,
    send_sems, recv_sems,
):
    head_me, head_peers = peers_of("head", head_count)
    req_me, outer_index, near, far = two_level_peers(req_count, inner)
    greet([("head", peer) for _, peer in head_peers] + [("req", peer) for _, peer in near + far])
    summed[head_me] = parts_ref[head_me]
    send_all("head", head_peers, lambda peer: parts_ref.at[peer], summed.at[head_me], send_sems, recv_sems, 0)
    own[...] = (base_ref[...].astype(jnp.float32) + jnp.sum(summed[...], axis=0)).astype(own.dtype)
    two_level_gather(
        req_count, inner, req_me, outer_index, near, far, own, results, local_sem, send_sems, recv_sems, 1
    )
    rows, cols = base_ref.shape
    out_ref[head_me] = jnp.dot(
        picker_ref[...], results[...].reshape(req_count * rows, cols), preferred_element_type=jnp.float32
    ).astype(out_ref.dtype)
    send_all("head", head_peers, lambda peer: out_ref.at[head_me], out_ref.at[head_me], send_sems, recv_sems, 3)


def tail_exchange(parts, base, picker, head_count, req_count, inner, ident):
    rows, cols = base.shape
    most = max(head_count, req_count)
    return pl.pallas_call(
        functools.partial(tail_kernel, head_count, req_count, inner),
        out_shape=jax.ShapeDtypeStruct((head_count, rows, cols), jnp.bfloat16),
        in_specs=[pl.BlockSpec(memory_space=pltpu.VMEM)] * 3,
        out_specs=pl.BlockSpec(memory_space=pltpu.VMEM),
        scratch_shapes=[
            pltpu.VMEM(parts.shape, jnp.float32),
            pltpu.VMEM((rows, cols), jnp.bfloat16),
            pltpu.VMEM((req_count, rows, cols), jnp.bfloat16),
            pltpu.SemaphoreType.DMA(()),
            pltpu.SemaphoreType.DMA((4, most)),
            pltpu.SemaphoreType.DMA((4, most)),
        ],
        compiler_params=pltpu.CompilerParams(collective_id=ident, has_side_effects=True),
    )(parts, base, picker)


def req_groups(mesh):
    try:
        column = mesh.devices[:, 0]
        inner = len({device.coords[1] for device in column})
    except (AttributeError, IndexError, TypeError):
        inner = 1
    return inner if inner > 1 and mesh.shape["req"] % inner == 0 else 1


def body(
    req_count,
    head_count,
    inner,
    hidden,
    deal_order,
    lengths,
    page_table,
    key_cache,
    value_cache,
    attn_gain,
    w_query,
    w_key,
    w_value,
    w_gate,
    w_out,
    query_gain,
    key_gain,
    mlp_gain,
    mlp_gate,
    mlp_up,
    mlp_down,
):
    local_rows, model_width = hidden.shape
    req_index = lax.axis_index("req")
    head_index = lax.axis_index("head")
    all_rows = local_rows * req_count
    head_width = query_gain.shape[0]
    pool_pages, page_size, local_kv = key_cache.shape[:3]
    group_size = w_query.shape[1] // (local_kv * head_width)
    head_cols = local_kv * group_size * head_width
    pairs = local_kv * group_size
    chunk = model_width // head_count
    scale_factor = 1.0 / math.sqrt(head_width)
    first_own = req_index * local_rows

    with jax.named_scope("projections"):
        hidden_f = hidden.astype(jnp.float32)
        normed = (hidden_f * rms_inv(hidden_f) * attn_gain).astype(jnp.bfloat16)
        own_requests = lax.dynamic_slice_in_dim(deal_order, first_own, local_rows)
        request_ids = jnp.arange(all_rows, dtype=jnp.int32)
        own_pick = own_requests[:, None] == request_ids[None, :]
        position = jnp.sum(jnp.where(own_pick, lengths[None, :], 0), axis=1).astype(jnp.float32)
        queries = jnp.dot(normed, w_query, preferred_element_type=jnp.float32).reshape(
            local_rows, local_kv, group_size, head_width
        )
        queries = norm_rotate(queries, query_gain, position).astype(jnp.bfloat16)
        new_keys = jnp.dot(normed, w_key, preferred_element_type=jnp.float32).reshape(
            local_rows, local_kv, head_width
        )
        new_keys = norm_rotate(new_keys, key_gain, position).astype(jnp.bfloat16)
        new_values = (
            jnp.dot(normed, w_value, preferred_element_type=jnp.float32)
            .astype(jnp.bfloat16)
            .reshape(local_rows, local_kv, head_width)
        )
        gate_logits = jnp.dot(normed, w_gate, preferred_element_type=jnp.float32)

    all_queries = req_gather(queries.reshape(local_rows, head_cols), req_count, inner, 0)
    all_queries = all_queries.reshape(all_rows, head_cols)

    with jax.named_scope("page_owners"):
        page_counts = (lengths + page_size - 1) // page_size
        slot_ids = jnp.arange(page_table.shape[1], dtype=jnp.int32)
        local_ids = page_table - req_index * pool_pages
        usable = (
            (slot_ids[None, :] < page_counts[:, None]) & (local_ids >= 0) & (local_ids < pool_pages)
        )
        keyed = jnp.where(usable, local_ids, pool_pages)
        page_ids = jnp.arange(pool_pages, dtype=jnp.int32)
        match = keyed[None, :, :] == page_ids[:, None, None]
        owned_requests = jnp.any(match, axis=2)
        owner_slot = jnp.sum(jnp.where(match, slot_ids[None, None, :], 0), axis=(1, 2))
        owner_length = jnp.sum(jnp.where(owned_requests, lengths[None, :], 0), axis=1)
        filled = jnp.clip(owner_length - owner_slot * page_size, 0, page_size)
        filled = jnp.where(jnp.any(owned_requests, axis=1), filled, 0)
        dealing = (request_ids[:, None] == deal_order[None, :]).astype(jnp.bfloat16)
        owned = (
            jnp.dot(owned_requests.astype(jnp.bfloat16), dealing, preferred_element_type=jnp.float32)
            > 0.5
        )
        page_queries = (
            jnp.dot(owned.astype(jnp.bfloat16), all_queries, preferred_element_type=jnp.float32)
            .astype(jnp.bfloat16)
            .reshape(pool_pages, local_kv, group_size, head_width)
        )

    with jax.named_scope("page_attention"):
        scores = (
            jnp.einsum("pkgd,ptkd->pkgt", page_queries, key_cache, preferred_element_type=jnp.float32)
            * scale_factor
        )
        live_mask = (
            jnp.arange(page_size, dtype=jnp.int32)[None, None, None, :] < filled[:, None, None, None]
        )
        scores = jnp.where(live_mask, scores, LOW_SCORE)
        page_peaks = jnp.max(scores, axis=-1)
        owned_b = owned[:, :, None, None]
        row_peaks = jnp.max(jnp.where(owned_b, page_peaks[:, None], LOW_SCORE), axis=0)
        row_shift = LOG_TWO * jnp.ceil(row_peaks / LOG_TWO)
        page_shift = jnp.max(jnp.where(owned_b, row_shift[None], LOW_SCORE), axis=1)
        weights = jnp.where(live_mask, jnp.exp(scores - page_shift[..., None]), 0.0)
        page_totals = jnp.sum(weights, axis=-1)
        page_numerators = jnp.einsum(
            "pkgt,ptkd->pkgd",
            weights.astype(jnp.bfloat16),
            value_cache,
            preferred_element_type=jnp.float32,
        )
        owned_f = owned.astype(jnp.float32)
        row_totals = jnp.dot(
            owned_f.T, page_totals.reshape(pool_pages, pairs), precision=lax.Precision.HIGHEST
        )
        row_numerators = jnp.dot(
            owned_f.T,
            page_numerators.reshape(pool_pages, head_cols),
            precision=lax.Precision.HIGHEST,
        )
        numerator_message = row_numerators.astype(jnp.bfloat16).reshape(req_count, local_rows, head_cols)
        stats_message = jnp.concatenate(
            [row_shift.reshape(req_count, local_rows, pairs), row_totals.reshape(req_count, local_rows, pairs)],
            axis=2,
        ).transpose(0, 2, 1)

    got_numerators, got_stats = exchange_many(
        (numerator_message, stats_message), (True, True), "req", req_count, 1
    )

    with jax.named_scope("combine"):
        got_numerators = got_numerators.astype(jnp.float32).reshape(
            req_count, local_rows, local_kv, group_size, head_width
        )
        got_stats = got_stats.transpose(0, 2, 1)
        got_shift = got_stats[:, :, :pairs].reshape(req_count, local_rows, local_kv, group_size)
        got_totals = got_stats[:, :, pairs:].reshape(req_count, local_rows, local_kv, group_size)
        self_scores = (
            jnp.einsum("rkgd,rkd->rkg", queries, new_keys, preferred_element_type=jnp.float32)
            * scale_factor
        )
        self_shift = LOG_TWO * jnp.ceil(self_scores / LOG_TWO)
        shift = jnp.maximum(jnp.max(got_shift, axis=0), self_shift)
        factor = jnp.exp(got_shift - shift[None])
        self_weight = jnp.exp(self_scores - shift)
        totals = jnp.sum(got_totals * factor, axis=0) + self_weight
        self_rounded = self_weight.astype(jnp.bfloat16).astype(jnp.float32)
        numerators = (
            jnp.sum(got_numerators * factor[..., None], axis=0)
            + self_rounded[..., None] * new_values.astype(jnp.float32)[:, :, None, :]
        )
        heads_out = (numerators / totals[..., None]).reshape(local_rows, head_cols)
        attended = (heads_out * jax.nn.sigmoid(gate_logits)).astype(jnp.bfloat16)
        projected = jnp.dot(attended, w_out, preferred_element_type=jnp.float32)
        projected = projected.reshape(local_rows, head_count, chunk).transpose(1, 0, 2)

    hidden_chunk = lax.dynamic_slice_in_dim(hidden_f, head_index * chunk, chunk, axis=1)
    mixed_all = residual_exchange(projected, hidden_chunk, head_count, 2)
    mixed_chunk = lax.dynamic_index_in_dim(mixed_all, head_index, axis=0, keepdims=False)

    with jax.named_scope("mlp"):
        mixed_rows = mixed_all.transpose(1, 0, 2).reshape(local_rows, model_width)
        mixed_f = mixed_rows.astype(jnp.float32)
        normed_two = (mixed_f * rms_inv(mixed_f) * mlp_gain).astype(jnp.bfloat16)
        gate_part = jnp.dot(normed_two, mlp_gate, preferred_element_type=jnp.float32)
        up_part = jnp.dot(normed_two, mlp_up, preferred_element_type=jnp.float32)
        inner_act = (jax.nn.silu(gate_part) * up_part).astype(jnp.bfloat16)
        down_part = jnp.dot(inner_act, mlp_down, preferred_element_type=jnp.float32)
        down_part = down_part.reshape(local_rows, head_count, chunk).transpose(1, 0, 2)

    with jax.named_scope("reorder"):
        wanted = first_own + jnp.arange(local_rows, dtype=jnp.int32)
        picker = (deal_order[None, :] == wanted[:, None]).astype(jnp.bfloat16)

    output_parts = tail_exchange(down_part, mixed_chunk, picker, head_count, req_count, inner, 3)
    return output_parts.transpose(1, 0, 2).reshape(local_rows, model_width)


def solution(mesh):
    return jax.shard_map(
        functools.partial(body, mesh.shape["req"], mesh.shape["head"], req_groups(mesh)),
        mesh=mesh,
        in_specs=(
            P("req", None),
            P(),
            P(),
            P(),
            P("req", None, "head", None),
            P("req", None, "head", None),
            P(),
            P(None, "head"),
            P(None, "head"),
            P(None, "head"),
            P(None, "head"),
            P("head", None),
            P(),
            P(),
            P(),
            P(None, "head"),
            P(None, "head"),
            P("head", None),
        ),
        out_specs=P("req", None),
        check_vma=False,
    )
```

```python
import functools
import math

import jax
import jax.numpy as jnp
from jax import lax
from jax.experimental import pallas as pl
from jax.experimental.pallas import tpu as pltpu
from jax.sharding import PartitionSpec as P

EPSILON = 1e-06
ROPE_BASE = 1000000.0
LOW_SCORE = -1e30
LOG_TWO = math.log(2.0)
MESH_IDS = pl.DeviceIdType.MESH


def rms_inv(values):
    return lax.rsqrt(jnp.mean(values * values, axis=-1, keepdims=True) + EPSILON)


def rotate(values, position):
    half_dim = values.shape[-1] // 2
    exponent = jnp.arange(half_dim, dtype=jnp.float32) * (2.0 / values.shape[-1])
    frequency = ROPE_BASE ** (-exponent)
    angles = position[:, None] * frequency[None, :]
    ones_tail = (1,) * (values.ndim - 2)
    angles = angles.reshape((angles.shape[0],) + ones_tail + (half_dim,))
    cosine = jnp.cos(angles)
    sine_vals = jnp.sin(angles)
    front_half = values[..., :half_dim]
    back_half = values[..., half_dim:]
    return jnp.concatenate(
        [front_half * cosine - back_half * sine_vals, back_half * cosine + front_half * sine_vals],
        axis=-1,
    )


def norm_rotate(values, gain_vec, position):
    return rotate(values * rms_inv(values) * gain_vec, position)


def exchange_kernel(axis, count, spreads, *refs):
    arrays = len(spreads)
    sources, outputs = refs[:arrays], refs[arrays : 2 * arrays]
    send_sems, recv_sems = refs[2 * arrays], refs[2 * arrays + 1]
    me = lax.axis_index(axis)
    barrier = pltpu.get_barrier_semaphore()
    for offset in range(1, count):
        peer = lax.rem(me + offset, count)
        pl.semaphore_signal(barrier, inc=1, device_id={axis: peer}, device_id_type=MESH_IDS)
    pl.semaphore_wait(barrier, count - 1)
    copies = []
    for offset in range(1, count):
        peer = lax.rem(me + offset, count)
        for which in range(arrays):
            src_ref, out_ref = sources[which], outputs[which]
            copy = pltpu.make_async_remote_copy(
                src_ref=src_ref.at[peer] if spreads[which] else src_ref,
                dst_ref=out_ref.at[me],
                send_sem=send_sems.at[which, offset],
                recv_sem=recv_sems.at[which, offset],
                device_id={axis: peer},
                device_id_type=MESH_IDS,
            )
            copy.start()
            copies.append(copy)
    for which in range(arrays):
        src_ref, out_ref = sources[which], outputs[which]
        out_ref[me] = src_ref[me] if spreads[which] else src_ref[...]
    for copy in copies:
        copy.wait()


def exchange_many(arrays, spreads, axis, count, ident):
    shapes = []
    for values, spread in zip(arrays, spreads):
        block = values.shape[1:] if spread else values.shape
        shapes.append(jax.ShapeDtypeStruct((count,) + tuple(block), values.dtype))
    return pl.pallas_call(
        functools.partial(exchange_kernel, axis, count, tuple(spreads)),
        out_shape=tuple(shapes),
        in_specs=[pl.BlockSpec(memory_space=pltpu.VMEM)] * len(arrays),
        out_specs=tuple(pl.BlockSpec(memory_space=pltpu.VMEM) for _ in arrays),
        scratch_shapes=[
            pltpu.SemaphoreType.DMA((len(arrays), count)),
            pltpu.SemaphoreType.DMA((len(arrays), count)),
        ],
        compiler_params=pltpu.CompilerParams(collective_id=ident, has_side_effects=True),
    )(*arrays)


def exchange(values, axis, count, spread, ident):
    return exchange_many((values,), (spread,), axis, count, ident)[0]


def greet(peers):
    barrier = pltpu.get_barrier_semaphore()
    for axis, peer in peers:
        pl.semaphore_signal(barrier, inc=1, device_id={axis: peer}, device_id_type=MESH_IDS)
    pl.semaphore_wait(barrier, len(peers))


def peers_of(axis, count):
    me = lax.axis_index(axis)
    return me, [(offset, lax.rem(me + offset, count)) for offset in range(1, count)]


def send_all(axis, peers, src_of, dst, send_sems, recv_sems, phase):
    copies = []
    for offset, peer in peers:
        copy = pltpu.make_async_remote_copy(
            src_ref=src_of(peer),
            dst_ref=dst,
            send_sem=send_sems.at[phase, offset],
            recv_sem=recv_sems.at[phase, offset],
            device_id={axis: peer},
            device_id_type=MESH_IDS,
        )
        copy.start()
        copies.append(copy)
    for copy in copies:
        copy.wait()


def residual_kernel(count, parts_ref, hidden_ref, out_ref, summed, send_sems, recv_sems):
    me, peers = peers_of("head", count)
    cols = out_ref.shape[1] // count
    mine = pl.ds(pl.multiple_of(me * cols, cols), cols)
    greet([("head", peer) for _, peer in peers])
    summed[me] = parts_ref[:, mine]
    send_all(
        "head", peers, lambda peer: parts_ref.at[:, pl.ds(peer * cols, cols)], summed.at[me], send_sems, recv_sems, 0
    )
    out_ref[:, mine] = (hidden_ref[:, mine].astype(jnp.float32) + jnp.sum(summed[...], axis=0)).astype(
        out_ref.dtype
    )
    send_all("head", peers, lambda peer: out_ref.at[:, mine], out_ref.at[:, mine], send_sems, recv_sems, 1)


def residual_exchange(parts, hidden, count, ident):
    rows, width = parts.shape
    return pl.pallas_call(
        functools.partial(residual_kernel, count),
        out_shape=jax.ShapeDtypeStruct((rows, width), jnp.bfloat16),
        in_specs=[pl.BlockSpec(memory_space=pltpu.VMEM)] * 2,
        out_specs=pl.BlockSpec(memory_space=pltpu.VMEM),
        scratch_shapes=[
            pltpu.VMEM((count, rows, width // count), jnp.float32),
            pltpu.SemaphoreType.DMA((2, count)),
            pltpu.SemaphoreType.DMA((2, count)),
        ],
        compiler_params=pltpu.CompilerParams(collective_id=ident, has_side_effects=True),
    )(parts, hidden)


def tail_kernel(
    head_count, req_count, parts_ref, mixed_ref, order_ref, out_ref, summed, results, send_sems, recv_sems
):
    head_me, head_peers = peers_of("head", head_count)
    req_me, req_peers = peers_of("req", req_count)
    rows, width = out_ref.shape
    cols = width // head_count
    mine = pl.ds(pl.multiple_of(head_me * cols, cols), cols)
    greet([("head", peer) for _, peer in head_peers] + [("req", peer) for _, peer in req_peers])
    summed[head_me] = parts_ref[:, mine]
    send_all(
        "head",
        head_peers,
        lambda peer: parts_ref.at[:, pl.ds(peer * cols, cols)],
        summed.at[head_me],
        send_sems,
        recv_sems,
        0,
    )
    results[req_me] = (mixed_ref[:, mine].astype(jnp.float32) + jnp.sum(summed[...], axis=0)).astype(
        results.dtype
    )
    send_all("req", req_peers, lambda peer: results.at[req_me], results.at[req_me], send_sems, recv_sems, 1)
    wanted = req_me * rows + lax.broadcasted_iota(jnp.int32, (rows, req_count * rows), 0)
    picker = (order_ref[...] == wanted).astype(jnp.bfloat16)
    out_ref[:, mine] = jnp.dot(
        picker, results[...].reshape(req_count * rows, cols), preferred_element_type=jnp.float32
    ).astype(out_ref.dtype)
    send_all("head", head_peers, lambda peer: out_ref.at[:, mine], out_ref.at[:, mine], send_sems, recv_sems, 2)


def tail_exchange(parts, mixed, order, head_count, req_count, ident):
    rows, width = parts.shape
    most = max(head_count, req_count)
    return pl.pallas_call(
        functools.partial(tail_kernel, head_count, req_count),
        out_shape=jax.ShapeDtypeStruct((rows, width), jnp.bfloat16),
        in_specs=[pl.BlockSpec(memory_space=pltpu.VMEM)] * 3,
        out_specs=pl.BlockSpec(memory_space=pltpu.VMEM),
        scratch_shapes=[
            pltpu.VMEM((head_count, rows, width // head_count), jnp.float32),
            pltpu.VMEM((req_count, rows, width // head_count), jnp.bfloat16),
            pltpu.SemaphoreType.DMA((3, most)),
            pltpu.SemaphoreType.DMA((3, most)),
        ],
        compiler_params=pltpu.CompilerParams(collective_id=ident, has_side_effects=True),
    )(parts, mixed, order)


def body(
    req_count,
    head_count,
    hidden,
    deal_order,
    lengths,
    page_table,
    key_cache,
    value_cache,
    attn_gain,
    w_query,
    w_key,
    w_value,
    w_gate,
    w_out,
    query_gain,
    key_gain,
    mlp_gain,
    mlp_gate,
    mlp_up,
    mlp_down,
):
    local_rows, model_width = hidden.shape
    req_index = lax.axis_index("req")
    head_index = lax.axis_index("head")
    all_rows = local_rows * req_count
    head_width = query_gain.shape[0]
    pool_pages, page_size, local_kv = key_cache.shape[:3]
    group_size = w_query.shape[1] // (local_kv * head_width)
    head_cols = local_kv * group_size * head_width
    pairs = local_kv * group_size
    chunk = model_width // head_count
    scale_factor = 1.0 / math.sqrt(head_width)
    first_own = req_index * local_rows

    with jax.named_scope("projections"):
        hidden_f = hidden.astype(jnp.float32)
        normed = (hidden_f * rms_inv(hidden_f) * attn_gain).astype(jnp.bfloat16)
        own_requests = lax.dynamic_slice_in_dim(deal_order, first_own, local_rows)
        request_ids = jnp.arange(all_rows, dtype=jnp.int32)
        own_pick = own_requests[:, None] == request_ids[None, :]
        position = jnp.sum(jnp.where(own_pick, lengths[None, :], 0), axis=1).astype(jnp.float32)
        queries = jnp.dot(normed, w_query, preferred_element_type=jnp.float32).reshape(
            local_rows, local_kv, group_size, head_width
        )
        queries = norm_rotate(queries, query_gain, position).astype(jnp.bfloat16)
        new_keys = jnp.dot(normed, w_key, preferred_element_type=jnp.float32).reshape(
            local_rows, local_kv, head_width
        )
        new_keys = norm_rotate(new_keys, key_gain, position).astype(jnp.bfloat16)
        new_values = (
            jnp.dot(normed, w_value, preferred_element_type=jnp.float32)
            .astype(jnp.bfloat16)
            .reshape(local_rows, local_kv, head_width)
        )
        gate_logits = jnp.dot(normed, w_gate, preferred_element_type=jnp.float32)

    all_queries = exchange(queries.reshape(local_rows, head_cols), "req", req_count, False, 0)
    all_queries = all_queries.reshape(all_rows, head_cols)

    with jax.named_scope("page_owners"):
        page_counts = (lengths + page_size - 1) // page_size
        slot_ids = jnp.arange(page_table.shape[1], dtype=jnp.int32)
        local_ids = page_table - req_index * pool_pages
        usable = (
            (slot_ids[None, :] < page_counts[:, None]) & (local_ids >= 0) & (local_ids < pool_pages)
        )
        keyed = jnp.where(usable, local_ids, pool_pages)
        page_ids = jnp.arange(pool_pages, dtype=jnp.int32)
        match = keyed[None, :, :] == page_ids[:, None, None]
        owned_requests = jnp.any(match, axis=2)
        owner_slot = jnp.sum(jnp.where(match, slot_ids[None, None, :], 0), axis=(1, 2))
        owner_length = jnp.sum(jnp.where(owned_requests, lengths[None, :], 0), axis=1)
        filled = jnp.clip(owner_length - owner_slot * page_size, 0, page_size)
        filled = jnp.where(jnp.any(owned_requests, axis=1), filled, 0)
        dealing = (request_ids[:, None] == deal_order[None, :]).astype(jnp.bfloat16)
        owned = (
            jnp.dot(owned_requests.astype(jnp.bfloat16), dealing, preferred_element_type=jnp.float32)
            > 0.5
        )
        page_queries = (
            jnp.dot(owned.astype(jnp.bfloat16), all_queries, preferred_element_type=jnp.float32)
            .astype(jnp.bfloat16)
            .reshape(pool_pages, local_kv, group_size, head_width)
        )

    with jax.named_scope("page_attention"):
        scores = (
            jnp.einsum("pkgd,ptkd->pkgt", page_queries, key_cache, preferred_element_type=jnp.float32)
            * scale_factor
        )
        live_mask = (
            jnp.arange(page_size, dtype=jnp.int32)[None, None, None, :] < filled[:, None, None, None]
        )
        scores = jnp.where(live_mask, scores, LOW_SCORE)
        page_peaks = jnp.max(scores, axis=-1)
        owned_b = owned[:, :, None, None]
        row_peaks = jnp.max(jnp.where(owned_b, page_peaks[:, None], LOW_SCORE), axis=0)
        row_shift = LOG_TWO * jnp.ceil(row_peaks / LOG_TWO)
        page_shift = jnp.max(jnp.where(owned_b, row_shift[None], LOW_SCORE), axis=1)
        weights = jnp.where(live_mask, jnp.exp(scores - page_shift[..., None]), 0.0)
        page_totals = jnp.sum(weights, axis=-1)
        page_numerators = jnp.einsum(
            "pkgt,ptkd->pkgd",
            weights.astype(jnp.bfloat16),
            value_cache,
            preferred_element_type=jnp.float32,
        )
        owned_f = owned.astype(jnp.float32)
        row_totals = jnp.dot(
            owned_f.T, page_totals.reshape(pool_pages, pairs), precision=lax.Precision.HIGHEST
        )
        row_numerators = jnp.dot(
            owned_f.T,
            page_numerators.reshape(pool_pages, head_cols),
            precision=lax.Precision.HIGHEST,
        )
        numerator_message = row_numerators.astype(jnp.bfloat16).reshape(req_count, local_rows, head_cols)
        stats_message = jnp.concatenate(
            [row_shift.reshape(req_count, local_rows, pairs), row_totals.reshape(req_count, local_rows, pairs)],
            axis=2,
        ).transpose(0, 2, 1)

    got_numerators, got_stats = exchange_many(
        (numerator_message, stats_message), (True, True), "req", req_count, 1
    )

    with jax.named_scope("combine"):
        got_numerators = got_numerators.astype(jnp.float32).reshape(
            req_count, local_rows, local_kv, group_size, head_width
        )
        got_stats = got_stats.transpose(0, 2, 1)
        got_shift = got_stats[:, :, :pairs].reshape(req_count, local_rows, local_kv, group_size)
        got_totals = got_stats[:, :, pairs:].reshape(req_count, local_rows, local_kv, group_size)
        self_scores = (
            jnp.einsum("rkgd,rkd->rkg", queries, new_keys, preferred_element_type=jnp.float32)
            * scale_factor
        )
        self_shift = LOG_TWO * jnp.ceil(self_scores / LOG_TWO)
        shift = jnp.maximum(jnp.max(got_shift, axis=0), self_shift)
        factor = jnp.exp(got_shift - shift[None])
        self_weight = jnp.exp(self_scores - shift)
        totals = jnp.sum(got_totals * factor, axis=0) + self_weight
        self_rounded = self_weight.astype(jnp.bfloat16).astype(jnp.float32)
        numerators = (
            jnp.sum(got_numerators * factor[..., None], axis=0)
            + self_rounded[..., None] * new_values.astype(jnp.float32)[:, :, None, :]
        )
        heads_out = (numerators / totals[..., None]).reshape(local_rows, head_cols)
        attended = (heads_out * jax.nn.sigmoid(gate_logits)).astype(jnp.bfloat16)
        projected = jnp.dot(attended, w_out, preferred_element_type=jnp.float32)

    mixed_rows = residual_exchange(projected, hidden, head_count, 2)

    with jax.named_scope("mlp"):
        mixed_f = mixed_rows.astype(jnp.float32)
        normed_two = (mixed_f * rms_inv(mixed_f) * mlp_gain).astype(jnp.bfloat16)
        gate_part = jnp.dot(normed_two, mlp_gate, preferred_element_type=jnp.float32)
        up_part = jnp.dot(normed_two, mlp_up, preferred_element_type=jnp.float32)
        inner_act = (jax.nn.silu(gate_part) * up_part).astype(jnp.bfloat16)
        down_part = jnp.dot(inner_act, mlp_down, preferred_element_type=jnp.float32)

    return tail_exchange(down_part, mixed_rows, deal_order.reshape(1, all_rows), head_count, req_count, 3)


def solution(mesh):
    return jax.shard_map(
        functools.partial(body, mesh.shape["req"], mesh.shape["head"]),
        mesh=mesh,
        in_specs=(
            P("req", None),
            P(),
            P(),
            P(),
            P("req", None, "head", None),
            P("req", None, "head", None),
            P(),
            P(None, "head"),
            P(None, "head"),
            P(None, "head"),
            P(None, "head"),
            P("head", None),
            P(),
            P(),
            P(),
            P(None, "head"),
            P(None, "head"),
            P("head", None),
        ),
        out_specs=P("req", None),
        check_vma=False,
    )
```

```python
import functools
import math

import jax
import jax.numpy as jnp
from jax import lax
from jax.experimental import pallas as pl
from jax.experimental.pallas import tpu as pltpu
from jax.sharding import PartitionSpec as P

EPSILON = 1e-06
ROPE_BASE = 1000000.0
LOW_SCORE = -1e30
LOG_TWO = math.log(2.0)
MESH_IDS = pl.DeviceIdType.MESH


def rms_inv(values):
    return lax.rsqrt(jnp.mean(values * values, axis=-1, keepdims=True) + EPSILON)


def rotate(values, position):
    half_dim = values.shape[-1] // 2
    exponent = jnp.arange(half_dim, dtype=jnp.float32) * (2.0 / values.shape[-1])
    frequency = ROPE_BASE ** (-exponent)
    angles = position[:, None] * frequency[None, :]
    ones_tail = (1,) * (values.ndim - 2)
    angles = angles.reshape((angles.shape[0],) + ones_tail + (half_dim,))
    cosine = jnp.cos(angles)
    sine_vals = jnp.sin(angles)
    front_half = values[..., :half_dim]
    back_half = values[..., half_dim:]
    return jnp.concatenate(
        [front_half * cosine - back_half * sine_vals, back_half * cosine + front_half * sine_vals],
        axis=-1,
    )


def norm_rotate(values, gain_vec, position):
    return rotate(values * rms_inv(values) * gain_vec, position)


def exchange_kernel(axis, count, spreads, *refs):
    arrays = len(spreads)
    sources, outputs = refs[:arrays], refs[arrays : 2 * arrays]
    send_sems, recv_sems = refs[2 * arrays], refs[2 * arrays + 1]
    me = lax.axis_index(axis)
    barrier = pltpu.get_barrier_semaphore()
    for offset in range(1, count):
        peer = lax.rem(me + offset, count)
        pl.semaphore_signal(barrier, inc=1, device_id={axis: peer}, device_id_type=MESH_IDS)
    pl.semaphore_wait(barrier, count - 1)
    copies = []
    for offset in range(1, count):
        peer = lax.rem(me + offset, count)
        for which in range(arrays):
            src_ref, out_ref = sources[which], outputs[which]
            copy = pltpu.make_async_remote_copy(
                src_ref=src_ref.at[peer] if spreads[which] else src_ref,
                dst_ref=out_ref.at[me],
                send_sem=send_sems.at[which, offset],
                recv_sem=recv_sems.at[which, offset],
                device_id={axis: peer},
                device_id_type=MESH_IDS,
            )
            copy.start()
            copies.append(copy)
    for which in range(arrays):
        src_ref, out_ref = sources[which], outputs[which]
        out_ref[me] = src_ref[me] if spreads[which] else src_ref[...]
    for copy in copies:
        copy.wait()


def exchange_many(arrays, spreads, axis, count, ident):
    shapes = []
    for values, spread in zip(arrays, spreads):
        block = values.shape[1:] if spread else values.shape
        shapes.append(jax.ShapeDtypeStruct((count,) + tuple(block), values.dtype))
    return pl.pallas_call(
        functools.partial(exchange_kernel, axis, count, tuple(spreads)),
        out_shape=tuple(shapes),
        in_specs=[pl.BlockSpec(memory_space=pltpu.VMEM)] * len(arrays),
        out_specs=tuple(pl.BlockSpec(memory_space=pltpu.VMEM) for _ in arrays),
        scratch_shapes=[
            pltpu.SemaphoreType.DMA((len(arrays), count)),
            pltpu.SemaphoreType.DMA((len(arrays), count)),
        ],
        compiler_params=pltpu.CompilerParams(collective_id=ident, has_side_effects=True),
    )(*arrays)


def exchange(values, axis, count, spread, ident):
    return exchange_many((values,), (spread,), axis, count, ident)[0]


def greet(peers):
    barrier = pltpu.get_barrier_semaphore()
    for axis, peer in peers:
        pl.semaphore_signal(barrier, inc=1, device_id={axis: peer}, device_id_type=MESH_IDS)
    pl.semaphore_wait(barrier, len(peers))


def peers_of(axis, count):
    me = lax.axis_index(axis)
    return me, [(offset, lax.rem(me + offset, count)) for offset in range(1, count)]


def send_all(axis, peers, src_of, dst, send_sems, recv_sems, phase):
    copies = []
    for offset, peer in peers:
        copy = pltpu.make_async_remote_copy(
            src_ref=src_of(peer),
            dst_ref=dst,
            send_sem=send_sems.at[phase, offset],
            recv_sem=recv_sems.at[phase, offset],
            device_id={axis: peer},
            device_id_type=MESH_IDS,
        )
        copy.start()
        copies.append(copy)
    for copy in copies:
        copy.wait()


def residual_kernel(count, parts_ref, hidden_ref, out_ref, summed, send_sems, recv_sems):
    me, peers = peers_of("head", count)
    cols = out_ref.shape[1] // count
    mine = pl.ds(pl.multiple_of(me * cols, cols), cols)
    greet([("head", peer) for _, peer in peers])
    summed[me] = parts_ref[:, mine]
    send_all(
        "head", peers, lambda peer: parts_ref.at[:, pl.ds(peer * cols, cols)], summed.at[me], send_sems, recv_sems, 0
    )
    out_ref[:, mine] = (hidden_ref[:, mine].astype(jnp.float32) + jnp.sum(summed[...], axis=0)).astype(
        out_ref.dtype
    )
    send_all("head", peers, lambda peer: out_ref.at[:, mine], out_ref.at[:, mine], send_sems, recv_sems, 1)


def residual_exchange(parts, hidden, count, ident):
    rows, width = parts.shape
    return pl.pallas_call(
        functools.partial(residual_kernel, count),
        out_shape=jax.ShapeDtypeStruct((rows, width), jnp.bfloat16),
        in_specs=[pl.BlockSpec(memory_space=pltpu.VMEM)] * 2,
        out_specs=pl.BlockSpec(memory_space=pltpu.VMEM),
        scratch_shapes=[
            pltpu.VMEM((count, rows, width // count), jnp.float32),
            pltpu.SemaphoreType.DMA((2, count)),
            pltpu.SemaphoreType.DMA((2, count)),
        ],
        compiler_params=pltpu.CompilerParams(collective_id=ident, has_side_effects=True),
    )(parts, hidden)


def attend_kernel(
    req_count, head_count, group_size, scale_factor, num_ref, stats_ref, query_ref, key_ref, value_ref, gate_ref,
    w_out_ref, hidden_ref, out_ref, got_num, got_stats, projected, summed, send_sems, recv_sems,
):
    req_me, req_peers = peers_of("req", req_count)
    head_me, head_peers = peers_of("head", head_count)
    rows, width = out_ref.shape
    cols = width // head_count
    pairs = stats_ref.shape[1] // 2
    head_width = query_ref.shape[1] // pairs
    mine = pl.ds(pl.multiple_of(head_me * cols, cols), cols)
    greet([("req", peer) for _, peer in req_peers] + [("head", peer) for _, peer in head_peers])
    got_num[req_me] = num_ref[req_me]
    got_stats[req_me] = stats_ref[req_me]
    copies = []
    for offset, peer in req_peers:
        for which, (src_ref, dst_ref) in enumerate(((num_ref, got_num), (stats_ref, got_stats))):
            copy = pltpu.make_async_remote_copy(
                src_ref=src_ref.at[peer],
                dst_ref=dst_ref.at[req_me],
                send_sem=send_sems.at[which, offset],
                recv_sem=recv_sems.at[which, offset],
                device_id={"req": peer},
                device_id_type=MESH_IDS,
            )
            copy.start()
            copies.append(copy)
    for copy in copies:
        copy.wait()
    eye = (
        lax.broadcasted_iota(jnp.int32, (rows, rows), 0) == lax.broadcasted_iota(jnp.int32, (rows, rows), 1)
    ).astype(jnp.float32)
    flip = (((1,), (1,)), ((), ()))
    heads = []
    for pair in range(pairs):
        kv = pair // group_size
        lanes = slice(pair * head_width, (pair + 1) * head_width)
        kv_lanes = slice(kv * head_width, (kv + 1) * head_width)
        shifts = lax.dot_general(
            eye, got_stats[:, pair, :], flip, precision=lax.Precision.HIGHEST, preferred_element_type=jnp.float32
        )
        totals = lax.dot_general(
            eye,
            got_stats[:, pairs + pair, :],
            flip,
            precision=lax.Precision.HIGHEST,
            preferred_element_type=jnp.float32,
        )
        query = query_ref[:, lanes].astype(jnp.float32)
        self_score = jnp.sum(query * key_ref[:, kv_lanes].astype(jnp.float32), axis=1, keepdims=True) * scale_factor
        self_shift = LOG_TWO * jnp.ceil(self_score / LOG_TWO)
        shift = jnp.maximum(jnp.max(shifts, axis=1, keepdims=True), self_shift)
        factor = jnp.exp(shifts - shift)
        self_weight = jnp.exp(self_score - shift)
        total = jnp.sum(totals * factor, axis=1, keepdims=True) + self_weight
        acc = self_weight.astype(jnp.bfloat16).astype(jnp.float32) * value_ref[:, kv_lanes].astype(jnp.float32)
        for source in range(req_count):
            acc = acc + factor[:, source : source + 1] * got_num[source, :, lanes].astype(jnp.float32)
        heads.append(acc / total)
    heads_out = jnp.concatenate(heads, axis=1)
    gate = gate_ref[...]
    attended = (heads_out * (1.0 / (1.0 + jnp.exp(-gate)))).astype(jnp.bfloat16)
    projected[...] = jnp.dot(attended, w_out_ref[...], preferred_element_type=jnp.float32)
    summed[head_me] = projected[:, mine]
    send_all(
        "head", head_peers, lambda peer: projected.at[:, pl.ds(peer * cols, cols)], summed.at[head_me],
        send_sems, recv_sems, 2,
    )
    out_ref[:, mine] = (hidden_ref[:, mine].astype(jnp.float32) + jnp.sum(summed[...], axis=0)).astype(
        out_ref.dtype
    )
    send_all("head", head_peers, lambda peer: out_ref.at[:, mine], out_ref.at[:, mine], send_sems, recv_sems, 3)


def attend_exchange(
    num, stats, queries, keys, values, gate, w_out, hidden, head_count, group_size, scale_factor, ident
):
    req_count = num.shape[0]
    rows, width = hidden.shape
    most = max(head_count, req_count)
    return pl.pallas_call(
        functools.partial(attend_kernel, req_count, head_count, group_size, scale_factor),
        out_shape=jax.ShapeDtypeStruct((rows, width), jnp.bfloat16),
        in_specs=[pl.BlockSpec(memory_space=pltpu.VMEM)] * 8,
        out_specs=pl.BlockSpec(memory_space=pltpu.VMEM),
        scratch_shapes=[
            pltpu.VMEM(num.shape, num.dtype),
            pltpu.VMEM(stats.shape, stats.dtype),
            pltpu.VMEM((rows, width), jnp.float32),
            pltpu.VMEM((head_count, rows, width // head_count), jnp.float32),
            pltpu.SemaphoreType.DMA((4, most)),
            pltpu.SemaphoreType.DMA((4, most)),
        ],
        compiler_params=pltpu.CompilerParams(collective_id=ident, has_side_effects=True),
    )(num, stats, queries, keys, values, gate, w_out, hidden)


def tail_kernel(
    head_count, req_count, parts_ref, mixed_ref, order_ref, out_ref, summed, results, send_sems, recv_sems
):
    head_me, head_peers = peers_of("head", head_count)
    req_me, req_peers = peers_of("req", req_count)
    rows, width = out_ref.shape
    cols = width // head_count
    mine = pl.ds(pl.multiple_of(head_me * cols, cols), cols)
    greet([("head", peer) for _, peer in head_peers] + [("req", peer) for _, peer in req_peers])
    summed[head_me] = parts_ref[:, mine]
    send_all(
        "head",
        head_peers,
        lambda peer: parts_ref.at[:, pl.ds(peer * cols, cols)],
        summed.at[head_me],
        send_sems,
        recv_sems,
        0,
    )
    results[req_me] = (mixed_ref[:, mine].astype(jnp.float32) + jnp.sum(summed[...], axis=0)).astype(
        results.dtype
    )
    send_all("req", req_peers, lambda peer: results.at[req_me], results.at[req_me], send_sems, recv_sems, 1)
    wanted = req_me * rows + lax.broadcasted_iota(jnp.int32, (rows, req_count * rows), 0)
    picker = (order_ref[...] == wanted).astype(jnp.bfloat16)
    out_ref[:, mine] = jnp.dot(
        picker, results[...].reshape(req_count * rows, cols), preferred_element_type=jnp.float32
    ).astype(out_ref.dtype)
    send_all("head", head_peers, lambda peer: out_ref.at[:, mine], out_ref.at[:, mine], send_sems, recv_sems, 2)


def tail_exchange(parts, mixed, order, head_count, req_count, ident):
    rows, width = parts.shape
    most = max(head_count, req_count)
    return pl.pallas_call(
        functools.partial(tail_kernel, head_count, req_count),
        out_shape=jax.ShapeDtypeStruct((rows, width), jnp.bfloat16),
        in_specs=[pl.BlockSpec(memory_space=pltpu.VMEM)] * 3,
        out_specs=pl.BlockSpec(memory_space=pltpu.VMEM),
        scratch_shapes=[
            pltpu.VMEM((head_count, rows, width // head_count), jnp.float32),
            pltpu.VMEM((req_count, rows, width // head_count), jnp.bfloat16),
            pltpu.SemaphoreType.DMA((3, most)),
            pltpu.SemaphoreType.DMA((3, most)),
        ],
        compiler_params=pltpu.CompilerParams(collective_id=ident, has_side_effects=True),
    )(parts, mixed, order)


def body(
    req_count,
    head_count,
    hidden,
    deal_order,
    lengths,
    page_table,
    key_cache,
    value_cache,
    attn_gain,
    w_query,
    w_key,
    w_value,
    w_gate,
    w_out,
    query_gain,
    key_gain,
    mlp_gain,
    mlp_gate,
    mlp_up,
    mlp_down,
):
    local_rows, model_width = hidden.shape
    req_index = lax.axis_index("req")
    head_index = lax.axis_index("head")
    all_rows = local_rows * req_count
    head_width = query_gain.shape[0]
    pool_pages, page_size, local_kv = key_cache.shape[:3]
    group_size = w_query.shape[1] // (local_kv * head_width)
    head_cols = local_kv * group_size * head_width
    pairs = local_kv * group_size
    chunk = model_width // head_count
    scale_factor = 1.0 / math.sqrt(head_width)
    first_own = req_index * local_rows

    with jax.named_scope("projections"):
        hidden_f = hidden.astype(jnp.float32)
        normed = (hidden_f * rms_inv(hidden_f) * attn_gain).astype(jnp.bfloat16)
        own_requests = lax.dynamic_slice_in_dim(deal_order, first_own, local_rows)
        request_ids = jnp.arange(all_rows, dtype=jnp.int32)
        own_pick = own_requests[:, None] == request_ids[None, :]
        position = jnp.sum(jnp.where(own_pick, lengths[None, :], 0), axis=1).astype(jnp.float32)
        queries = jnp.dot(normed, w_query, preferred_element_type=jnp.float32).reshape(
            local_rows, local_kv, group_size, head_width
        )
        queries = norm_rotate(queries, query_gain, position).astype(jnp.bfloat16)
        new_keys = jnp.dot(normed, w_key, preferred_element_type=jnp.float32).reshape(
            local_rows, local_kv, head_width
        )
        new_keys = norm_rotate(new_keys, key_gain, position).astype(jnp.bfloat16)
        new_values = (
            jnp.dot(normed, w_value, preferred_element_type=jnp.float32)
            .astype(jnp.bfloat16)
            .reshape(local_rows, local_kv, head_width)
        )
        gate_logits = jnp.dot(normed, w_gate, preferred_element_type=jnp.float32)

    all_queries = exchange(queries.reshape(local_rows, head_cols), "req", req_count, False, 0)
    all_queries = all_queries.reshape(all_rows, head_cols)

    with jax.named_scope("page_owners"):
        page_counts = (lengths + page_size - 1) // page_size
        slot_ids = jnp.arange(page_table.shape[1], dtype=jnp.int32)
        local_ids = page_table - req_index * pool_pages
        usable = (
            (slot_ids[None, :] < page_counts[:, None]) & (local_ids >= 0) & (local_ids < pool_pages)
        )
        keyed = jnp.where(usable, local_ids, pool_pages)
        page_ids = jnp.arange(pool_pages, dtype=jnp.int32)
        match = keyed[None, :, :] == page_ids[:, None, None]
        owned_requests = jnp.any(match, axis=2)
        owner_slot = jnp.sum(jnp.where(match, slot_ids[None, None, :], 0), axis=(1, 2))
        owner_length = jnp.sum(jnp.where(owned_requests, lengths[None, :], 0), axis=1)
        filled = jnp.clip(owner_length - owner_slot * page_size, 0, page_size)
        filled = jnp.where(jnp.any(owned_requests, axis=1), filled, 0)
        dealing = (request_ids[:, None] == deal_order[None, :]).astype(jnp.bfloat16)
        owned = (
            jnp.dot(owned_requests.astype(jnp.bfloat16), dealing, preferred_element_type=jnp.float32)
            > 0.5
        )
        page_queries = (
            jnp.dot(owned.astype(jnp.bfloat16), all_queries, preferred_element_type=jnp.float32)
            .astype(jnp.bfloat16)
            .reshape(pool_pages, local_kv, group_size, head_width)
        )

    with jax.named_scope("page_attention"):
        scores = (
            jnp.einsum("pkgd,ptkd->pkgt", page_queries, key_cache, preferred_element_type=jnp.float32)
            * scale_factor
        )
        live_mask = (
            jnp.arange(page_size, dtype=jnp.int32)[None, None, None, :] < filled[:, None, None, None]
        )
        scores = jnp.where(live_mask, scores, LOW_SCORE)
        page_peaks = jnp.max(scores, axis=-1)
        owned_b = owned[:, :, None, None]
        row_peaks = jnp.max(jnp.where(owned_b, page_peaks[:, None], LOW_SCORE), axis=0)
        row_shift = LOG_TWO * jnp.ceil(row_peaks / LOG_TWO)
        page_shift = jnp.max(jnp.where(owned_b, row_shift[None], LOW_SCORE), axis=1)
        weights = jnp.where(live_mask, jnp.exp(scores - page_shift[..., None]), 0.0)
        page_totals = jnp.sum(weights, axis=-1)
        page_numerators = jnp.einsum(
            "pkgt,ptkd->pkgd",
            weights.astype(jnp.bfloat16),
            value_cache,
            preferred_element_type=jnp.float32,
        )
        owned_f = owned.astype(jnp.float32)
        row_totals = jnp.dot(
            owned_f.T, page_totals.reshape(pool_pages, pairs), precision=lax.Precision.HIGHEST
        )
        row_numerators = jnp.dot(
            owned_f.T,
            page_numerators.reshape(pool_pages, head_cols),
            precision=lax.Precision.HIGHEST,
        )
        numerator_message = row_numerators.astype(jnp.bfloat16).reshape(req_count, local_rows, head_cols)
        stats_message = jnp.concatenate(
            [row_shift.reshape(req_count, local_rows, pairs), row_totals.reshape(req_count, local_rows, pairs)],
            axis=2,
        ).transpose(0, 2, 1)

    mixed_rows = attend_exchange(
        numerator_message,
        stats_message,
        queries.reshape(local_rows, head_cols),
        new_keys.reshape(local_rows, local_kv * head_width),
        new_values.reshape(local_rows, local_kv * head_width),
        gate_logits,
        w_out,
        hidden,
        head_count,
        group_size,
        scale_factor,
        1,
    )

    with jax.named_scope("mlp"):
        mixed_f = mixed_rows.astype(jnp.float32)
        normed_two = (mixed_f * rms_inv(mixed_f) * mlp_gain).astype(jnp.bfloat16)
        gate_part = jnp.dot(normed_two, mlp_gate, preferred_element_type=jnp.float32)
        up_part = jnp.dot(normed_two, mlp_up, preferred_element_type=jnp.float32)
        inner_act = (jax.nn.silu(gate_part) * up_part).astype(jnp.bfloat16)
        down_part = jnp.dot(inner_act, mlp_down, preferred_element_type=jnp.float32)

    return tail_exchange(down_part, mixed_rows, deal_order.reshape(1, all_rows), head_count, req_count, 3)


def solution(mesh):
    return jax.shard_map(
        functools.partial(body, mesh.shape["req"], mesh.shape["head"]),
        mesh=mesh,
        in_specs=(
            P("req", None),
            P(),
            P(),
            P(),
            P("req", None, "head", None),
            P("req", None, "head", None),
            P(),
            P(None, "head"),
            P(None, "head"),
            P(None, "head"),
            P(None, "head"),
            P("head", None),
            P(),
            P(),
            P(),
            P(None, "head"),
            P(None, "head"),
            P("head", None),
        ),
        out_specs=P("req", None),
        check_vma=False,
    )
```

```python
import functools
import math

import jax
import jax.numpy as jnp
from jax import lax
from jax.experimental import pallas as pl
from jax.experimental.pallas import tpu as pltpu
from jax.sharding import PartitionSpec as P

EPSILON = 1e-06
ROPE_BASE = 1000000.0
LOW_SCORE = -1e30
LOG_TWO = math.log(2.0)
MESH_IDS = pl.DeviceIdType.MESH


def rms_inv(values):
    return lax.rsqrt(jnp.mean(values * values, axis=-1, keepdims=True) + EPSILON)


def rotate(values, position):
    half_dim = values.shape[-1] // 2
    exponent = jnp.arange(half_dim, dtype=jnp.float32) * (2.0 / values.shape[-1])
    frequency = ROPE_BASE ** (-exponent)
    angles = position[:, None] * frequency[None, :]
    ones_tail = (1,) * (values.ndim - 2)
    angles = angles.reshape((angles.shape[0],) + ones_tail + (half_dim,))
    cosine = jnp.cos(angles)
    sine_vals = jnp.sin(angles)
    front_half = values[..., :half_dim]
    back_half = values[..., half_dim:]
    return jnp.concatenate(
        [front_half * cosine - back_half * sine_vals, back_half * cosine + front_half * sine_vals],
        axis=-1,
    )


def norm_rotate(values, gain_vec, position):
    return rotate(values * rms_inv(values) * gain_vec, position)


def exchange_kernel(axis, count, spreads, *refs):
    arrays = len(spreads)
    sources, outputs = refs[:arrays], refs[arrays : 2 * arrays]
    send_sems, recv_sems = refs[2 * arrays], refs[2 * arrays + 1]
    me = lax.axis_index(axis)
    barrier = pltpu.get_barrier_semaphore()
    for offset in range(1, count):
        peer = lax.rem(me + offset, count)
        pl.semaphore_signal(barrier, inc=1, device_id={axis: peer}, device_id_type=MESH_IDS)
    pl.semaphore_wait(barrier, count - 1)
    copies = []
    for offset in range(1, count):
        peer = lax.rem(me + offset, count)
        for which in range(arrays):
            src_ref, out_ref = sources[which], outputs[which]
            copy = pltpu.make_async_remote_copy(
                src_ref=src_ref.at[peer] if spreads[which] else src_ref,
                dst_ref=out_ref.at[me],
                send_sem=send_sems.at[which, offset],
                recv_sem=recv_sems.at[which, offset],
                device_id={axis: peer},
                device_id_type=MESH_IDS,
            )
            copy.start()
            copies.append(copy)
    for which in range(arrays):
        src_ref, out_ref = sources[which], outputs[which]
        out_ref[me] = src_ref[me] if spreads[which] else src_ref[...]
    for copy in copies:
        copy.wait()


def exchange_many(arrays, spreads, axis, count, ident):
    shapes = []
    for values, spread in zip(arrays, spreads):
        block = values.shape[1:] if spread else values.shape
        shapes.append(jax.ShapeDtypeStruct((count,) + tuple(block), values.dtype))
    return pl.pallas_call(
        functools.partial(exchange_kernel, axis, count, tuple(spreads)),
        out_shape=tuple(shapes),
        in_specs=[pl.BlockSpec(memory_space=pltpu.VMEM)] * len(arrays),
        out_specs=tuple(pl.BlockSpec(memory_space=pltpu.VMEM) for _ in arrays),
        scratch_shapes=[
            pltpu.SemaphoreType.DMA((len(arrays), count)),
            pltpu.SemaphoreType.DMA((len(arrays), count)),
        ],
        compiler_params=pltpu.CompilerParams(collective_id=ident, has_side_effects=True),
    )(*arrays)


def exchange(values, axis, count, spread, ident):
    return exchange_many((values,), (spread,), axis, count, ident)[0]


def greet(peers):
    barrier = pltpu.get_barrier_semaphore()
    for axis, peer in peers:
        pl.semaphore_signal(barrier, inc=1, device_id={axis: peer}, device_id_type=MESH_IDS)
    pl.semaphore_wait(barrier, len(peers))


def peers_of(axis, count):
    me = lax.axis_index(axis)
    return me, [(offset, lax.rem(me + offset, count)) for offset in range(1, count)]


def send_all(axis, peers, src_of, dst, send_sems, recv_sems, phase):
    copies = []
    for offset, peer in peers:
        copy = pltpu.make_async_remote_copy(
            src_ref=src_of(peer),
            dst_ref=dst,
            send_sem=send_sems.at[phase, offset],
            recv_sem=recv_sems.at[phase, offset],
            device_id={axis: peer},
            device_id_type=MESH_IDS,
        )
        copy.start()
        copies.append(copy)
    for copy in copies:
        copy.wait()


def residual_kernel(count, parts_ref, hidden_ref, out_ref, summed, send_sems, recv_sems):
    me, peers = peers_of("head", count)
    cols = out_ref.shape[1] // count
    mine = pl.ds(pl.multiple_of(me * cols, cols), cols)
    greet([("head", peer) for _, peer in peers])
    summed[me] = parts_ref[:, mine]
    send_all(
        "head", peers, lambda peer: parts_ref.at[:, pl.ds(peer * cols, cols)], summed.at[me], send_sems, recv_sems, 0
    )
    out_ref[:, mine] = (hidden_ref[:, mine].astype(jnp.float32) + jnp.sum(summed[...], axis=0)).astype(
        out_ref.dtype
    )
    send_all("head", peers, lambda peer: out_ref.at[:, mine], out_ref.at[:, mine], send_sems, recv_sems, 1)


def residual_exchange(parts, hidden, count, ident):
    rows, width = parts.shape
    return pl.pallas_call(
        functools.partial(residual_kernel, count),
        out_shape=jax.ShapeDtypeStruct((rows, width), jnp.bfloat16),
        in_specs=[pl.BlockSpec(memory_space=pltpu.VMEM)] * 2,
        out_specs=pl.BlockSpec(memory_space=pltpu.VMEM),
        scratch_shapes=[
            pltpu.VMEM((count, rows, width // count), jnp.float32),
            pltpu.SemaphoreType.DMA((2, count)),
            pltpu.SemaphoreType.DMA((2, count)),
        ],
        compiler_params=pltpu.CompilerParams(collective_id=ident, has_side_effects=True),
    )(parts, hidden)


def query_kernel(count, query_ref, normed_ref, w_gate_ref, w_value_ref, out_ref, gate_ref, value_ref, send_sems, recv_sems):
    me, peers = peers_of("req", count)
    greet([("req", peer) for _, peer in peers])
    copies = []
    for offset, peer in peers:
        copy = pltpu.make_async_remote_copy(
            src_ref=query_ref,
            dst_ref=out_ref.at[me],
            send_sem=send_sems.at[offset],
            recv_sem=recv_sems.at[offset],
            device_id={"req": peer},
            device_id_type=MESH_IDS,
        )
        copy.start()
        copies.append(copy)
    out_ref[me] = query_ref[...]
    normed = normed_ref[...]
    gate_ref[...] = jnp.dot(normed, w_gate_ref[...], preferred_element_type=jnp.float32)
    value_ref[...] = jnp.dot(normed, w_value_ref[...], preferred_element_type=jnp.float32).astype(value_ref.dtype)
    for copy in copies:
        copy.wait()


def query_exchange(queries, normed, w_gate, w_value, count, ident):
    rows = queries.shape[0]
    return pl.pallas_call(
        functools.partial(query_kernel, count),
        out_shape=(
            jax.ShapeDtypeStruct((count,) + queries.shape, queries.dtype),
            jax.ShapeDtypeStruct((rows, w_gate.shape[1]), jnp.float32),
            jax.ShapeDtypeStruct((rows, w_value.shape[1]), jnp.bfloat16),
        ),
        in_specs=[pl.BlockSpec(memory_space=pltpu.VMEM)] * 4,
        out_specs=tuple(pl.BlockSpec(memory_space=pltpu.VMEM) for _ in range(3)),
        scratch_shapes=[pltpu.SemaphoreType.DMA((count,)), pltpu.SemaphoreType.DMA((count,))],
        compiler_params=pltpu.CompilerParams(collective_id=ident, has_side_effects=True),
    )(queries, normed, w_gate, w_value)


def attend_kernel(
    req_count, head_count, group_size, scale_factor, num_ref, stats_ref, query_ref, key_ref, value_ref, gate_ref,
    w_out_ref, hidden_ref, out_ref, got_num, got_stats, projected, summed, send_sems, recv_sems,
):
    req_me, req_peers = peers_of("req", req_count)
    head_me, head_peers = peers_of("head", head_count)
    rows, width = out_ref.shape
    cols = width // head_count
    pairs = stats_ref.shape[1] // 2
    head_width = query_ref.shape[1] // pairs
    mine = pl.ds(pl.multiple_of(head_me * cols, cols), cols)
    greet([("req", peer) for _, peer in req_peers] + [("head", peer) for _, peer in head_peers])
    got_num[req_me] = num_ref[req_me]
    got_stats[req_me] = stats_ref[req_me]
    copies = []
    for offset, peer in req_peers:
        for which, (src_ref, dst_ref) in enumerate(((num_ref, got_num), (stats_ref, got_stats))):
            copy = pltpu.make_async_remote_copy(
                src_ref=src_ref.at[peer],
                dst_ref=dst_ref.at[req_me],
                send_sem=send_sems.at[which, offset],
                recv_sem=recv_sems.at[which, offset],
                device_id={"req": peer},
                device_id_type=MESH_IDS,
            )
            copy.start()
            copies.append(copy)
    for copy in copies:
        copy.wait()
    eye = (
        lax.broadcasted_iota(jnp.int32, (rows, rows), 0) == lax.broadcasted_iota(jnp.int32, (rows, rows), 1)
    ).astype(jnp.float32)
    flip = (((1,), (1,)), ((), ()))
    heads = []
    for pair in range(pairs):
        kv = pair // group_size
        lanes = slice(pair * head_width, (pair + 1) * head_width)
        kv_lanes = slice(kv * head_width, (kv + 1) * head_width)
        shifts = lax.dot_general(
            eye, got_stats[:, pair, :], flip, precision=lax.Precision.HIGHEST, preferred_element_type=jnp.float32
        )
        totals = lax.dot_general(
            eye,
            got_stats[:, pairs + pair, :],
            flip,
            precision=lax.Precision.HIGHEST,
            preferred_element_type=jnp.float32,
        )
        query = query_ref[:, lanes].astype(jnp.float32)
        self_score = jnp.sum(query * key_ref[:, kv_lanes].astype(jnp.float32), axis=1, keepdims=True) * scale_factor
        self_shift = LOG_TWO * jnp.ceil(self_score / LOG_TWO)
        shift = jnp.maximum(jnp.max(shifts, axis=1, keepdims=True), self_shift)
        factor = jnp.exp(shifts - shift)
        self_weight = jnp.exp(self_score - shift)
        total = jnp.sum(totals * factor, axis=1, keepdims=True) + self_weight
        acc = self_weight.astype(jnp.bfloat16).astype(jnp.float32) * value_ref[:, kv_lanes].astype(jnp.float32)
        for source in range(req_count):
            acc = acc + factor[:, source : source + 1] * got_num[source, :, lanes].astype(jnp.float32)
        heads.append(acc / total)
    heads_out = jnp.concatenate(heads, axis=1)
    gate = gate_ref[...]
    attended = (heads_out * (1.0 / (1.0 + jnp.exp(-gate)))).astype(jnp.bfloat16)
    projected[...] = jnp.dot(attended, w_out_ref[...], preferred_element_type=jnp.float32)
    summed[head_me] = projected[:, mine]
    send_all(
        "head", head_peers, lambda peer: projected.at[:, pl.ds(peer * cols, cols)], summed.at[head_me],
        send_sems, recv_sems, 2,
    )
    out_ref[:, mine] = (hidden_ref[:, mine].astype(jnp.float32) + jnp.sum(summed[...], axis=0)).astype(
        out_ref.dtype
    )
    send_all("head", head_peers, lambda peer: out_ref.at[:, mine], out_ref.at[:, mine], send_sems, recv_sems, 3)


def attend_exchange(
    num, stats, queries, keys, values, gate, w_out, hidden, head_count, group_size, scale_factor, ident
):
    req_count = num.shape[0]
    rows, width = hidden.shape
    most = max(head_count, req_count)
    return pl.pallas_call(
        functools.partial(attend_kernel, req_count, head_count, group_size, scale_factor),
        out_shape=jax.ShapeDtypeStruct((rows, width), jnp.bfloat16),
        in_specs=[pl.BlockSpec(memory_space=pltpu.VMEM)] * 8,
        out_specs=pl.BlockSpec(memory_space=pltpu.VMEM),
        scratch_shapes=[
            pltpu.VMEM(num.shape, num.dtype),
            pltpu.VMEM(stats.shape, stats.dtype),
            pltpu.VMEM((rows, width), jnp.float32),
            pltpu.VMEM((head_count, rows, width // head_count), jnp.float32),
            pltpu.SemaphoreType.DMA((4, most)),
            pltpu.SemaphoreType.DMA((4, most)),
        ],
        compiler_params=pltpu.CompilerParams(collective_id=ident, has_side_effects=True),
    )(num, stats, queries, keys, values, gate, w_out, hidden)


def tail_kernel(
    head_count, req_count, mixed_ref, gain_ref, w_gate_ref, w_up_ref, w_down_ref, order_ref, out_ref, parts_ref,
    summed, results, send_sems, recv_sems,
):
    head_me, head_peers = peers_of("head", head_count)
    req_me, req_peers = peers_of("req", req_count)
    rows, width = out_ref.shape
    cols = width // head_count
    mine = pl.ds(pl.multiple_of(head_me * cols, cols), cols)
    barrier = pltpu.get_barrier_semaphore()
    everyone = [("head", peer) for _, peer in head_peers] + [("req", peer) for _, peer in req_peers]
    for axis, peer in everyone:
        pl.semaphore_signal(barrier, inc=1, device_id={axis: peer}, device_id_type=MESH_IDS)
    mixed = mixed_ref[...].astype(jnp.float32)
    normed = (mixed * rms_inv(mixed) * gain_ref[...]).astype(jnp.bfloat16)
    gate_part = jnp.dot(normed, w_gate_ref[...], preferred_element_type=jnp.float32)
    up_part = jnp.dot(normed, w_up_ref[...], preferred_element_type=jnp.float32)
    inner_act = (gate_part / (1.0 + jnp.exp(-gate_part)) * up_part).astype(jnp.bfloat16)
    parts_ref[...] = jnp.dot(inner_act, w_down_ref[...], preferred_element_type=jnp.float32)
    pl.semaphore_wait(barrier, len(everyone))
    summed[head_me] = parts_ref[:, mine]
    send_all(
        "head",
        head_peers,
        lambda peer: parts_ref.at[:, pl.ds(peer * cols, cols)],
        summed.at[head_me],
        send_sems,
        recv_sems,
        0,
    )
    results[req_me] = (mixed_ref[:, mine].astype(jnp.float32) + jnp.sum(summed[...], axis=0)).astype(
        results.dtype
    )
    send_all("req", req_peers, lambda peer: results.at[req_me], results.at[req_me], send_sems, recv_sems, 1)
    wanted = req_me * rows + lax.broadcasted_iota(jnp.int32, (rows, req_count * rows), 0)
    picker = (order_ref[...] == wanted).astype(jnp.bfloat16)
    out_ref[:, mine] = jnp.dot(
        picker, results[...].reshape(req_count * rows, cols), preferred_element_type=jnp.float32
    ).astype(out_ref.dtype)
    send_all("head", head_peers, lambda peer: out_ref.at[:, mine], out_ref.at[:, mine], send_sems, recv_sems, 2)


def tail_exchange(mixed, gain, w_gate, w_up, w_down, order, head_count, req_count, ident):
    rows, width = mixed.shape
    most = max(head_count, req_count)
    return pl.pallas_call(
        functools.partial(tail_kernel, head_count, req_count),
        out_shape=jax.ShapeDtypeStruct((rows, width), jnp.bfloat16),
        in_specs=[pl.BlockSpec(memory_space=pltpu.VMEM)] * 6,
        out_specs=pl.BlockSpec(memory_space=pltpu.VMEM),
        scratch_shapes=[
            pltpu.VMEM((rows, width), jnp.float32),
            pltpu.VMEM((head_count, rows, width // head_count), jnp.float32),
            pltpu.VMEM((req_count, rows, width // head_count), jnp.bfloat16),
            pltpu.SemaphoreType.DMA((3, most)),
            pltpu.SemaphoreType.DMA((3, most)),
        ],
        compiler_params=pltpu.CompilerParams(collective_id=ident, has_side_effects=True),
    )(mixed, gain, w_gate, w_up, w_down, order)


def body(
    req_count,
    head_count,
    hidden,
    deal_order,
    lengths,
    page_table,
    key_cache,
    value_cache,
    attn_gain,
    w_query,
    w_key,
    w_value,
    w_gate,
    w_out,
    query_gain,
    key_gain,
    mlp_gain,
    mlp_gate,
    mlp_up,
    mlp_down,
):
    local_rows, model_width = hidden.shape
    req_index = lax.axis_index("req")
    head_index = lax.axis_index("head")
    all_rows = local_rows * req_count
    head_width = query_gain.shape[0]
    pool_pages, page_size, local_kv = key_cache.shape[:3]
    group_size = w_query.shape[1] // (local_kv * head_width)
    head_cols = local_kv * group_size * head_width
    pairs = local_kv * group_size
    chunk = model_width // head_count
    scale_factor = 1.0 / math.sqrt(head_width)
    first_own = req_index * local_rows

    with jax.named_scope("projections"):
        hidden_f = hidden.astype(jnp.float32)
        normed = (hidden_f * rms_inv(hidden_f) * attn_gain).astype(jnp.bfloat16)
        own_requests = lax.dynamic_slice_in_dim(deal_order, first_own, local_rows)
        request_ids = jnp.arange(all_rows, dtype=jnp.int32)
        own_pick = own_requests[:, None] == request_ids[None, :]
        position = jnp.sum(jnp.where(own_pick, lengths[None, :], 0), axis=1).astype(jnp.float32)
        queries = jnp.dot(normed, w_query, preferred_element_type=jnp.float32).reshape(
            local_rows, local_kv, group_size, head_width
        )
        queries = norm_rotate(queries, query_gain, position).astype(jnp.bfloat16)
        new_keys = jnp.dot(normed, w_key, preferred_element_type=jnp.float32).reshape(
            local_rows, local_kv, head_width
        )
        new_keys = norm_rotate(new_keys, key_gain, position).astype(jnp.bfloat16)

    all_queries, gate_logits, new_values = query_exchange(
        queries.reshape(local_rows, head_cols), normed, w_gate, w_value, req_count, 0
    )
    all_queries = all_queries.reshape(all_rows, head_cols)
    new_values = new_values.reshape(local_rows, local_kv, head_width)

    with jax.named_scope("page_owners"):
        page_counts = (lengths + page_size - 1) // page_size
        slot_ids = jnp.arange(page_table.shape[1], dtype=jnp.int32)
        local_ids = page_table - req_index * pool_pages
        usable = (
            (slot_ids[None, :] < page_counts[:, None]) & (local_ids >= 0) & (local_ids < pool_pages)
        )
        keyed = jnp.where(usable, local_ids, pool_pages)
        page_ids = jnp.arange(pool_pages, dtype=jnp.int32)
        match = keyed[None, :, :] == page_ids[:, None, None]
        owned_requests = jnp.any(match, axis=2)
        owner_slot = jnp.sum(jnp.where(match, slot_ids[None, None, :], 0), axis=(1, 2))
        owner_length = jnp.sum(jnp.where(owned_requests, lengths[None, :], 0), axis=1)
        filled = jnp.clip(owner_length - owner_slot * page_size, 0, page_size)
        filled = jnp.where(jnp.any(owned_requests, axis=1), filled, 0)
        dealing = (request_ids[:, None] == deal_order[None, :]).astype(jnp.bfloat16)
        owned = (
            jnp.dot(owned_requests.astype(jnp.bfloat16), dealing, preferred_element_type=jnp.float32)
            > 0.5
        )
        page_queries = (
            jnp.dot(owned.astype(jnp.bfloat16), all_queries, preferred_element_type=jnp.float32)
            .astype(jnp.bfloat16)
            .reshape(pool_pages, local_kv, group_size, head_width)
        )

    with jax.named_scope("page_attention"):
        scores = (
            jnp.einsum("pkgd,ptkd->pkgt", page_queries, key_cache, preferred_element_type=jnp.float32)
            * scale_factor
        )
        live_mask = (
            jnp.arange(page_size, dtype=jnp.int32)[None, None, None, :] < filled[:, None, None, None]
        )
        scores = jnp.where(live_mask, scores, LOW_SCORE)
        page_peaks = jnp.max(scores, axis=-1)
        owned_b = owned[:, :, None, None]
        row_peaks = jnp.max(jnp.where(owned_b, page_peaks[:, None], LOW_SCORE), axis=0)
        row_shift = LOG_TWO * jnp.ceil(row_peaks / LOG_TWO)
        page_shift = jnp.max(jnp.where(owned_b, row_shift[None], LOW_SCORE), axis=1)
        weights = jnp.where(live_mask, jnp.exp(scores - page_shift[..., None]), 0.0)
        page_totals = jnp.sum(weights, axis=-1)
        page_numerators = jnp.einsum(
            "pkgt,ptkd->pkgd",
            weights.astype(jnp.bfloat16),
            value_cache,
            preferred_element_type=jnp.float32,
        )
        owned_f = owned.astype(jnp.float32)
        row_totals = jnp.dot(
            owned_f.T, page_totals.reshape(pool_pages, pairs), precision=lax.Precision.HIGHEST
        )
        row_numerators = jnp.dot(
            owned_f.T,
            page_numerators.reshape(pool_pages, head_cols),
            precision=lax.Precision.HIGHEST,
        )
        numerator_message = row_numerators.astype(jnp.bfloat16).reshape(req_count, local_rows, head_cols)
        stats_message = jnp.concatenate(
            [row_shift.reshape(req_count, local_rows, pairs), row_totals.reshape(req_count, local_rows, pairs)],
            axis=2,
        ).transpose(0, 2, 1)

    mixed_rows = attend_exchange(
        numerator_message,
        stats_message,
        queries.reshape(local_rows, head_cols),
        new_keys.reshape(local_rows, local_kv * head_width),
        new_values.reshape(local_rows, local_kv * head_width),
        gate_logits,
        w_out,
        hidden,
        head_count,
        group_size,
        scale_factor,
        1,
    )

    return tail_exchange(
        mixed_rows,
        mlp_gain.reshape(1, model_width),
        mlp_gate,
        mlp_up,
        mlp_down,
        deal_order.reshape(1, all_rows),
        head_count,
        req_count,
        3,
    )


def solution(mesh):
    return jax.shard_map(
        functools.partial(body, mesh.shape["req"], mesh.shape["head"]),
        mesh=mesh,
        in_specs=(
            P("req", None),
            P(),
            P(),
            P(),
            P("req", None, "head", None),
            P("req", None, "head", None),
            P(),
            P(None, "head"),
            P(None, "head"),
            P(None, "head"),
            P(None, "head"),
            P("head", None),
            P(),
            P(),
            P(),
            P(None, "head"),
            P(None, "head"),
            P("head", None),
        ),
        out_specs=P("req", None),
        check_vma=False,
    )
```

```python
import functools
import math

import jax
import jax.numpy as jnp
from jax import lax
from jax.experimental import pallas as pl
from jax.experimental.pallas import tpu as pltpu
from jax.sharding import PartitionSpec as P

EPSILON = 1e-06
ROPE_BASE = 1000000.0
LOW_SCORE = -1e30
LOG_TWO = math.log(2.0)
MESH_IDS = pl.DeviceIdType.MESH


def rms_inv(values):
    return lax.rsqrt(jnp.mean(values * values, axis=-1, keepdims=True) + EPSILON)


def rotate(values, position):
    half_dim = values.shape[-1] // 2
    exponent = jnp.arange(half_dim, dtype=jnp.float32) * (2.0 / values.shape[-1])
    frequency = ROPE_BASE ** (-exponent)
    angles = position[:, None] * frequency[None, :]
    ones_tail = (1,) * (values.ndim - 2)
    angles = angles.reshape((angles.shape[0],) + ones_tail + (half_dim,))
    cosine = jnp.cos(angles)
    sine_vals = jnp.sin(angles)
    front_half = values[..., :half_dim]
    back_half = values[..., half_dim:]
    return jnp.concatenate(
        [front_half * cosine - back_half * sine_vals, back_half * cosine + front_half * sine_vals],
        axis=-1,
    )


def norm_rotate(values, gain_vec, position):
    return rotate(values * rms_inv(values) * gain_vec, position)


def exchange_kernel(axis, count, spreads, *refs):
    arrays = len(spreads)
    sources, outputs = refs[:arrays], refs[arrays : 2 * arrays]
    send_sems, recv_sems = refs[2 * arrays], refs[2 * arrays + 1]
    me = lax.axis_index(axis)
    barrier = pltpu.get_barrier_semaphore()
    for offset in range(1, count):
        peer = lax.rem(me + offset, count)
        pl.semaphore_signal(barrier, inc=1, device_id={axis: peer}, device_id_type=MESH_IDS)
    pl.semaphore_wait(barrier, count - 1)
    copies = []
    for offset in range(1, count):
        peer = lax.rem(me + offset, count)
        for which in range(arrays):
            src_ref, out_ref = sources[which], outputs[which]
            copy = pltpu.make_async_remote_copy(
                src_ref=src_ref.at[peer] if spreads[which] else src_ref,
                dst_ref=out_ref.at[me],
                send_sem=send_sems.at[which, offset],
                recv_sem=recv_sems.at[which, offset],
                device_id={axis: peer},
                device_id_type=MESH_IDS,
            )
            copy.start()
            copies.append(copy)
    for which in range(arrays):
        src_ref, out_ref = sources[which], outputs[which]
        out_ref[me] = src_ref[me] if spreads[which] else src_ref[...]
    for copy in copies:
        copy.wait()


def exchange_many(arrays, spreads, axis, count, ident):
    shapes = []
    for values, spread in zip(arrays, spreads):
        block = values.shape[1:] if spread else values.shape
        shapes.append(jax.ShapeDtypeStruct((count,) + tuple(block), values.dtype))
    return pl.pallas_call(
        functools.partial(exchange_kernel, axis, count, tuple(spreads)),
        out_shape=tuple(shapes),
        in_specs=[pl.BlockSpec(memory_space=pltpu.VMEM)] * len(arrays),
        out_specs=tuple(pl.BlockSpec(memory_space=pltpu.VMEM) for _ in arrays),
        scratch_shapes=[
            pltpu.SemaphoreType.DMA((len(arrays), count)),
            pltpu.SemaphoreType.DMA((len(arrays), count)),
        ],
        compiler_params=pltpu.CompilerParams(collective_id=ident, has_side_effects=True),
    )(*arrays)


def exchange(values, axis, count, spread, ident):
    return exchange_many((values,), (spread,), axis, count, ident)[0]


def greet(peers):
    barrier = pltpu.get_barrier_semaphore()
    for axis, peer in peers:
        pl.semaphore_signal(barrier, inc=1, device_id={axis: peer}, device_id_type=MESH_IDS)
    pl.semaphore_wait(barrier, len(peers))


def peers_of(axis, count):
    me = lax.axis_index(axis)
    return me, [(offset, lax.rem(me + offset, count)) for offset in range(1, count)]


def send_all(axis, peers, src_of, dst, send_sems, recv_sems, phase):
    copies = []
    for offset, peer in peers:
        copy = pltpu.make_async_remote_copy(
            src_ref=src_of(peer),
            dst_ref=dst,
            send_sem=send_sems.at[phase, offset],
            recv_sem=recv_sems.at[phase, offset],
            device_id={axis: peer},
            device_id_type=MESH_IDS,
        )
        copy.start()
        copies.append(copy)
    for copy in copies:
        copy.wait()


def residual_kernel(count, parts_ref, hidden_ref, out_ref, summed, send_sems, recv_sems):
    me, peers = peers_of("head", count)
    cols = out_ref.shape[1] // count
    mine = pl.ds(pl.multiple_of(me * cols, cols), cols)
    greet([("head", peer) for _, peer in peers])
    summed[me] = parts_ref[:, mine]
    send_all(
        "head", peers, lambda peer: parts_ref.at[:, pl.ds(peer * cols, cols)], summed.at[me], send_sems, recv_sems, 0
    )
    out_ref[:, mine] = (hidden_ref[:, mine].astype(jnp.float32) + jnp.sum(summed[...], axis=0)).astype(
        out_ref.dtype
    )
    send_all("head", peers, lambda peer: out_ref.at[:, mine], out_ref.at[:, mine], send_sems, recv_sems, 1)


def residual_exchange(parts, hidden, count, ident):
    rows, width = parts.shape
    return pl.pallas_call(
        functools.partial(residual_kernel, count),
        out_shape=jax.ShapeDtypeStruct((rows, width), jnp.bfloat16),
        in_specs=[pl.BlockSpec(memory_space=pltpu.VMEM)] * 2,
        out_specs=pl.BlockSpec(memory_space=pltpu.VMEM),
        scratch_shapes=[
            pltpu.VMEM((count, rows, width // count), jnp.float32),
            pltpu.SemaphoreType.DMA((2, count)),
            pltpu.SemaphoreType.DMA((2, count)),
        ],
        compiler_params=pltpu.CompilerParams(collective_id=ident, has_side_effects=True),
    )(parts, hidden)


def query_kernel(
    count, query_ref, normed_ref, w_gate_ref, w_value_ref, w_key_ref, key_gain_ref, cos_ref, sin_ref, swap_ref,
    out_ref, gate_ref, value_ref, key_ref, send_sems, recv_sems,
):
    me, peers = peers_of("req", count)
    greet([("req", peer) for _, peer in peers])
    copies = []
    for offset, peer in peers:
        copy = pltpu.make_async_remote_copy(
            src_ref=query_ref,
            dst_ref=out_ref.at[me],
            send_sem=send_sems.at[offset],
            recv_sem=recv_sems.at[offset],
            device_id={"req": peer},
            device_id_type=MESH_IDS,
        )
        copy.start()
        copies.append(copy)
    out_ref[me] = query_ref[...]
    normed = normed_ref[...]
    gate_ref[...] = jnp.dot(normed, w_gate_ref[...], preferred_element_type=jnp.float32)
    value_ref[...] = jnp.dot(normed, w_value_ref[...], preferred_element_type=jnp.float32).astype(value_ref.dtype)
    head_width = swap_ref.shape[0]
    keys = jnp.dot(normed, w_key_ref[...], preferred_element_type=jnp.float32)
    for kv in range(keys.shape[1] // head_width):
        key = keys[:, kv * head_width : (kv + 1) * head_width]
        key = key * rms_inv(key) * key_gain_ref[...]
        swapped = jnp.dot(key, swap_ref[...], precision=lax.Precision.HIGHEST, preferred_element_type=jnp.float32)
        key_ref[:, kv * head_width : (kv + 1) * head_width] = (key * cos_ref[...] + swapped * sin_ref[...]).astype(
            key_ref.dtype
        )
    for copy in copies:
        copy.wait()


def query_exchange(queries, normed, w_gate, w_value, w_key, key_gain, cosine, sine, swap, count, ident):
    rows = queries.shape[0]
    return pl.pallas_call(
        functools.partial(query_kernel, count),
        out_shape=(
            jax.ShapeDtypeStruct((count,) + queries.shape, queries.dtype),
            jax.ShapeDtypeStruct((rows, w_gate.shape[1]), jnp.float32),
            jax.ShapeDtypeStruct((rows, w_value.shape[1]), jnp.bfloat16),
            jax.ShapeDtypeStruct((rows, w_key.shape[1]), jnp.bfloat16),
        ),
        in_specs=[pl.BlockSpec(memory_space=pltpu.VMEM)] * 9,
        out_specs=tuple(pl.BlockSpec(memory_space=pltpu.VMEM) for _ in range(4)),
        scratch_shapes=[pltpu.SemaphoreType.DMA((count,)), pltpu.SemaphoreType.DMA((count,))],
        compiler_params=pltpu.CompilerParams(collective_id=ident, has_side_effects=True),
    )(queries, normed, w_gate, w_value, w_key, key_gain, cosine, sine, swap)


def attend_kernel(
    req_count, head_count, group_size, scale_factor, num_ref, stats_ref, query_ref, key_ref, value_ref, gate_ref,
    w_out_ref, hidden_ref, out_ref, got_num, got_stats, projected, summed, send_sems, recv_sems,
):
    req_me, req_peers = peers_of("req", req_count)
    head_me, head_peers = peers_of("head", head_count)
    rows, width = out_ref.shape
    cols = width // head_count
    pairs = stats_ref.shape[1] // 2
    head_width = query_ref.shape[1] // pairs
    mine = pl.ds(pl.multiple_of(head_me * cols, cols), cols)
    greet([("req", peer) for _, peer in req_peers] + [("head", peer) for _, peer in head_peers])
    got_num[req_me] = num_ref[req_me]
    got_stats[req_me] = stats_ref[req_me]
    copies = []
    for offset, peer in req_peers:
        for which, (src_ref, dst_ref) in enumerate(((num_ref, got_num), (stats_ref, got_stats))):
            copy = pltpu.make_async_remote_copy(
                src_ref=src_ref.at[peer],
                dst_ref=dst_ref.at[req_me],
                send_sem=send_sems.at[which, offset],
                recv_sem=recv_sems.at[which, offset],
                device_id={"req": peer},
                device_id_type=MESH_IDS,
            )
            copy.start()
            copies.append(copy)
    for copy in copies:
        copy.wait()
    eye = (
        lax.broadcasted_iota(jnp.int32, (rows, rows), 0) == lax.broadcasted_iota(jnp.int32, (rows, rows), 1)
    ).astype(jnp.float32)
    flip = (((1,), (1,)), ((), ()))
    heads = []
    for pair in range(pairs):
        kv = pair // group_size
        lanes = slice(pair * head_width, (pair + 1) * head_width)
        kv_lanes = slice(kv * head_width, (kv + 1) * head_width)
        shifts = lax.dot_general(
            eye, got_stats[:, pair, :], flip, precision=lax.Precision.HIGHEST, preferred_element_type=jnp.float32
        )
        totals = lax.dot_general(
            eye,
            got_stats[:, pairs + pair, :],
            flip,
            precision=lax.Precision.HIGHEST,
            preferred_element_type=jnp.float32,
        )
        query = query_ref[:, lanes].astype(jnp.float32)
        self_score = jnp.sum(query * key_ref[:, kv_lanes].astype(jnp.float32), axis=1, keepdims=True) * scale_factor
        self_shift = LOG_TWO * jnp.ceil(self_score / LOG_TWO)
        shift = jnp.maximum(jnp.max(shifts, axis=1, keepdims=True), self_shift)
        factor = jnp.exp(shifts - shift)
        self_weight = jnp.exp(self_score - shift)
        total = jnp.sum(totals * factor, axis=1, keepdims=True) + self_weight
        acc = self_weight.astype(jnp.bfloat16).astype(jnp.float32) * value_ref[:, kv_lanes].astype(jnp.float32)
        for source in range(req_count):
            acc = acc + factor[:, source : source + 1] * got_num[source, :, lanes].astype(jnp.float32)
        heads.append(acc / total)
    heads_out = jnp.concatenate(heads, axis=1)
    gate = gate_ref[...]
    attended = (heads_out * (1.0 / (1.0 + jnp.exp(-gate)))).astype(jnp.bfloat16)
    projected[...] = jnp.dot(attended, w_out_ref[...], preferred_element_type=jnp.float32)
    summed[head_me] = projected[:, mine]
    send_all(
        "head", head_peers, lambda peer: projected.at[:, pl.ds(peer * cols, cols)], summed.at[head_me],
        send_sems, recv_sems, 2,
    )
    out_ref[:, mine] = (hidden_ref[:, mine].astype(jnp.float32) + jnp.sum(summed[...], axis=0)).astype(
        out_ref.dtype
    )
    send_all("head", head_peers, lambda peer: out_ref.at[:, mine], out_ref.at[:, mine], send_sems, recv_sems, 3)


def attend_exchange(
    num, stats, queries, keys, values, gate, w_out, hidden, head_count, group_size, scale_factor, ident
):
    req_count = num.shape[0]
    rows, width = hidden.shape
    most = max(head_count, req_count)
    return pl.pallas_call(
        functools.partial(attend_kernel, req_count, head_count, group_size, scale_factor),
        out_shape=jax.ShapeDtypeStruct((rows, width), jnp.bfloat16),
        in_specs=[pl.BlockSpec(memory_space=pltpu.VMEM)] * 8,
        out_specs=pl.BlockSpec(memory_space=pltpu.VMEM),
        scratch_shapes=[
            pltpu.VMEM(num.shape, num.dtype),
            pltpu.VMEM(stats.shape, stats.dtype),
            pltpu.VMEM((rows, width), jnp.float32),
            pltpu.VMEM((head_count, rows, width // head_count), jnp.float32),
            pltpu.SemaphoreType.DMA((4, most)),
            pltpu.SemaphoreType.DMA((4, most)),
        ],
        compiler_params=pltpu.CompilerParams(collective_id=ident, has_side_effects=True),
    )(num, stats, queries, keys, values, gate, w_out, hidden)


def tail_kernel(
    head_count, req_count, mixed_ref, gain_ref, w_gate_ref, w_up_ref, w_down_ref, order_ref, out_ref, parts_ref,
    summed, results, send_sems, recv_sems,
):
    head_me, head_peers = peers_of("head", head_count)
    req_me, req_peers = peers_of("req", req_count)
    rows, width = out_ref.shape
    cols = width // head_count
    mine = pl.ds(pl.multiple_of(head_me * cols, cols), cols)
    barrier = pltpu.get_barrier_semaphore()
    everyone = [("head", peer) for _, peer in head_peers] + [("req", peer) for _, peer in req_peers]
    for axis, peer in everyone:
        pl.semaphore_signal(barrier, inc=1, device_id={axis: peer}, device_id_type=MESH_IDS)
    mixed = mixed_ref[...].astype(jnp.float32)
    normed = (mixed * rms_inv(mixed) * gain_ref[...]).astype(jnp.bfloat16)
    gate_part = jnp.dot(normed, w_gate_ref[...], preferred_element_type=jnp.float32)
    up_part = jnp.dot(normed, w_up_ref[...], preferred_element_type=jnp.float32)
    inner_act = (gate_part / (1.0 + jnp.exp(-gate_part)) * up_part).astype(jnp.bfloat16)
    parts_ref[...] = jnp.dot(inner_act, w_down_ref[...], preferred_element_type=jnp.float32)
    pl.semaphore_wait(barrier, len(everyone))
    summed[head_me] = parts_ref[:, mine]
    send_all(
        "head",
        head_peers,
        lambda peer: parts_ref.at[:, pl.ds(peer * cols, cols)],
        summed.at[head_me],
        send_sems,
        recv_sems,
        0,
    )
    results[req_me] = (mixed_ref[:, mine].astype(jnp.float32) + jnp.sum(summed[...], axis=0)).astype(
        results.dtype
    )
    send_all("req", req_peers, lambda peer: results.at[req_me], results.at[req_me], send_sems, recv_sems, 1)
    wanted = req_me * rows + lax.broadcasted_iota(jnp.int32, (rows, req_count * rows), 0)
    picker = (order_ref[...] == wanted).astype(jnp.bfloat16)
    out_ref[:, mine] = jnp.dot(
        picker, results[...].reshape(req_count * rows, cols), preferred_element_type=jnp.float32
    ).astype(out_ref.dtype)
    send_all("head", head_peers, lambda peer: out_ref.at[:, mine], out_ref.at[:, mine], send_sems, recv_sems, 2)


def tail_exchange(mixed, gain, w_gate, w_up, w_down, order, head_count, req_count, ident):
    rows, width = mixed.shape
    most = max(head_count, req_count)
    return pl.pallas_call(
        functools.partial(tail_kernel, head_count, req_count),
        out_shape=jax.ShapeDtypeStruct((rows, width), jnp.bfloat16),
        in_specs=[pl.BlockSpec(memory_space=pltpu.VMEM)] * 6,
        out_specs=pl.BlockSpec(memory_space=pltpu.VMEM),
        scratch_shapes=[
            pltpu.VMEM((rows, width), jnp.float32),
            pltpu.VMEM((head_count, rows, width // head_count), jnp.float32),
            pltpu.VMEM((req_count, rows, width // head_count), jnp.bfloat16),
            pltpu.SemaphoreType.DMA((3, most)),
            pltpu.SemaphoreType.DMA((3, most)),
        ],
        compiler_params=pltpu.CompilerParams(collective_id=ident, has_side_effects=True),
    )(mixed, gain, w_gate, w_up, w_down, order)


def body(
    req_count,
    head_count,
    hidden,
    deal_order,
    lengths,
    page_table,
    key_cache,
    value_cache,
    attn_gain,
    w_query,
    w_key,
    w_value,
    w_gate,
    w_out,
    query_gain,
    key_gain,
    mlp_gain,
    mlp_gate,
    mlp_up,
    mlp_down,
):
    local_rows, model_width = hidden.shape
    req_index = lax.axis_index("req")
    head_index = lax.axis_index("head")
    all_rows = local_rows * req_count
    head_width = query_gain.shape[0]
    pool_pages, page_size, local_kv = key_cache.shape[:3]
    group_size = w_query.shape[1] // (local_kv * head_width)
    head_cols = local_kv * group_size * head_width
    pairs = local_kv * group_size
    chunk = model_width // head_count
    scale_factor = 1.0 / math.sqrt(head_width)
    first_own = req_index * local_rows

    with jax.named_scope("projections"):
        hidden_f = hidden.astype(jnp.float32)
        normed = (hidden_f * rms_inv(hidden_f) * attn_gain).astype(jnp.bfloat16)
        own_requests = lax.dynamic_slice_in_dim(deal_order, first_own, local_rows)
        request_ids = jnp.arange(all_rows, dtype=jnp.int32)
        own_pick = own_requests[:, None] == request_ids[None, :]
        position = jnp.sum(jnp.where(own_pick, lengths[None, :], 0), axis=1).astype(jnp.float32)
        queries = jnp.dot(normed, w_query, preferred_element_type=jnp.float32).reshape(
            local_rows, local_kv, group_size, head_width
        )
        queries = norm_rotate(queries, query_gain, position).astype(jnp.bfloat16)
        half = head_width // 2
        frequency = ROPE_BASE ** (-(jnp.arange(half, dtype=jnp.float32) * (2.0 / head_width)))
        angles = position[:, None] * frequency[None, :]
        cosine = jnp.concatenate([jnp.cos(angles)] * 2, axis=1)
        sine = jnp.concatenate([jnp.sin(angles)] * 2, axis=1)
        lanes = jnp.arange(head_width, dtype=jnp.int32)
        swap = jnp.where(
            lanes[:, None] == (lanes[None, :] + half) % head_width,
            jnp.where(lanes[None, :] < half, -1.0, 1.0),
            0.0,
        ).astype(jnp.float32)

    all_queries, gate_logits, new_values, new_keys = query_exchange(
        queries.reshape(local_rows, head_cols),
        normed,
        w_gate,
        w_value,
        w_key,
        key_gain.reshape(1, head_width),
        cosine,
        sine,
        swap,
        req_count,
        0,
    )
    all_queries = all_queries.reshape(all_rows, head_cols)
    new_values = new_values.reshape(local_rows, local_kv, head_width)
    new_keys = new_keys.reshape(local_rows, local_kv, head_width)

    with jax.named_scope("page_owners"):
        page_counts = (lengths + page_size - 1) // page_size
        slot_ids = jnp.arange(page_table.shape[1], dtype=jnp.int32)
        local_ids = page_table - req_index * pool_pages
        usable = (
            (slot_ids[None, :] < page_counts[:, None]) & (local_ids >= 0) & (local_ids < pool_pages)
        )
        keyed = jnp.where(usable, local_ids, pool_pages)
        page_ids = jnp.arange(pool_pages, dtype=jnp.int32)
        match = keyed[None, :, :] == page_ids[:, None, None]
        owned_requests = jnp.any(match, axis=2)
        owner_slot = jnp.sum(jnp.where(match, slot_ids[None, None, :], 0), axis=(1, 2))
        owner_length = jnp.sum(jnp.where(owned_requests, lengths[None, :], 0), axis=1)
        filled = jnp.clip(owner_length - owner_slot * page_size, 0, page_size)
        filled = jnp.where(jnp.any(owned_requests, axis=1), filled, 0)
        dealing = (request_ids[:, None] == deal_order[None, :]).astype(jnp.bfloat16)
        owned = (
            jnp.dot(owned_requests.astype(jnp.bfloat16), dealing, preferred_element_type=jnp.float32)
            > 0.5
        )
        page_queries = (
            jnp.dot(owned.astype(jnp.bfloat16), all_queries, preferred_element_type=jnp.float32)
            .astype(jnp.bfloat16)
            .reshape(pool_pages, local_kv, group_size, head_width)
        )

    with jax.named_scope("page_attention"):
        scores = (
            jnp.einsum("pkgd,ptkd->pkgt", page_queries, key_cache, preferred_element_type=jnp.float32)
            * scale_factor
        )
        live_mask = (
            jnp.arange(page_size, dtype=jnp.int32)[None, None, None, :] < filled[:, None, None, None]
        )
        scores = jnp.where(live_mask, scores, LOW_SCORE)
        page_peaks = jnp.max(scores, axis=-1)
        owned_b = owned[:, :, None, None]
        row_peaks = jnp.max(jnp.where(owned_b, page_peaks[:, None], LOW_SCORE), axis=0)
        row_shift = LOG_TWO * jnp.ceil(row_peaks / LOG_TWO)
        page_shift = jnp.max(jnp.where(owned_b, row_shift[None], LOW_SCORE), axis=1)
        weights = jnp.where(live_mask, jnp.exp(scores - page_shift[..., None]), 0.0)
        page_totals = jnp.sum(weights, axis=-1)
        page_numerators = jnp.einsum(
            "pkgt,ptkd->pkgd",
            weights.astype(jnp.bfloat16),
            value_cache,
            preferred_element_type=jnp.float32,
        )
        owned_f = owned.astype(jnp.float32)
        row_totals = jnp.dot(
            owned_f.T, page_totals.reshape(pool_pages, pairs), precision=lax.Precision.HIGHEST
        )
        row_numerators = jnp.dot(
            owned_f.T,
            page_numerators.reshape(pool_pages, head_cols),
            precision=lax.Precision.HIGHEST,
        )
        numerator_message = row_numerators.astype(jnp.bfloat16).reshape(req_count, local_rows, head_cols)
        stats_message = jnp.concatenate(
            [row_shift.reshape(req_count, local_rows, pairs), row_totals.reshape(req_count, local_rows, pairs)],
            axis=2,
        ).transpose(0, 2, 1)

    mixed_rows = attend_exchange(
        numerator_message,
        stats_message,
        queries.reshape(local_rows, head_cols),
        new_keys.reshape(local_rows, local_kv * head_width),
        new_values.reshape(local_rows, local_kv * head_width),
        gate_logits,
        w_out,
        hidden,
        head_count,
        group_size,
        scale_factor,
        1,
    )

    return tail_exchange(
        mixed_rows,
        mlp_gain.reshape(1, model_width),
        mlp_gate,
        mlp_up,
        mlp_down,
        deal_order.reshape(1, all_rows),
        head_count,
        req_count,
        3,
    )


def solution(mesh):
    return jax.shard_map(
        functools.partial(body, mesh.shape["req"], mesh.shape["head"]),
        mesh=mesh,
        in_specs=(
            P("req", None),
            P(),
            P(),
            P(),
            P("req", None, "head", None),
            P("req", None, "head", None),
            P(),
            P(None, "head"),
            P(None, "head"),
            P(None, "head"),
            P(None, "head"),
            P("head", None),
            P(),
            P(),
            P(),
            P(None, "head"),
            P(None, "head"),
            P("head", None),
        ),
        out_specs=P("req", None),
        check_vma=False,
    )
```

```python
import functools
import math

import jax
import jax.numpy as jnp
from jax import lax
from jax.experimental import pallas as pl
from jax.experimental.pallas import tpu as pltpu
from jax.sharding import PartitionSpec as P

EPSILON = 1e-06
ROPE_BASE = 1000000.0
LOW_SCORE = -1e30
LOG_TWO = math.log(2.0)
MESH_IDS = pl.DeviceIdType.MESH


def rms_inv(values):
    return lax.rsqrt(jnp.mean(values * values, axis=-1, keepdims=True) + EPSILON)


def rotate(values, position):
    half_dim = values.shape[-1] // 2
    exponent = jnp.arange(half_dim, dtype=jnp.float32) * (2.0 / values.shape[-1])
    frequency = ROPE_BASE ** (-exponent)
    angles = position[:, None] * frequency[None, :]
    ones_tail = (1,) * (values.ndim - 2)
    angles = angles.reshape((angles.shape[0],) + ones_tail + (half_dim,))
    cosine = jnp.cos(angles)
    sine_vals = jnp.sin(angles)
    front_half = values[..., :half_dim]
    back_half = values[..., half_dim:]
    return jnp.concatenate(
        [front_half * cosine - back_half * sine_vals, back_half * cosine + front_half * sine_vals],
        axis=-1,
    )


def norm_rotate(values, gain_vec, position):
    return rotate(values * rms_inv(values) * gain_vec, position)


def exchange_kernel(axis, count, spreads, *refs):
    arrays = len(spreads)
    sources, outputs = refs[:arrays], refs[arrays : 2 * arrays]
    send_sems, recv_sems = refs[2 * arrays], refs[2 * arrays + 1]
    me = lax.axis_index(axis)
    barrier = pltpu.get_barrier_semaphore()
    for offset in range(1, count):
        peer = lax.rem(me + offset, count)
        pl.semaphore_signal(barrier, inc=1, device_id={axis: peer}, device_id_type=MESH_IDS)
    pl.semaphore_wait(barrier, count - 1)
    copies = []
    for offset in range(1, count):
        peer = lax.rem(me + offset, count)
        for which in range(arrays):
            src_ref, out_ref = sources[which], outputs[which]
            copy = pltpu.make_async_remote_copy(
                src_ref=src_ref.at[peer] if spreads[which] else src_ref,
                dst_ref=out_ref.at[me],
                send_sem=send_sems.at[which, offset],
                recv_sem=recv_sems.at[which, offset],
                device_id={axis: peer},
                device_id_type=MESH_IDS,
            )
            copy.start()
            copies.append(copy)
    for which in range(arrays):
        src_ref, out_ref = sources[which], outputs[which]
        out_ref[me] = src_ref[me] if spreads[which] else src_ref[...]
    for copy in copies:
        copy.wait()


def exchange_many(arrays, spreads, axis, count, ident):
    shapes = []
    for values, spread in zip(arrays, spreads):
        block = values.shape[1:] if spread else values.shape
        shapes.append(jax.ShapeDtypeStruct((count,) + tuple(block), values.dtype))
    return pl.pallas_call(
        functools.partial(exchange_kernel, axis, count, tuple(spreads)),
        out_shape=tuple(shapes),
        in_specs=[pl.BlockSpec(memory_space=pltpu.VMEM)] * len(arrays),
        out_specs=tuple(pl.BlockSpec(memory_space=pltpu.VMEM) for _ in arrays),
        scratch_shapes=[
            pltpu.SemaphoreType.DMA((len(arrays), count)),
            pltpu.SemaphoreType.DMA((len(arrays), count)),
        ],
        compiler_params=pltpu.CompilerParams(collective_id=ident, has_side_effects=True),
    )(*arrays)


def exchange(values, axis, count, spread, ident):
    return exchange_many((values,), (spread,), axis, count, ident)[0]


def greet(peers):
    barrier = pltpu.get_barrier_semaphore()
    for axis, peer in peers:
        pl.semaphore_signal(barrier, inc=1, device_id={axis: peer}, device_id_type=MESH_IDS)
    pl.semaphore_wait(barrier, len(peers))


def peers_of(axis, count):
    me = lax.axis_index(axis)
    return me, [(offset, lax.rem(me + offset, count)) for offset in range(1, count)]


def send_all(axis, peers, src_of, dst, send_sems, recv_sems, phase):
    copies = []
    for offset, peer in peers:
        copy = pltpu.make_async_remote_copy(
            src_ref=src_of(peer),
            dst_ref=dst,
            send_sem=send_sems.at[phase, offset],
            recv_sem=recv_sems.at[phase, offset],
            device_id={axis: peer},
            device_id_type=MESH_IDS,
        )
        copy.start()
        copies.append(copy)
    for copy in copies:
        copy.wait()


def residual_kernel(count, parts_ref, hidden_ref, out_ref, summed, send_sems, recv_sems):
    me, peers = peers_of("head", count)
    cols = out_ref.shape[1] // count
    mine = pl.ds(pl.multiple_of(me * cols, cols), cols)
    greet([("head", peer) for _, peer in peers])
    summed[me] = parts_ref[:, mine]
    send_all(
        "head", peers, lambda peer: parts_ref.at[:, pl.ds(peer * cols, cols)], summed.at[me], send_sems, recv_sems, 0
    )
    out_ref[:, mine] = (hidden_ref[:, mine].astype(jnp.float32) + jnp.sum(summed[...], axis=0)).astype(
        out_ref.dtype
    )
    send_all("head", peers, lambda peer: out_ref.at[:, mine], out_ref.at[:, mine], send_sems, recv_sems, 1)


def residual_exchange(parts, hidden, count, ident):
    rows, width = parts.shape
    return pl.pallas_call(
        functools.partial(residual_kernel, count),
        out_shape=jax.ShapeDtypeStruct((rows, width), jnp.bfloat16),
        in_specs=[pl.BlockSpec(memory_space=pltpu.VMEM)] * 2,
        out_specs=pl.BlockSpec(memory_space=pltpu.VMEM),
        scratch_shapes=[
            pltpu.VMEM((count, rows, width // count), jnp.float32),
            pltpu.SemaphoreType.DMA((2, count)),
            pltpu.SemaphoreType.DMA((2, count)),
        ],
        compiler_params=pltpu.CompilerParams(collective_id=ident, has_side_effects=True),
    )(parts, hidden)


def rope(values, cos_ref, sin_ref, swap):
    swapped = jnp.dot(values, swap, precision=lax.Precision.HIGHEST, preferred_element_type=jnp.float32)
    return values * cos_ref[...] + swapped * sin_ref[...]


def query_kernel(
    count, hidden_ref, attn_gain_ref, w_query_ref, query_gain_ref, w_gate_ref, w_value_ref, w_key_ref,
    key_gain_ref, cos_ref, sin_ref, out_ref, query_ref, gate_ref, value_ref, key_ref, send_sems, recv_sems,
):
    me, peers = peers_of("req", count)
    barrier = pltpu.get_barrier_semaphore()
    for _, peer in peers:
        pl.semaphore_signal(barrier, inc=1, device_id={"req": peer}, device_id_type=MESH_IDS)
    head_width = cos_ref.shape[1]
    lanes_in = lax.broadcasted_iota(jnp.int32, (head_width, head_width), 0)
    lanes_out = lax.broadcasted_iota(jnp.int32, (head_width, head_width), 1)
    swap = jnp.where(
        lanes_in == lax.rem(lanes_out + head_width // 2, head_width),
        jnp.where(lanes_out < head_width // 2, -1.0, 1.0),
        0.0,
    ).astype(jnp.float32)
    hidden = hidden_ref[...].astype(jnp.float32)
    normed = (hidden * rms_inv(hidden) * attn_gain_ref[...]).astype(jnp.bfloat16)
    queries = jnp.dot(normed, w_query_ref[...], preferred_element_type=jnp.float32)
    for pair in range(queries.shape[1] // head_width):
        lanes = slice(pair * head_width, (pair + 1) * head_width)
        query = queries[:, lanes]
        query = query * rms_inv(query) * query_gain_ref[...]
        query_ref[:, lanes] = rope(query, cos_ref, sin_ref, swap).astype(query_ref.dtype)
    pl.semaphore_wait(barrier, len(peers))
    copies = []
    for offset, peer in peers:
        copy = pltpu.make_async_remote_copy(
            src_ref=query_ref,
            dst_ref=out_ref.at[me],
            send_sem=send_sems.at[offset],
            recv_sem=recv_sems.at[offset],
            device_id={"req": peer},
            device_id_type=MESH_IDS,
        )
        copy.start()
        copies.append(copy)
    out_ref[me] = query_ref[...]
    gate_ref[...] = jnp.dot(normed, w_gate_ref[...], preferred_element_type=jnp.float32)
    value_ref[...] = jnp.dot(normed, w_value_ref[...], preferred_element_type=jnp.float32).astype(value_ref.dtype)
    keys = jnp.dot(normed, w_key_ref[...], preferred_element_type=jnp.float32)
    for kv in range(keys.shape[1] // head_width):
        lanes = slice(kv * head_width, (kv + 1) * head_width)
        key = keys[:, lanes]
        key = key * rms_inv(key) * key_gain_ref[...]
        key_ref[:, lanes] = rope(key, cos_ref, sin_ref, swap).astype(key_ref.dtype)
    for copy in copies:
        copy.wait()


def query_exchange(
    hidden, attn_gain, w_query, query_gain, w_gate, w_value, w_key, key_gain, cosine, sine, count, ident
):
    rows = hidden.shape[0]
    return pl.pallas_call(
        functools.partial(query_kernel, count),
        out_shape=(
            jax.ShapeDtypeStruct((count, rows, w_query.shape[1]), jnp.bfloat16),
            jax.ShapeDtypeStruct((rows, w_query.shape[1]), jnp.bfloat16),
            jax.ShapeDtypeStruct((rows, w_gate.shape[1]), jnp.float32),
            jax.ShapeDtypeStruct((rows, w_value.shape[1]), jnp.bfloat16),
            jax.ShapeDtypeStruct((rows, w_key.shape[1]), jnp.bfloat16),
        ),
        in_specs=[pl.BlockSpec(memory_space=pltpu.VMEM)] * 10,
        out_specs=tuple(pl.BlockSpec(memory_space=pltpu.VMEM) for _ in range(5)),
        scratch_shapes=[pltpu.SemaphoreType.DMA((count,)), pltpu.SemaphoreType.DMA((count,))],
        compiler_params=pltpu.CompilerParams(collective_id=ident, has_side_effects=True),
    )(hidden, attn_gain, w_query, query_gain, w_gate, w_value, w_key, key_gain, cosine, sine)


def attend_kernel(
    req_count, head_count, group_size, scale_factor, num_ref, stats_ref, query_ref, key_ref, value_ref, gate_ref,
    w_out_ref, hidden_ref, out_ref, got_num, got_stats, projected, summed, send_sems, recv_sems,
):
    req_me, req_peers = peers_of("req", req_count)
    head_me, head_peers = peers_of("head", head_count)
    rows, width = out_ref.shape
    cols = width // head_count
    pairs = stats_ref.shape[1] // 2
    head_width = query_ref.shape[1] // pairs
    mine = pl.ds(pl.multiple_of(head_me * cols, cols), cols)
    greet([("req", peer) for _, peer in req_peers] + [("head", peer) for _, peer in head_peers])
    got_num[req_me] = num_ref[req_me]
    got_stats[req_me] = stats_ref[req_me]
    copies = []
    for offset, peer in req_peers:
        for which, (src_ref, dst_ref) in enumerate(((num_ref, got_num), (stats_ref, got_stats))):
            copy = pltpu.make_async_remote_copy(
                src_ref=src_ref.at[peer],
                dst_ref=dst_ref.at[req_me],
                send_sem=send_sems.at[which, offset],
                recv_sem=recv_sems.at[which, offset],
                device_id={"req": peer},
                device_id_type=MESH_IDS,
            )
            copy.start()
            copies.append(copy)
    for copy in copies:
        copy.wait()
    eye = (
        lax.broadcasted_iota(jnp.int32, (rows, rows), 0) == lax.broadcasted_iota(jnp.int32, (rows, rows), 1)
    ).astype(jnp.float32)
    flip = (((1,), (1,)), ((), ()))
    heads = []
    for pair in range(pairs):
        kv = pair // group_size
        lanes = slice(pair * head_width, (pair + 1) * head_width)
        kv_lanes = slice(kv * head_width, (kv + 1) * head_width)
        shifts = lax.dot_general(
            eye, got_stats[:, pair, :], flip, precision=lax.Precision.HIGHEST, preferred_element_type=jnp.float32
        )
        totals = lax.dot_general(
            eye,
            got_stats[:, pairs + pair, :],
            flip,
            precision=lax.Precision.HIGHEST,
            preferred_element_type=jnp.float32,
        )
        query = query_ref[:, lanes].astype(jnp.float32)
        self_score = jnp.sum(query * key_ref[:, kv_lanes].astype(jnp.float32), axis=1, keepdims=True) * scale_factor
        self_shift = LOG_TWO * jnp.ceil(self_score / LOG_TWO)
        shift = jnp.maximum(jnp.max(shifts, axis=1, keepdims=True), self_shift)
        factor = jnp.exp(shifts - shift)
        self_weight = jnp.exp(self_score - shift)
        total = jnp.sum(totals * factor, axis=1, keepdims=True) + self_weight
        acc = self_weight.astype(jnp.bfloat16).astype(jnp.float32) * value_ref[:, kv_lanes].astype(jnp.float32)
        for source in range(req_count):
            acc = acc + factor[:, source : source + 1] * got_num[source, :, lanes].astype(jnp.float32)
        heads.append(acc / total)
    heads_out = jnp.concatenate(heads, axis=1)
    gate = gate_ref[...]
    attended = (heads_out * (1.0 / (1.0 + jnp.exp(-gate)))).astype(jnp.bfloat16)
    projected[...] = jnp.dot(attended, w_out_ref[...], preferred_element_type=jnp.float32)
    summed[head_me] = projected[:, mine]
    send_all(
        "head", head_peers, lambda peer: projected.at[:, pl.ds(peer * cols, cols)], summed.at[head_me],
        send_sems, recv_sems, 2,
    )
    out_ref[:, mine] = (hidden_ref[:, mine].astype(jnp.float32) + jnp.sum(summed[...], axis=0)).astype(
        out_ref.dtype
    )
    send_all("head", head_peers, lambda peer: out_ref.at[:, mine], out_ref.at[:, mine], send_sems, recv_sems, 3)


def attend_exchange(
    num, stats, queries, keys, values, gate, w_out, hidden, head_count, group_size, scale_factor, ident
):
    req_count = num.shape[0]
    rows, width = hidden.shape
    most = max(head_count, req_count)
    return pl.pallas_call(
        functools.partial(attend_kernel, req_count, head_count, group_size, scale_factor),
        out_shape=jax.ShapeDtypeStruct((rows, width), jnp.bfloat16),
        in_specs=[pl.BlockSpec(memory_space=pltpu.VMEM)] * 8,
        out_specs=pl.BlockSpec(memory_space=pltpu.VMEM),
        scratch_shapes=[
            pltpu.VMEM(num.shape, num.dtype),
            pltpu.VMEM(stats.shape, stats.dtype),
            pltpu.VMEM((rows, width), jnp.float32),
            pltpu.VMEM((head_count, rows, width // head_count), jnp.float32),
            pltpu.SemaphoreType.DMA((4, most)),
            pltpu.SemaphoreType.DMA((4, most)),
        ],
        compiler_params=pltpu.CompilerParams(collective_id=ident, has_side_effects=True),
    )(num, stats, queries, keys, values, gate, w_out, hidden)


def tail_kernel(
    head_count, req_count, mixed_ref, gain_ref, w_gate_ref, w_up_ref, w_down_ref, order_ref, out_ref, parts_ref,
    summed, results, send_sems, recv_sems,
):
    head_me, head_peers = peers_of("head", head_count)
    req_me, req_peers = peers_of("req", req_count)
    rows, width = out_ref.shape
    cols = width // head_count
    mine = pl.ds(pl.multiple_of(head_me * cols, cols), cols)
    barrier = pltpu.get_barrier_semaphore()
    everyone = [("head", peer) for _, peer in head_peers] + [("req", peer) for _, peer in req_peers]
    for axis, peer in everyone:
        pl.semaphore_signal(barrier, inc=1, device_id={axis: peer}, device_id_type=MESH_IDS)
    mixed = mixed_ref[...].astype(jnp.float32)
    normed = (mixed * rms_inv(mixed) * gain_ref[...]).astype(jnp.bfloat16)
    gate_part = jnp.dot(normed, w_gate_ref[...], preferred_element_type=jnp.float32)
    up_part = jnp.dot(normed, w_up_ref[...], preferred_element_type=jnp.float32)
    inner_act = (gate_part / (1.0 + jnp.exp(-gate_part)) * up_part).astype(jnp.bfloat16)
    parts_ref[...] = jnp.dot(inner_act, w_down_ref[...], preferred_element_type=jnp.float32)
    pl.semaphore_wait(barrier, len(everyone))
    summed[head_me] = parts_ref[:, mine]
    send_all(
        "head",
        head_peers,
        lambda peer: parts_ref.at[:, pl.ds(peer * cols, cols)],
        summed.at[head_me],
        send_sems,
        recv_sems,
        0,
    )
    results[req_me] = (mixed_ref[:, mine].astype(jnp.float32) + jnp.sum(summed[...], axis=0)).astype(
        results.dtype
    )
    send_all("req", req_peers, lambda peer: results.at[req_me], results.at[req_me], send_sems, recv_sems, 1)
    wanted = req_me * rows + lax.broadcasted_iota(jnp.int32, (rows, req_count * rows), 0)
    picker = (order_ref[...] == wanted).astype(jnp.bfloat16)
    out_ref[:, mine] = jnp.dot(
        picker, results[...].reshape(req_count * rows, cols), preferred_element_type=jnp.float32
    ).astype(out_ref.dtype)
    send_all("head", head_peers, lambda peer: out_ref.at[:, mine], out_ref.at[:, mine], send_sems, recv_sems, 2)


def tail_exchange(mixed, gain, w_gate, w_up, w_down, order, head_count, req_count, ident):
    rows, width = mixed.shape
    most = max(head_count, req_count)
    return pl.pallas_call(
        functools.partial(tail_kernel, head_count, req_count),
        out_shape=jax.ShapeDtypeStruct((rows, width), jnp.bfloat16),
        in_specs=[pl.BlockSpec(memory_space=pltpu.VMEM)] * 6,
        out_specs=pl.BlockSpec(memory_space=pltpu.VMEM),
        scratch_shapes=[
            pltpu.VMEM((rows, width), jnp.float32),
            pltpu.VMEM((head_count, rows, width // head_count), jnp.float32),
            pltpu.VMEM((req_count, rows, width // head_count), jnp.bfloat16),
            pltpu.SemaphoreType.DMA((3, most)),
            pltpu.SemaphoreType.DMA((3, most)),
        ],
        compiler_params=pltpu.CompilerParams(collective_id=ident, has_side_effects=True),
    )(mixed, gain, w_gate, w_up, w_down, order)


def body(
    req_count,
    head_count,
    hidden,
    deal_order,
    lengths,
    page_table,
    key_cache,
    value_cache,
    attn_gain,
    w_query,
    w_key,
    w_value,
    w_gate,
    w_out,
    query_gain,
    key_gain,
    mlp_gain,
    mlp_gate,
    mlp_up,
    mlp_down,
):
    local_rows, model_width = hidden.shape
    req_index = lax.axis_index("req")
    head_index = lax.axis_index("head")
    all_rows = local_rows * req_count
    head_width = query_gain.shape[0]
    pool_pages, page_size, local_kv = key_cache.shape[:3]
    group_size = w_query.shape[1] // (local_kv * head_width)
    head_cols = local_kv * group_size * head_width
    pairs = local_kv * group_size
    chunk = model_width // head_count
    scale_factor = 1.0 / math.sqrt(head_width)
    first_own = req_index * local_rows

    with jax.named_scope("rotary_tables"):
        own_requests = lax.dynamic_slice_in_dim(deal_order, first_own, local_rows)
        request_ids = jnp.arange(all_rows, dtype=jnp.int32)
        own_pick = own_requests[:, None] == request_ids[None, :]
        position = jnp.sum(jnp.where(own_pick, lengths[None, :], 0), axis=1).astype(jnp.float32)
        half = head_width // 2
        frequency = ROPE_BASE ** (-(jnp.arange(half, dtype=jnp.float32) * (2.0 / head_width)))
        angles = position[:, None] * frequency[None, :]
        cosine = jnp.concatenate([jnp.cos(angles)] * 2, axis=1)
        sine = jnp.concatenate([jnp.sin(angles)] * 2, axis=1)

    all_queries, own_queries, gate_logits, new_values, new_keys = query_exchange(
        hidden,
        attn_gain.reshape(1, model_width),
        w_query,
        query_gain.reshape(1, head_width),
        w_gate,
        w_value,
        w_key,
        key_gain.reshape(1, head_width),
        cosine,
        sine,
        req_count,
        0,
    )
    all_queries = all_queries.reshape(all_rows, head_cols)
    new_values = new_values.reshape(local_rows, local_kv, head_width)
    new_keys = new_keys.reshape(local_rows, local_kv, head_width)

    with jax.named_scope("page_owners"):
        page_counts = (lengths + page_size - 1) // page_size
        slot_ids = jnp.arange(page_table.shape[1], dtype=jnp.int32)
        local_ids = page_table - req_index * pool_pages
        usable = (
            (slot_ids[None, :] < page_counts[:, None]) & (local_ids >= 0) & (local_ids < pool_pages)
        )
        keyed = jnp.where(usable, local_ids, pool_pages)
        page_ids = jnp.arange(pool_pages, dtype=jnp.int32)
        match = keyed[None, :, :] == page_ids[:, None, None]
        owned_requests = jnp.any(match, axis=2)
        owner_slot = jnp.sum(jnp.where(match, slot_ids[None, None, :], 0), axis=(1, 2))
        owner_length = jnp.sum(jnp.where(owned_requests, lengths[None, :], 0), axis=1)
        filled = jnp.clip(owner_length - owner_slot * page_size, 0, page_size)
        filled = jnp.where(jnp.any(owned_requests, axis=1), filled, 0)
        dealing = (request_ids[:, None] == deal_order[None, :]).astype(jnp.bfloat16)
        owned = (
            jnp.dot(owned_requests.astype(jnp.bfloat16), dealing, preferred_element_type=jnp.float32)
            > 0.5
        )
        page_queries = (
            jnp.dot(owned.astype(jnp.bfloat16), all_queries, preferred_element_type=jnp.float32)
            .astype(jnp.bfloat16)
            .reshape(pool_pages, local_kv, group_size, head_width)
        )

    with jax.named_scope("page_attention"):
        scores = (
            jnp.einsum("pkgd,ptkd->pkgt", page_queries, key_cache, preferred_element_type=jnp.float32)
            * scale_factor
        )
        live_mask = (
            jnp.arange(page_size, dtype=jnp.int32)[None, None, None, :] < filled[:, None, None, None]
        )
        scores = jnp.where(live_mask, scores, LOW_SCORE)
        page_peaks = jnp.max(scores, axis=-1)
        owned_b = owned[:, :, None, None]
        row_peaks = jnp.max(jnp.where(owned_b, page_peaks[:, None], LOW_SCORE), axis=0)
        row_shift = LOG_TWO * jnp.ceil(row_peaks / LOG_TWO)
        page_shift = jnp.max(jnp.where(owned_b, row_shift[None], LOW_SCORE), axis=1)
        weights = jnp.where(live_mask, jnp.exp(scores - page_shift[..., None]), 0.0)
        page_totals = jnp.sum(weights, axis=-1)
        page_numerators = jnp.einsum(
            "pkgt,ptkd->pkgd",
            weights.astype(jnp.bfloat16),
            value_cache,
            preferred_element_type=jnp.float32,
        )
        owned_f = owned.astype(jnp.float32)
        row_totals = jnp.dot(
            owned_f.T, page_totals.reshape(pool_pages, pairs), precision=lax.Precision.HIGHEST
        )
        row_numerators = jnp.dot(
            owned_f.T,
            page_numerators.reshape(pool_pages, head_cols),
            precision=lax.Precision.HIGHEST,
        )
        numerator_message = row_numerators.astype(jnp.bfloat16).reshape(req_count, local_rows, head_cols)
        stats_message = jnp.concatenate(
            [row_shift.reshape(req_count, local_rows, pairs), row_totals.reshape(req_count, local_rows, pairs)],
            axis=2,
        ).transpose(0, 2, 1)

    mixed_rows = attend_exchange(
        numerator_message,
        stats_message,
        own_queries,
        new_keys.reshape(local_rows, local_kv * head_width),
        new_values.reshape(local_rows, local_kv * head_width),
        gate_logits,
        w_out,
        hidden,
        head_count,
        group_size,
        scale_factor,
        1,
    )

    return tail_exchange(
        mixed_rows,
        mlp_gain.reshape(1, model_width),
        mlp_gate,
        mlp_up,
        mlp_down,
        deal_order.reshape(1, all_rows),
        head_count,
        req_count,
        3,
    )


def solution(mesh):
    return jax.shard_map(
        functools.partial(body, mesh.shape["req"], mesh.shape["head"]),
        mesh=mesh,
        in_specs=(
            P("req", None),
            P(),
            P(),
            P(),
            P("req", None, "head", None),
            P("req", None, "head", None),
            P(),
            P(None, "head"),
            P(None, "head"),
            P(None, "head"),
            P(None, "head"),
            P("head", None),
            P(),
            P(),
            P(),
            P(None, "head"),
            P(None, "head"),
            P("head", None),
        ),
        out_specs=P("req", None),
        check_vma=False,
    )
```

```python
import functools
import math

import jax
import jax.numpy as jnp
from jax import lax
from jax.experimental import pallas as pl
from jax.experimental.pallas import tpu as pltpu
from jax.sharding import PartitionSpec as P

EPSILON = 1e-06
ROPE_BASE = 1000000.0
LOW_SCORE = -1e30
LOG_TWO = math.log(2.0)
MESH_IDS = pl.DeviceIdType.MESH


def rms_inv(values):
    return lax.rsqrt(jnp.mean(values * values, axis=-1, keepdims=True) + EPSILON)


def rotate(values, position):
    half_dim = values.shape[-1] // 2
    exponent = jnp.arange(half_dim, dtype=jnp.float32) * (2.0 / values.shape[-1])
    frequency = ROPE_BASE ** (-exponent)
    angles = position[:, None] * frequency[None, :]
    ones_tail = (1,) * (values.ndim - 2)
    angles = angles.reshape((angles.shape[0],) + ones_tail + (half_dim,))
    cosine = jnp.cos(angles)
    sine_vals = jnp.sin(angles)
    front_half = values[..., :half_dim]
    back_half = values[..., half_dim:]
    return jnp.concatenate(
        [front_half * cosine - back_half * sine_vals, back_half * cosine + front_half * sine_vals],
        axis=-1,
    )


def norm_rotate(values, gain_vec, position):
    return rotate(values * rms_inv(values) * gain_vec, position)


def exchange_kernel(axis, count, spreads, *refs):
    arrays = len(spreads)
    sources, outputs = refs[:arrays], refs[arrays : 2 * arrays]
    send_sems, recv_sems = refs[2 * arrays], refs[2 * arrays + 1]
    me = lax.axis_index(axis)
    barrier = pltpu.get_barrier_semaphore()
    for offset in range(1, count):
        peer = lax.rem(me + offset, count)
        pl.semaphore_signal(barrier, inc=1, device_id={axis: peer}, device_id_type=MESH_IDS)
    pl.semaphore_wait(barrier, count - 1)
    copies = []
    for offset in range(1, count):
        peer = lax.rem(me + offset, count)
        for which in range(arrays):
            src_ref, out_ref = sources[which], outputs[which]
            copy = pltpu.make_async_remote_copy(
                src_ref=src_ref.at[peer] if spreads[which] else src_ref,
                dst_ref=out_ref.at[me],
                send_sem=send_sems.at[which, offset],
                recv_sem=recv_sems.at[which, offset],
                device_id={axis: peer},
                device_id_type=MESH_IDS,
            )
            copy.start()
            copies.append(copy)
    for which in range(arrays):
        src_ref, out_ref = sources[which], outputs[which]
        out_ref[me] = src_ref[me] if spreads[which] else src_ref[...]
    for copy in copies:
        copy.wait()


def exchange_many(arrays, spreads, axis, count, ident):
    shapes = []
    for values, spread in zip(arrays, spreads):
        block = values.shape[1:] if spread else values.shape
        shapes.append(jax.ShapeDtypeStruct((count,) + tuple(block), values.dtype))
    return pl.pallas_call(
        functools.partial(exchange_kernel, axis, count, tuple(spreads)),
        out_shape=tuple(shapes),
        in_specs=[pl.BlockSpec(memory_space=pltpu.VMEM)] * len(arrays),
        out_specs=tuple(pl.BlockSpec(memory_space=pltpu.VMEM) for _ in arrays),
        scratch_shapes=[
            pltpu.SemaphoreType.DMA((len(arrays), count)),
            pltpu.SemaphoreType.DMA((len(arrays), count)),
        ],
        compiler_params=pltpu.CompilerParams(collective_id=ident, has_side_effects=True),
    )(*arrays)


def exchange(values, axis, count, spread, ident):
    return exchange_many((values,), (spread,), axis, count, ident)[0]


def greet(peers):
    barrier = pltpu.get_barrier_semaphore()
    for axis, peer in peers:
        pl.semaphore_signal(barrier, inc=1, device_id={axis: peer}, device_id_type=MESH_IDS)
    pl.semaphore_wait(barrier, len(peers))


def peers_of(axis, count):
    me = lax.axis_index(axis)
    return me, [(offset, lax.rem(me + offset, count)) for offset in range(1, count)]


def send_all(axis, peers, src_of, dst, send_sems, recv_sems, phase):
    copies = []
    for offset, peer in peers:
        copy = pltpu.make_async_remote_copy(
            src_ref=src_of(peer),
            dst_ref=dst,
            send_sem=send_sems.at[phase, offset],
            recv_sem=recv_sems.at[phase, offset],
            device_id={axis: peer},
            device_id_type=MESH_IDS,
        )
        copy.start()
        copies.append(copy)
    for copy in copies:
        copy.wait()


def residual_kernel(count, parts_ref, hidden_ref, out_ref, summed, send_sems, recv_sems):
    me, peers = peers_of("head", count)
    cols = out_ref.shape[1] // count
    mine = pl.ds(pl.multiple_of(me * cols, cols), cols)
    greet([("head", peer) for _, peer in peers])
    summed[me] = parts_ref[:, mine]
    send_all(
        "head", peers, lambda peer: parts_ref.at[:, pl.ds(peer * cols, cols)], summed.at[me], send_sems, recv_sems, 0
    )
    out_ref[:, mine] = (hidden_ref[:, mine].astype(jnp.float32) + jnp.sum(summed[...], axis=0)).astype(
        out_ref.dtype
    )
    send_all("head", peers, lambda peer: out_ref.at[:, mine], out_ref.at[:, mine], send_sems, recv_sems, 1)


def residual_exchange(parts, hidden, count, ident):
    rows, width = parts.shape
    return pl.pallas_call(
        functools.partial(residual_kernel, count),
        out_shape=jax.ShapeDtypeStruct((rows, width), jnp.bfloat16),
        in_specs=[pl.BlockSpec(memory_space=pltpu.VMEM)] * 2,
        out_specs=pl.BlockSpec(memory_space=pltpu.VMEM),
        scratch_shapes=[
            pltpu.VMEM((count, rows, width // count), jnp.float32),
            pltpu.SemaphoreType.DMA((2, count)),
            pltpu.SemaphoreType.DMA((2, count)),
        ],
        compiler_params=pltpu.CompilerParams(collective_id=ident, has_side_effects=True),
    )(parts, hidden)


def rope(values, cos_ref, sin_ref, swap):
    swapped = jnp.dot(values, swap, precision=lax.Precision.HIGHEST, preferred_element_type=jnp.float32)
    return values * cos_ref[...] + swapped * sin_ref[...]


def query_kernel(
    count, pool_pages, page_size, hidden_ref, attn_gain_ref, w_query_ref, query_gain_ref, w_gate_ref, w_value_ref,
    w_key_ref, key_gain_ref, cos_ref, sin_ref, table_ref, lengths_ref, order_ref, out_ref, query_ref, gate_ref,
    value_ref, key_ref, owned_ref, filled_ref, page_query_ref, slot_scratch, send_sems, recv_sems,
):
    me, peers = peers_of("req", count)
    barrier = pltpu.get_barrier_semaphore()
    for _, peer in peers:
        pl.semaphore_signal(barrier, inc=1, device_id={"req": peer}, device_id_type=MESH_IDS)
    head_width = cos_ref.shape[1]
    lanes_in = lax.broadcasted_iota(jnp.int32, (head_width, head_width), 0)
    lanes_out = lax.broadcasted_iota(jnp.int32, (head_width, head_width), 1)
    swap = jnp.where(
        lanes_in == lax.rem(lanes_out + head_width // 2, head_width),
        jnp.where(lanes_out < head_width // 2, -1.0, 1.0),
        0.0,
    ).astype(jnp.float32)
    hidden = hidden_ref[...].astype(jnp.float32)
    normed = (hidden * rms_inv(hidden) * attn_gain_ref[...]).astype(jnp.bfloat16)
    queries = jnp.dot(normed, w_query_ref[...], preferred_element_type=jnp.float32)
    for pair in range(queries.shape[1] // head_width):
        lanes = slice(pair * head_width, (pair + 1) * head_width)
        query = queries[:, lanes]
        query = query * rms_inv(query) * query_gain_ref[...]
        query_ref[:, lanes] = rope(query, cos_ref, sin_ref, swap).astype(query_ref.dtype)
    pl.semaphore_wait(barrier, len(peers))
    copies = []
    for offset, peer in peers:
        copy = pltpu.make_async_remote_copy(
            src_ref=query_ref,
            dst_ref=out_ref.at[me],
            send_sem=send_sems.at[offset],
            recv_sem=recv_sems.at[offset],
            device_id={"req": peer},
            device_id_type=MESH_IDS,
        )
        copy.start()
        copies.append(copy)
    out_ref[me] = query_ref[...]
    gate_ref[...] = jnp.dot(normed, w_gate_ref[...], preferred_element_type=jnp.float32)
    value_ref[...] = jnp.dot(normed, w_value_ref[...], preferred_element_type=jnp.float32).astype(value_ref.dtype)
    keys = jnp.dot(normed, w_key_ref[...], preferred_element_type=jnp.float32)
    for kv in range(keys.shape[1] // head_width):
        lanes = slice(kv * head_width, (kv + 1) * head_width)
        key = keys[:, lanes]
        key = key * rms_inv(key) * key_gain_ref[...]
        key_ref[:, lanes] = rope(key, cos_ref, sin_ref, swap).astype(key_ref.dtype)
    slots, requests = table_ref.shape
    slot_ids = lax.broadcasted_iota(jnp.int32, (slots, requests), 0)
    lengths = lengths_ref[...]
    local_ids = table_ref[...] - me * pool_pages
    usable = (slot_ids < (lengths + page_size - 1) // page_size) & (local_ids >= 0) & (local_ids < pool_pages)
    keyed = jnp.where(usable, local_ids, pool_pages)
    slot_f = slot_ids.astype(jnp.float32)

    def one_page(page, carry):
        hit = keyed == page
        owned_ref[pl.ds(page, 1), :] = jnp.max(jnp.where(hit, 1.0, 0.0), axis=0, keepdims=True)
        slot_scratch[pl.ds(page, 1), :] = jnp.sum(jnp.where(hit, slot_f, 0.0), axis=0, keepdims=True)
        return carry

    lax.fori_loop(0, pool_pages, one_page, 0)
    owned_requests = owned_ref[...]
    owner_slot = jnp.sum(slot_scratch[...], axis=1, keepdims=True)
    owner_length = jnp.sum(owned_requests * lengths.astype(jnp.float32), axis=1, keepdims=True)
    filled = jnp.clip(owner_length - owner_slot * page_size, 0.0, float(page_size))
    filled_ref[...] = jnp.where(jnp.max(owned_requests, axis=1, keepdims=True) > 0.5, filled, 0.0).astype(
        jnp.int32
    )
    dealing = (lax.broadcasted_iota(jnp.int32, (requests, requests), 0) == order_ref[...]).astype(jnp.bfloat16)
    owned_rows = jnp.dot(owned_requests.astype(jnp.bfloat16), dealing, preferred_element_type=jnp.float32)
    owned_ref[...] = jnp.where(owned_rows > 0.5, 1.0, 0.0)
    for copy in copies:
        copy.wait()
    rows = query_ref.shape[0]
    page_query_ref[...] = jnp.dot(
        owned_ref[...].astype(jnp.bfloat16),
        out_ref[...].reshape(count * rows, query_ref.shape[1]),
        preferred_element_type=jnp.float32,
    ).astype(page_query_ref.dtype)


def query_exchange(
    hidden, attn_gain, w_query, query_gain, w_gate, w_value, w_key, key_gain, cosine, sine, table, lengths, order,
    pool_pages, page_size, count, ident,
):
    rows = hidden.shape[0]
    requests = table.shape[1]
    return pl.pallas_call(
        functools.partial(query_kernel, count, pool_pages, page_size),
        out_shape=(
            jax.ShapeDtypeStruct((count, rows, w_query.shape[1]), jnp.bfloat16),
            jax.ShapeDtypeStruct((rows, w_query.shape[1]), jnp.bfloat16),
            jax.ShapeDtypeStruct((rows, w_gate.shape[1]), jnp.float32),
            jax.ShapeDtypeStruct((rows, w_value.shape[1]), jnp.bfloat16),
            jax.ShapeDtypeStruct((rows, w_key.shape[1]), jnp.bfloat16),
            jax.ShapeDtypeStruct((pool_pages, requests), jnp.float32),
            jax.ShapeDtypeStruct((pool_pages, 1), jnp.int32),
            jax.ShapeDtypeStruct((pool_pages, w_query.shape[1]), jnp.bfloat16),
        ),
        in_specs=[pl.BlockSpec(memory_space=pltpu.VMEM)] * 13,
        out_specs=tuple(pl.BlockSpec(memory_space=pltpu.VMEM) for _ in range(8)),
        scratch_shapes=[
            pltpu.VMEM((pool_pages, requests), jnp.float32),
            pltpu.SemaphoreType.DMA((count,)),
            pltpu.SemaphoreType.DMA((count,)),
        ],
        compiler_params=pltpu.CompilerParams(collective_id=ident, has_side_effects=True),
    )(hidden, attn_gain, w_query, query_gain, w_gate, w_value, w_key, key_gain, cosine, sine, table, lengths, order)


def attend_kernel(
    req_count, head_count, group_size, scale_factor, num_ref, stats_ref, query_ref, key_ref, value_ref, gate_ref,
    w_out_ref, hidden_ref, out_ref, got_num, got_stats, projected, summed, send_sems, recv_sems,
):
    req_me, req_peers = peers_of("req", req_count)
    head_me, head_peers = peers_of("head", head_count)
    rows, width = out_ref.shape
    cols = width // head_count
    pairs = stats_ref.shape[1] // 2
    head_width = query_ref.shape[1] // pairs
    mine = pl.ds(pl.multiple_of(head_me * cols, cols), cols)
    greet([("req", peer) for _, peer in req_peers] + [("head", peer) for _, peer in head_peers])
    got_num[req_me] = num_ref[req_me]
    got_stats[req_me] = stats_ref[req_me]
    copies = []
    for offset, peer in req_peers:
        for which, (src_ref, dst_ref) in enumerate(((num_ref, got_num), (stats_ref, got_stats))):
            copy = pltpu.make_async_remote_copy(
                src_ref=src_ref.at[peer],
                dst_ref=dst_ref.at[req_me],
                send_sem=send_sems.at[which, offset],
                recv_sem=recv_sems.at[which, offset],
                device_id={"req": peer},
                device_id_type=MESH_IDS,
            )
            copy.start()
            copies.append(copy)
    for copy in copies:
        copy.wait()
    eye = (
        lax.broadcasted_iota(jnp.int32, (rows, rows), 0) == lax.broadcasted_iota(jnp.int32, (rows, rows), 1)
    ).astype(jnp.float32)
    flip = (((1,), (1,)), ((), ()))
    heads = []
    for pair in range(pairs):
        kv = pair // group_size
        lanes = slice(pair * head_width, (pair + 1) * head_width)
        kv_lanes = slice(kv * head_width, (kv + 1) * head_width)
        shifts = lax.dot_general(
            eye, got_stats[:, pair, :], flip, precision=lax.Precision.HIGHEST, preferred_element_type=jnp.float32
        )
        totals = lax.dot_general(
            eye,
            got_stats[:, pairs + pair, :],
            flip,
            precision=lax.Precision.HIGHEST,
            preferred_element_type=jnp.float32,
        )
        query = query_ref[:, lanes].astype(jnp.float32)
        self_score = jnp.sum(query * key_ref[:, kv_lanes].astype(jnp.float32), axis=1, keepdims=True) * scale_factor
        self_shift = LOG_TWO * jnp.ceil(self_score / LOG_TWO)
        shift = jnp.maximum(jnp.max(shifts, axis=1, keepdims=True), self_shift)
        factor = jnp.exp(shifts - shift)
        self_weight = jnp.exp(self_score - shift)
        total = jnp.sum(totals * factor, axis=1, keepdims=True) + self_weight
        acc = self_weight.astype(jnp.bfloat16).astype(jnp.float32) * value_ref[:, kv_lanes].astype(jnp.float32)
        for source in range(req_count):
            acc = acc + factor[:, source : source + 1] * got_num[source, :, lanes].astype(jnp.float32)
        heads.append(acc / total)
    heads_out = jnp.concatenate(heads, axis=1)
    gate = gate_ref[...]
    attended = (heads_out * (1.0 / (1.0 + jnp.exp(-gate)))).astype(jnp.bfloat16)
    projected[...] = jnp.dot(attended, w_out_ref[...], preferred_element_type=jnp.float32)
    summed[head_me] = projected[:, mine]
    send_all(
        "head", head_peers, lambda peer: projected.at[:, pl.ds(peer * cols, cols)], summed.at[head_me],
        send_sems, recv_sems, 2,
    )
    out_ref[:, mine] = (hidden_ref[:, mine].astype(jnp.float32) + jnp.sum(summed[...], axis=0)).astype(
        out_ref.dtype
    )
    send_all("head", head_peers, lambda peer: out_ref.at[:, mine], out_ref.at[:, mine], send_sems, recv_sems, 3)


def attend_exchange(
    num, stats, queries, keys, values, gate, w_out, hidden, head_count, group_size, scale_factor, ident
):
    req_count = num.shape[0]
    rows, width = hidden.shape
    most = max(head_count, req_count)
    return pl.pallas_call(
        functools.partial(attend_kernel, req_count, head_count, group_size, scale_factor),
        out_shape=jax.ShapeDtypeStruct((rows, width), jnp.bfloat16),
        in_specs=[pl.BlockSpec(memory_space=pltpu.VMEM)] * 8,
        out_specs=pl.BlockSpec(memory_space=pltpu.VMEM),
        scratch_shapes=[
            pltpu.VMEM(num.shape, num.dtype),
            pltpu.VMEM(stats.shape, stats.dtype),
            pltpu.VMEM((rows, width), jnp.float32),
            pltpu.VMEM((head_count, rows, width // head_count), jnp.float32),
            pltpu.SemaphoreType.DMA((4, most)),
            pltpu.SemaphoreType.DMA((4, most)),
        ],
        compiler_params=pltpu.CompilerParams(collective_id=ident, has_side_effects=True),
    )(num, stats, queries, keys, values, gate, w_out, hidden)


def tail_kernel(
    head_count, req_count, mixed_ref, gain_ref, w_gate_ref, w_up_ref, w_down_ref, order_ref, out_ref, parts_ref,
    summed, results, send_sems, recv_sems,
):
    head_me, head_peers = peers_of("head", head_count)
    req_me, req_peers = peers_of("req", req_count)
    rows, width = out_ref.shape
    cols = width // head_count
    mine = pl.ds(pl.multiple_of(head_me * cols, cols), cols)
    barrier = pltpu.get_barrier_semaphore()
    everyone = [("head", peer) for _, peer in head_peers] + [("req", peer) for _, peer in req_peers]
    for axis, peer in everyone:
        pl.semaphore_signal(barrier, inc=1, device_id={axis: peer}, device_id_type=MESH_IDS)
    mixed = mixed_ref[...].astype(jnp.float32)
    normed = (mixed * rms_inv(mixed) * gain_ref[...]).astype(jnp.bfloat16)
    gate_part = jnp.dot(normed, w_gate_ref[...], preferred_element_type=jnp.float32)
    up_part = jnp.dot(normed, w_up_ref[...], preferred_element_type=jnp.float32)
    inner_act = (gate_part / (1.0 + jnp.exp(-gate_part)) * up_part).astype(jnp.bfloat16)
    parts_ref[...] = jnp.dot(inner_act, w_down_ref[...], preferred_element_type=jnp.float32)
    pl.semaphore_wait(barrier, len(everyone))
    summed[head_me] = parts_ref[:, mine]
    send_all(
        "head",
        head_peers,
        lambda peer: parts_ref.at[:, pl.ds(peer * cols, cols)],
        summed.at[head_me],
        send_sems,
        recv_sems,
        0,
    )
    results[req_me] = (mixed_ref[:, mine].astype(jnp.float32) + jnp.sum(summed[...], axis=0)).astype(
        results.dtype
    )
    send_all("req", req_peers, lambda peer: results.at[req_me], results.at[req_me], send_sems, recv_sems, 1)
    wanted = req_me * rows + lax.broadcasted_iota(jnp.int32, (rows, req_count * rows), 0)
    picker = (order_ref[...] == wanted).astype(jnp.bfloat16)
    out_ref[:, mine] = jnp.dot(
        picker, results[...].reshape(req_count * rows, cols), preferred_element_type=jnp.float32
    ).astype(out_ref.dtype)
    send_all("head", head_peers, lambda peer: out_ref.at[:, mine], out_ref.at[:, mine], send_sems, recv_sems, 2)


def tail_exchange(mixed, gain, w_gate, w_up, w_down, order, head_count, req_count, ident):
    rows, width = mixed.shape
    most = max(head_count, req_count)
    return pl.pallas_call(
        functools.partial(tail_kernel, head_count, req_count),
        out_shape=jax.ShapeDtypeStruct((rows, width), jnp.bfloat16),
        in_specs=[pl.BlockSpec(memory_space=pltpu.VMEM)] * 6,
        out_specs=pl.BlockSpec(memory_space=pltpu.VMEM),
        scratch_shapes=[
            pltpu.VMEM((rows, width), jnp.float32),
            pltpu.VMEM((head_count, rows, width // head_count), jnp.float32),
            pltpu.VMEM((req_count, rows, width // head_count), jnp.bfloat16),
            pltpu.SemaphoreType.DMA((3, most)),
            pltpu.SemaphoreType.DMA((3, most)),
        ],
        compiler_params=pltpu.CompilerParams(collective_id=ident, has_side_effects=True),
    )(mixed, gain, w_gate, w_up, w_down, order)


def body(
    req_count,
    head_count,
    hidden,
    deal_order,
    lengths,
    page_table,
    key_cache,
    value_cache,
    attn_gain,
    w_query,
    w_key,
    w_value,
    w_gate,
    w_out,
    query_gain,
    key_gain,
    mlp_gain,
    mlp_gate,
    mlp_up,
    mlp_down,
):
    local_rows, model_width = hidden.shape
    req_index = lax.axis_index("req")
    head_index = lax.axis_index("head")
    all_rows = local_rows * req_count
    head_width = query_gain.shape[0]
    pool_pages, page_size, local_kv = key_cache.shape[:3]
    group_size = w_query.shape[1] // (local_kv * head_width)
    head_cols = local_kv * group_size * head_width
    pairs = local_kv * group_size
    chunk = model_width // head_count
    scale_factor = 1.0 / math.sqrt(head_width)
    first_own = req_index * local_rows

    with jax.named_scope("rotary_tables"):
        own_requests = lax.dynamic_slice_in_dim(deal_order, first_own, local_rows)
        request_ids = jnp.arange(all_rows, dtype=jnp.int32)
        own_pick = own_requests[:, None] == request_ids[None, :]
        position = jnp.sum(jnp.where(own_pick, lengths[None, :], 0), axis=1).astype(jnp.float32)
        half = head_width // 2
        frequency = ROPE_BASE ** (-(jnp.arange(half, dtype=jnp.float32) * (2.0 / head_width)))
        angles = position[:, None] * frequency[None, :]
        cosine = jnp.concatenate([jnp.cos(angles)] * 2, axis=1)
        sine = jnp.concatenate([jnp.sin(angles)] * 2, axis=1)

    outs = query_exchange(
        hidden,
        attn_gain.reshape(1, model_width),
        w_query,
        query_gain.reshape(1, head_width),
        w_gate,
        w_value,
        w_key,
        key_gain.reshape(1, head_width),
        cosine,
        sine,
        page_table.T,
        lengths.reshape(1, all_rows),
        deal_order.reshape(1, all_rows),
        pool_pages,
        page_size,
        req_count,
        0,
    )
    _, own_queries, gate_logits, new_values, new_keys, owned_f, filled, page_queries = outs
    filled = filled.reshape(pool_pages)
    owned = owned_f > 0.5
    page_queries = page_queries.reshape(pool_pages, local_kv, group_size, head_width)
    new_values = new_values.reshape(local_rows, local_kv, head_width)
    new_keys = new_keys.reshape(local_rows, local_kv, head_width)

    with jax.named_scope("page_attention"):
        scores = (
            jnp.einsum("pkgd,ptkd->pkgt", page_queries, key_cache, preferred_element_type=jnp.float32)
            * scale_factor
        )
        live_mask = (
            jnp.arange(page_size, dtype=jnp.int32)[None, None, None, :] < filled[:, None, None, None]
        )
        scores = jnp.where(live_mask, scores, LOW_SCORE)
        page_peaks = jnp.max(scores, axis=-1)
        owned_b = owned[:, :, None, None]
        row_peaks = jnp.max(jnp.where(owned_b, page_peaks[:, None], LOW_SCORE), axis=0)
        row_shift = LOG_TWO * jnp.ceil(row_peaks / LOG_TWO)
        page_shift = jnp.max(jnp.where(owned_b, row_shift[None], LOW_SCORE), axis=1)
        weights = jnp.where(live_mask, jnp.exp(scores - page_shift[..., None]), 0.0)
        page_totals = jnp.sum(weights, axis=-1)
        page_numerators = jnp.einsum(
            "pkgt,ptkd->pkgd",
            weights.astype(jnp.bfloat16),
            value_cache,
            preferred_element_type=jnp.float32,
        )
        row_totals = jnp.dot(
            owned_f.T, page_totals.reshape(pool_pages, pairs), precision=lax.Precision.HIGHEST
        )
        row_numerators = jnp.dot(
            owned_f.T,
            page_numerators.reshape(pool_pages, head_cols),
            precision=lax.Precision.HIGHEST,
        )
        numerator_message = row_numerators.astype(jnp.bfloat16).reshape(req_count, local_rows, head_cols)
        stats_message = jnp.concatenate(
            [row_shift.reshape(req_count, local_rows, pairs), row_totals.reshape(req_count, local_rows, pairs)],
            axis=2,
        ).transpose(0, 2, 1)

    mixed_rows = attend_exchange(
        numerator_message,
        stats_message,
        own_queries,
        new_keys.reshape(local_rows, local_kv * head_width),
        new_values.reshape(local_rows, local_kv * head_width),
        gate_logits,
        w_out,
        hidden,
        head_count,
        group_size,
        scale_factor,
        1,
    )

    return tail_exchange(
        mixed_rows,
        mlp_gain.reshape(1, model_width),
        mlp_gate,
        mlp_up,
        mlp_down,
        deal_order.reshape(1, all_rows),
        head_count,
        req_count,
        3,
    )


def solution(mesh):
    return jax.shard_map(
        functools.partial(body, mesh.shape["req"], mesh.shape["head"]),
        mesh=mesh,
        in_specs=(
            P("req", None),
            P(),
            P(),
            P(),
            P("req", None, "head", None),
            P("req", None, "head", None),
            P(),
            P(None, "head"),
            P(None, "head"),
            P(None, "head"),
            P(None, "head"),
            P("head", None),
            P(),
            P(),
            P(),
            P(None, "head"),
            P(None, "head"),
            P("head", None),
        ),
        out_specs=P("req", None),
        check_vma=False,
    )
```

```python
import functools
import math

import jax
import jax.numpy as jnp
from jax import lax
from jax.experimental import pallas as pl
from jax.experimental.pallas import tpu as pltpu
from jax.sharding import PartitionSpec as P

EPSILON = 1e-06
ROPE_BASE = 1000000.0
LOW_SCORE = -1e30
LOG_TWO = math.log(2.0)
MESH_IDS = pl.DeviceIdType.MESH


def rms_inv(values):
    return lax.rsqrt(jnp.mean(values * values, axis=-1, keepdims=True) + EPSILON)


def rotate(values, position):
    half_dim = values.shape[-1] // 2
    exponent = jnp.arange(half_dim, dtype=jnp.float32) * (2.0 / values.shape[-1])
    frequency = ROPE_BASE ** (-exponent)
    angles = position[:, None] * frequency[None, :]
    ones_tail = (1,) * (values.ndim - 2)
    angles = angles.reshape((angles.shape[0],) + ones_tail + (half_dim,))
    cosine = jnp.cos(angles)
    sine_vals = jnp.sin(angles)
    front_half = values[..., :half_dim]
    back_half = values[..., half_dim:]
    return jnp.concatenate(
        [front_half * cosine - back_half * sine_vals, back_half * cosine + front_half * sine_vals],
        axis=-1,
    )


def norm_rotate(values, gain_vec, position):
    return rotate(values * rms_inv(values) * gain_vec, position)


def exchange_kernel(axis, count, spreads, *refs):
    arrays = len(spreads)
    sources, outputs = refs[:arrays], refs[arrays : 2 * arrays]
    send_sems, recv_sems = refs[2 * arrays], refs[2 * arrays + 1]
    me = lax.axis_index(axis)
    barrier = pltpu.get_barrier_semaphore()
    for offset in range(1, count):
        peer = lax.rem(me + offset, count)
        pl.semaphore_signal(barrier, inc=1, device_id={axis: peer}, device_id_type=MESH_IDS)
    pl.semaphore_wait(barrier, count - 1)
    copies = []
    for offset in range(1, count):
        peer = lax.rem(me + offset, count)
        for which in range(arrays):
            src_ref, out_ref = sources[which], outputs[which]
            copy = pltpu.make_async_remote_copy(
                src_ref=src_ref.at[peer] if spreads[which] else src_ref,
                dst_ref=out_ref.at[me],
                send_sem=send_sems.at[which, offset],
                recv_sem=recv_sems.at[which, offset],
                device_id={axis: peer},
                device_id_type=MESH_IDS,
            )
            copy.start()
            copies.append(copy)
    for which in range(arrays):
        src_ref, out_ref = sources[which], outputs[which]
        out_ref[me] = src_ref[me] if spreads[which] else src_ref[...]
    for copy in copies:
        copy.wait()


def exchange_many(arrays, spreads, axis, count, ident):
    shapes = []
    for values, spread in zip(arrays, spreads):
        block = values.shape[1:] if spread else values.shape
        shapes.append(jax.ShapeDtypeStruct((count,) + tuple(block), values.dtype))
    return pl.pallas_call(
        functools.partial(exchange_kernel, axis, count, tuple(spreads)),
        out_shape=tuple(shapes),
        in_specs=[pl.BlockSpec(memory_space=pltpu.VMEM)] * len(arrays),
        out_specs=tuple(pl.BlockSpec(memory_space=pltpu.VMEM) for _ in arrays),
        scratch_shapes=[
            pltpu.SemaphoreType.DMA((len(arrays), count)),
            pltpu.SemaphoreType.DMA((len(arrays), count)),
        ],
        compiler_params=pltpu.CompilerParams(collective_id=ident, has_side_effects=True),
    )(*arrays)


def exchange(values, axis, count, spread, ident):
    return exchange_many((values,), (spread,), axis, count, ident)[0]


def greet(peers):
    barrier = pltpu.get_barrier_semaphore()
    for axis, peer in peers:
        pl.semaphore_signal(barrier, inc=1, device_id={axis: peer}, device_id_type=MESH_IDS)
    pl.semaphore_wait(barrier, len(peers))


def peers_of(axis, count):
    me = lax.axis_index(axis)
    return me, [(offset, lax.rem(me + offset, count)) for offset in range(1, count)]


def send_all(axis, peers, src_of, dst, send_sems, recv_sems, phase):
    copies = []
    for offset, peer in peers:
        copy = pltpu.make_async_remote_copy(
            src_ref=src_of(peer),
            dst_ref=dst,
            send_sem=send_sems.at[phase, offset],
            recv_sem=recv_sems.at[phase, offset],
            device_id={axis: peer},
            device_id_type=MESH_IDS,
        )
        copy.start()
        copies.append(copy)
    for copy in copies:
        copy.wait()


def residual_kernel(count, parts_ref, hidden_ref, out_ref, summed, send_sems, recv_sems):
    me, peers = peers_of("head", count)
    cols = out_ref.shape[1] // count
    mine = pl.ds(pl.multiple_of(me * cols, cols), cols)
    greet([("head", peer) for _, peer in peers])
    summed[me] = parts_ref[:, mine]
    send_all(
        "head", peers, lambda peer: parts_ref.at[:, pl.ds(peer * cols, cols)], summed.at[me], send_sems, recv_sems, 0
    )
    out_ref[:, mine] = (hidden_ref[:, mine].astype(jnp.float32) + jnp.sum(summed[...], axis=0)).astype(
        out_ref.dtype
    )
    send_all("head", peers, lambda peer: out_ref.at[:, mine], out_ref.at[:, mine], send_sems, recv_sems, 1)


def residual_exchange(parts, hidden, count, ident):
    rows, width = parts.shape
    return pl.pallas_call(
        functools.partial(residual_kernel, count),
        out_shape=jax.ShapeDtypeStruct((rows, width), jnp.bfloat16),
        in_specs=[pl.BlockSpec(memory_space=pltpu.VMEM)] * 2,
        out_specs=pl.BlockSpec(memory_space=pltpu.VMEM),
        scratch_shapes=[
            pltpu.VMEM((count, rows, width // count), jnp.float32),
            pltpu.SemaphoreType.DMA((2, count)),
            pltpu.SemaphoreType.DMA((2, count)),
        ],
        compiler_params=pltpu.CompilerParams(collective_id=ident, has_side_effects=True),
    )(parts, hidden)


def rope(values, cos_ref, sin_ref, swap):
    swapped = jnp.dot(values, swap, precision=lax.Precision.HIGHEST, preferred_element_type=jnp.float32)
    return values * cos_ref[...] + swapped * sin_ref[...]


def query_kernel(
    count, pool_pages, page_size, hidden_ref, attn_gain_ref, w_query_ref, query_gain_ref, w_gate_ref, w_value_ref,
    w_key_ref, key_gain_ref, cos_ref, sin_ref, table_ref, lengths_ref, order_ref, out_ref, query_ref, gate_ref,
    value_ref, key_ref, owned_ref, filled_ref, page_query_ref, slot_scratch, send_sems, recv_sems,
):
    me, peers = peers_of("req", count)
    barrier = pltpu.get_barrier_semaphore()
    for _, peer in peers:
        pl.semaphore_signal(barrier, inc=1, device_id={"req": peer}, device_id_type=MESH_IDS)
    head_width = cos_ref.shape[1]
    lanes_in = lax.broadcasted_iota(jnp.int32, (head_width, head_width), 0)
    lanes_out = lax.broadcasted_iota(jnp.int32, (head_width, head_width), 1)
    swap = jnp.where(
        lanes_in == lax.rem(lanes_out + head_width // 2, head_width),
        jnp.where(lanes_out < head_width // 2, -1.0, 1.0),
        0.0,
    ).astype(jnp.float32)
    hidden = hidden_ref[...].astype(jnp.float32)
    normed = (hidden * rms_inv(hidden) * attn_gain_ref[...]).astype(jnp.bfloat16)
    queries = jnp.dot(normed, w_query_ref[...], preferred_element_type=jnp.float32)
    for pair in range(queries.shape[1] // head_width):
        lanes = slice(pair * head_width, (pair + 1) * head_width)
        query = queries[:, lanes]
        query = query * rms_inv(query) * query_gain_ref[...]
        query_ref[:, lanes] = rope(query, cos_ref, sin_ref, swap).astype(query_ref.dtype)
    pl.semaphore_wait(barrier, len(peers))
    copies = []
    for offset, peer in peers:
        copy = pltpu.make_async_remote_copy(
            src_ref=query_ref,
            dst_ref=out_ref.at[me],
            send_sem=send_sems.at[offset],
            recv_sem=recv_sems.at[offset],
            device_id={"req": peer},
            device_id_type=MESH_IDS,
        )
        copy.start()
        copies.append(copy)
    out_ref[me] = query_ref[...]
    gate_ref[...] = jnp.dot(normed, w_gate_ref[...], preferred_element_type=jnp.float32)
    value_ref[...] = jnp.dot(normed, w_value_ref[...], preferred_element_type=jnp.float32).astype(value_ref.dtype)
    keys = jnp.dot(normed, w_key_ref[...], preferred_element_type=jnp.float32)
    for kv in range(keys.shape[1] // head_width):
        lanes = slice(kv * head_width, (kv + 1) * head_width)
        key = keys[:, lanes]
        key = key * rms_inv(key) * key_gain_ref[...]
        key_ref[:, lanes] = rope(key, cos_ref, sin_ref, swap).astype(key_ref.dtype)
    slots, requests = table_ref.shape
    slot_ids = lax.broadcasted_iota(jnp.int32, (slots, requests), 0)
    lengths = lengths_ref[...]
    local_ids = table_ref[...] - me * pool_pages
    usable = (slot_ids < (lengths + page_size - 1) // page_size) & (local_ids >= 0) & (local_ids < pool_pages)
    keyed = jnp.where(usable, local_ids, pool_pages)
    slot_f = slot_ids.astype(jnp.float32)

    def one_page(page, carry):
        hit = keyed == page
        owned_ref[pl.ds(page, 1), :] = jnp.max(jnp.where(hit, 1.0, 0.0), axis=0, keepdims=True)
        slot_scratch[pl.ds(page, 1), :] = jnp.sum(jnp.where(hit, slot_f, 0.0), axis=0, keepdims=True)
        return carry

    lax.fori_loop(0, pool_pages, one_page, 0)
    owned_requests = owned_ref[...]
    owner_slot = jnp.sum(slot_scratch[...], axis=1, keepdims=True)
    owner_length = jnp.sum(owned_requests * lengths.astype(jnp.float32), axis=1, keepdims=True)
    filled = jnp.clip(owner_length - owner_slot * page_size, 0.0, float(page_size))
    filled = jnp.where(jnp.max(owned_requests, axis=1, keepdims=True) > 0.5, filled, 0.0)
    tokens = lax.broadcasted_iota(jnp.int32, filled_ref.shape, 1).astype(jnp.float32)
    filled_ref[...] = jnp.where(tokens < filled, 1.0, 0.0)
    dealing = (lax.broadcasted_iota(jnp.int32, (requests, requests), 0) == order_ref[...]).astype(jnp.bfloat16)
    owned_rows = jnp.dot(owned_requests.astype(jnp.bfloat16), dealing, preferred_element_type=jnp.float32)
    owned_ref[...] = jnp.where(owned_rows > 0.5, 1.0, 0.0)
    for copy in copies:
        copy.wait()
    rows = query_ref.shape[0]
    page_query_ref[...] = jnp.dot(
        owned_ref[...].astype(jnp.bfloat16),
        out_ref[...].reshape(count * rows, query_ref.shape[1]),
        preferred_element_type=jnp.float32,
    ).astype(page_query_ref.dtype)


def query_exchange(
    hidden, attn_gain, w_query, query_gain, w_gate, w_value, w_key, key_gain, cosine, sine, table, lengths, order,
    pool_pages, page_size, count, ident,
):
    rows = hidden.shape[0]
    requests = table.shape[1]
    return pl.pallas_call(
        functools.partial(query_kernel, count, pool_pages, page_size),
        out_shape=(
            jax.ShapeDtypeStruct((count, rows, w_query.shape[1]), jnp.bfloat16),
            jax.ShapeDtypeStruct((rows, w_query.shape[1]), jnp.bfloat16),
            jax.ShapeDtypeStruct((rows, w_gate.shape[1]), jnp.float32),
            jax.ShapeDtypeStruct((rows, w_value.shape[1]), jnp.bfloat16),
            jax.ShapeDtypeStruct((rows, w_key.shape[1]), jnp.bfloat16),
            jax.ShapeDtypeStruct((pool_pages, requests), jnp.float32),
            jax.ShapeDtypeStruct((pool_pages, page_size), jnp.float32),
            jax.ShapeDtypeStruct((pool_pages, w_query.shape[1]), jnp.bfloat16),
        ),
        in_specs=[pl.BlockSpec(memory_space=pltpu.VMEM)] * 13,
        out_specs=tuple(pl.BlockSpec(memory_space=pltpu.VMEM) for _ in range(8)),
        scratch_shapes=[
            pltpu.VMEM((pool_pages, requests), jnp.float32),
            pltpu.SemaphoreType.DMA((count,)),
            pltpu.SemaphoreType.DMA((count,)),
        ],
        compiler_params=pltpu.CompilerParams(collective_id=ident, has_side_effects=True),
    )(hidden, attn_gain, w_query, query_gain, w_gate, w_value, w_key, key_gain, cosine, sine, table, lengths, order)


def attend_kernel(
    req_count, head_count, group_size, scale_factor, num_ref, stats_ref, query_ref, key_ref, value_ref, gate_ref,
    w_out_ref, hidden_ref, out_ref, got_num, got_stats, projected, summed, send_sems, recv_sems,
):
    req_me, req_peers = peers_of("req", req_count)
    head_me, head_peers = peers_of("head", head_count)
    rows, width = out_ref.shape
    cols = width // head_count
    pairs = stats_ref.shape[1] // 2
    head_width = query_ref.shape[1] // pairs
    mine = pl.ds(pl.multiple_of(head_me * cols, cols), cols)
    greet([("req", peer) for _, peer in req_peers] + [("head", peer) for _, peer in head_peers])
    got_num[req_me] = num_ref[req_me]
    got_stats[req_me] = stats_ref[req_me]
    copies = []
    for offset, peer in req_peers:
        for which, (src_ref, dst_ref) in enumerate(((num_ref, got_num), (stats_ref, got_stats))):
            copy = pltpu.make_async_remote_copy(
                src_ref=src_ref.at[peer],
                dst_ref=dst_ref.at[req_me],
                send_sem=send_sems.at[which, offset],
                recv_sem=recv_sems.at[which, offset],
                device_id={"req": peer},
                device_id_type=MESH_IDS,
            )
            copy.start()
            copies.append(copy)
    for copy in copies:
        copy.wait()
    eye = (
        lax.broadcasted_iota(jnp.int32, (rows, rows), 0) == lax.broadcasted_iota(jnp.int32, (rows, rows), 1)
    ).astype(jnp.float32)
    flip = (((1,), (1,)), ((), ()))
    heads = []
    for pair in range(pairs):
        kv = pair // group_size
        lanes = slice(pair * head_width, (pair + 1) * head_width)
        kv_lanes = slice(kv * head_width, (kv + 1) * head_width)
        shifts = lax.dot_general(
            eye, got_stats[:, pair, :], flip, precision=lax.Precision.HIGHEST, preferred_element_type=jnp.float32
        )
        totals = lax.dot_general(
            eye,
            got_stats[:, pairs + pair, :],
            flip,
            precision=lax.Precision.HIGHEST,
            preferred_element_type=jnp.float32,
        )
        query = query_ref[:, lanes].astype(jnp.float32)
        self_score = jnp.sum(query * key_ref[:, kv_lanes].astype(jnp.float32), axis=1, keepdims=True) * scale_factor
        self_shift = LOG_TWO * jnp.ceil(self_score / LOG_TWO)
        shift = jnp.maximum(jnp.max(shifts, axis=1, keepdims=True), self_shift)
        factor = jnp.exp(shifts - shift)
        self_weight = jnp.exp(self_score - shift)
        total = jnp.sum(totals * factor, axis=1, keepdims=True) + self_weight
        acc = self_weight.astype(jnp.bfloat16).astype(jnp.float32) * value_ref[:, kv_lanes].astype(jnp.float32)
        for source in range(req_count):
            acc = acc + factor[:, source : source + 1] * got_num[source, :, lanes].astype(jnp.float32)
        heads.append(acc / total)
    heads_out = jnp.concatenate(heads, axis=1)
    gate = gate_ref[...]
    attended = (heads_out * (1.0 / (1.0 + jnp.exp(-gate)))).astype(jnp.bfloat16)
    projected[...] = jnp.dot(attended, w_out_ref[...], preferred_element_type=jnp.float32)
    summed[head_me] = projected[:, mine]
    send_all(
        "head", head_peers, lambda peer: projected.at[:, pl.ds(peer * cols, cols)], summed.at[head_me],
        send_sems, recv_sems, 2,
    )
    out_ref[:, mine] = (hidden_ref[:, mine].astype(jnp.float32) + jnp.sum(summed[...], axis=0)).astype(
        out_ref.dtype
    )
    send_all("head", head_peers, lambda peer: out_ref.at[:, mine], out_ref.at[:, mine], send_sems, recv_sems, 3)


def attend_exchange(
    num, stats, queries, keys, values, gate, w_out, hidden, head_count, group_size, scale_factor, ident
):
    req_count = num.shape[0]
    rows, width = hidden.shape
    most = max(head_count, req_count)
    return pl.pallas_call(
        functools.partial(attend_kernel, req_count, head_count, group_size, scale_factor),
        out_shape=jax.ShapeDtypeStruct((rows, width), jnp.bfloat16),
        in_specs=[pl.BlockSpec(memory_space=pltpu.VMEM)] * 8,
        out_specs=pl.BlockSpec(memory_space=pltpu.VMEM),
        scratch_shapes=[
            pltpu.VMEM(num.shape, num.dtype),
            pltpu.VMEM(stats.shape, stats.dtype),
            pltpu.VMEM((rows, width), jnp.float32),
            pltpu.VMEM((head_count, rows, width // head_count), jnp.float32),
            pltpu.SemaphoreType.DMA((4, most)),
            pltpu.SemaphoreType.DMA((4, most)),
        ],
        compiler_params=pltpu.CompilerParams(collective_id=ident, has_side_effects=True),
    )(num, stats, queries, keys, values, gate, w_out, hidden)


def tail_kernel(
    head_count, req_count, mixed_ref, gain_ref, w_gate_ref, w_up_ref, w_down_ref, order_ref, out_ref, parts_ref,
    summed, results, send_sems, recv_sems,
):
    head_me, head_peers = peers_of("head", head_count)
    req_me, req_peers = peers_of("req", req_count)
    rows, width = out_ref.shape
    cols = width // head_count
    mine = pl.ds(pl.multiple_of(head_me * cols, cols), cols)
    barrier = pltpu.get_barrier_semaphore()
    everyone = [("head", peer) for _, peer in head_peers] + [("req", peer) for _, peer in req_peers]
    for axis, peer in everyone:
        pl.semaphore_signal(barrier, inc=1, device_id={axis: peer}, device_id_type=MESH_IDS)
    mixed = mixed_ref[...].astype(jnp.float32)
    normed = (mixed * rms_inv(mixed) * gain_ref[...]).astype(jnp.bfloat16)
    gate_part = jnp.dot(normed, w_gate_ref[...], preferred_element_type=jnp.float32)
    up_part = jnp.dot(normed, w_up_ref[...], preferred_element_type=jnp.float32)
    inner_act = (gate_part / (1.0 + jnp.exp(-gate_part)) * up_part).astype(jnp.bfloat16)
    parts_ref[...] = jnp.dot(inner_act, w_down_ref[...], preferred_element_type=jnp.float32)
    pl.semaphore_wait(barrier, len(everyone))
    summed[head_me] = parts_ref[:, mine]
    send_all(
        "head",
        head_peers,
        lambda peer: parts_ref.at[:, pl.ds(peer * cols, cols)],
        summed.at[head_me],
        send_sems,
        recv_sems,
        0,
    )
    results[req_me] = (mixed_ref[:, mine].astype(jnp.float32) + jnp.sum(summed[...], axis=0)).astype(
        results.dtype
    )
    send_all("req", req_peers, lambda peer: results.at[req_me], results.at[req_me], send_sems, recv_sems, 1)
    wanted = req_me * rows + lax.broadcasted_iota(jnp.int32, (rows, req_count * rows), 0)
    picker = (order_ref[...] == wanted).astype(jnp.bfloat16)
    out_ref[:, mine] = jnp.dot(
        picker, results[...].reshape(req_count * rows, cols), preferred_element_type=jnp.float32
    ).astype(out_ref.dtype)
    send_all("head", head_peers, lambda peer: out_ref.at[:, mine], out_ref.at[:, mine], send_sems, recv_sems, 2)


def tail_exchange(mixed, gain, w_gate, w_up, w_down, order, head_count, req_count, ident):
    rows, width = mixed.shape
    most = max(head_count, req_count)
    return pl.pallas_call(
        functools.partial(tail_kernel, head_count, req_count),
        out_shape=jax.ShapeDtypeStruct((rows, width), jnp.bfloat16),
        in_specs=[pl.BlockSpec(memory_space=pltpu.VMEM)] * 6,
        out_specs=pl.BlockSpec(memory_space=pltpu.VMEM),
        scratch_shapes=[
            pltpu.VMEM((rows, width), jnp.float32),
            pltpu.VMEM((head_count, rows, width // head_count), jnp.float32),
            pltpu.VMEM((req_count, rows, width // head_count), jnp.bfloat16),
            pltpu.SemaphoreType.DMA((3, most)),
            pltpu.SemaphoreType.DMA((3, most)),
        ],
        compiler_params=pltpu.CompilerParams(collective_id=ident, has_side_effects=True),
    )(mixed, gain, w_gate, w_up, w_down, order)


def body(
    req_count,
    head_count,
    hidden,
    deal_order,
    lengths,
    page_table,
    key_cache,
    value_cache,
    attn_gain,
    w_query,
    w_key,
    w_value,
    w_gate,
    w_out,
    query_gain,
    key_gain,
    mlp_gain,
    mlp_gate,
    mlp_up,
    mlp_down,
):
    local_rows, model_width = hidden.shape
    req_index = lax.axis_index("req")
    head_index = lax.axis_index("head")
    all_rows = local_rows * req_count
    head_width = query_gain.shape[0]
    pool_pages, page_size, local_kv = key_cache.shape[:3]
    group_size = w_query.shape[1] // (local_kv * head_width)
    head_cols = local_kv * group_size * head_width
    pairs = local_kv * group_size
    chunk = model_width // head_count
    scale_factor = 1.0 / math.sqrt(head_width)
    first_own = req_index * local_rows

    with jax.named_scope("rotary_tables"):
        own_requests = lax.dynamic_slice_in_dim(deal_order, first_own, local_rows)
        request_ids = jnp.arange(all_rows, dtype=jnp.int32)
        own_pick = own_requests[:, None] == request_ids[None, :]
        position = jnp.sum(jnp.where(own_pick, lengths[None, :], 0), axis=1).astype(jnp.float32)
        half = head_width // 2
        frequency = ROPE_BASE ** (-(jnp.arange(half, dtype=jnp.float32) * (2.0 / head_width)))
        angles = position[:, None] * frequency[None, :]
        cosine = jnp.concatenate([jnp.cos(angles)] * 2, axis=1)
        sine = jnp.concatenate([jnp.sin(angles)] * 2, axis=1)

    outs = query_exchange(
        hidden,
        attn_gain.reshape(1, model_width),
        w_query,
        query_gain.reshape(1, head_width),
        w_gate,
        w_value,
        w_key,
        key_gain.reshape(1, head_width),
        cosine,
        sine,
        page_table.T,
        lengths.reshape(1, all_rows),
        deal_order.reshape(1, all_rows),
        pool_pages,
        page_size,
        req_count,
        0,
    )
    _, own_queries, gate_logits, new_values, new_keys, owned_f, live_tokens, page_queries = outs
    owned = owned_f > 0.5
    page_queries = page_queries.reshape(pool_pages, local_kv, group_size, head_width)
    new_values = new_values.reshape(local_rows, local_kv, head_width)
    new_keys = new_keys.reshape(local_rows, local_kv, head_width)

    with jax.named_scope("page_attention"):
        scores = (
            jnp.einsum("pkgd,ptkd->pkgt", page_queries, key_cache, preferred_element_type=jnp.float32)
            * scale_factor
        )
        live_mask = live_tokens[:, None, None, :] > 0.5
        scores = jnp.where(live_mask, scores, LOW_SCORE)
        page_peaks = jnp.max(scores, axis=-1)
        owned_b = owned[:, :, None, None]
        row_peaks = jnp.max(jnp.where(owned_b, page_peaks[:, None], LOW_SCORE), axis=0)
        row_shift = LOG_TWO * jnp.ceil(row_peaks / LOG_TWO)
        page_shift = jnp.max(jnp.where(owned_b, row_shift[None], LOW_SCORE), axis=1)
        weights = jnp.where(live_mask, jnp.exp(scores - page_shift[..., None]), 0.0)
        page_totals = jnp.sum(weights, axis=-1)
        page_numerators = jnp.einsum(
            "pkgt,ptkd->pkgd",
            weights.astype(jnp.bfloat16),
            value_cache,
            preferred_element_type=jnp.float32,
        )
        row_totals = jnp.sum(jnp.where(owned_b, page_totals[:, None], 0.0), axis=0).reshape(all_rows, pairs)
        row_numerators = jnp.dot(
            owned_f.T.astype(jnp.bfloat16),
            page_numerators.reshape(pool_pages, head_cols).astype(jnp.bfloat16),
            preferred_element_type=jnp.float32,
        )
        numerator_message = row_numerators.astype(jnp.bfloat16).reshape(req_count, local_rows, head_cols)
        stats_message = jnp.concatenate(
            [row_shift.reshape(req_count, local_rows, pairs), row_totals.reshape(req_count, local_rows, pairs)],
            axis=2,
        ).transpose(0, 2, 1)

    mixed_rows = attend_exchange(
        numerator_message,
        stats_message,
        own_queries,
        new_keys.reshape(local_rows, local_kv * head_width),
        new_values.reshape(local_rows, local_kv * head_width),
        gate_logits,
        w_out,
        hidden,
        head_count,
        group_size,
        scale_factor,
        1,
    )

    return tail_exchange(
        mixed_rows,
        mlp_gain.reshape(1, model_width),
        mlp_gate,
        mlp_up,
        mlp_down,
        deal_order.reshape(1, all_rows),
        head_count,
        req_count,
        3,
    )


def solution(mesh):
    return jax.shard_map(
        functools.partial(body, mesh.shape["req"], mesh.shape["head"]),
        mesh=mesh,
        in_specs=(
            P("req", None),
            P(),
            P(),
            P(),
            P("req", None, "head", None),
            P("req", None, "head", None),
            P(),
            P(None, "head"),
            P(None, "head"),
            P(None, "head"),
            P(None, "head"),
            P("head", None),
            P(),
            P(),
            P(),
            P(None, "head"),
            P(None, "head"),
            P("head", None),
        ),
        out_specs=P("req", None),
        check_vma=False,
    )
```

```python
import functools
import math

import jax
import jax.numpy as jnp
from jax import lax
from jax.experimental import pallas as pl
from jax.experimental.pallas import tpu as pltpu
from jax.sharding import PartitionSpec as P

EPSILON = 1e-06
ROPE_BASE = 1000000.0
LOW_SCORE = -1e30
LOG_TWO = math.log(2.0)
MESH_IDS = pl.DeviceIdType.MESH


def rms_inv(values):
    return lax.rsqrt(jnp.mean(values * values, axis=-1, keepdims=True) + EPSILON)


def rotate(values, position):
    half_dim = values.shape[-1] // 2
    exponent = jnp.arange(half_dim, dtype=jnp.float32) * (2.0 / values.shape[-1])
    frequency = ROPE_BASE ** (-exponent)
    angles = position[:, None] * frequency[None, :]
    ones_tail = (1,) * (values.ndim - 2)
    angles = angles.reshape((angles.shape[0],) + ones_tail + (half_dim,))
    cosine = jnp.cos(angles)
    sine_vals = jnp.sin(angles)
    front_half = values[..., :half_dim]
    back_half = values[..., half_dim:]
    return jnp.concatenate(
        [front_half * cosine - back_half * sine_vals, back_half * cosine + front_half * sine_vals],
        axis=-1,
    )


def norm_rotate(values, gain_vec, position):
    return rotate(values * rms_inv(values) * gain_vec, position)


def exchange_kernel(axis, count, spreads, *refs):
    arrays = len(spreads)
    sources, outputs = refs[:arrays], refs[arrays : 2 * arrays]
    send_sems, recv_sems = refs[2 * arrays], refs[2 * arrays + 1]
    me = lax.axis_index(axis)
    barrier = pltpu.get_barrier_semaphore()
    for offset in range(1, count):
        peer = lax.rem(me + offset, count)
        pl.semaphore_signal(barrier, inc=1, device_id={axis: peer}, device_id_type=MESH_IDS)
    pl.semaphore_wait(barrier, count - 1)
    copies = []
    for offset in range(1, count):
        peer = lax.rem(me + offset, count)
        for which in range(arrays):
            src_ref, out_ref = sources[which], outputs[which]
            copy = pltpu.make_async_remote_copy(
                src_ref=src_ref.at[peer] if spreads[which] else src_ref,
                dst_ref=out_ref.at[me],
                send_sem=send_sems.at[which, offset],
                recv_sem=recv_sems.at[which, offset],
                device_id={axis: peer},
                device_id_type=MESH_IDS,
            )
            copy.start()
            copies.append(copy)
    for which in range(arrays):
        src_ref, out_ref = sources[which], outputs[which]
        out_ref[me] = src_ref[me] if spreads[which] else src_ref[...]
    for copy in copies:
        copy.wait()


def exchange_many(arrays, spreads, axis, count, ident):
    shapes = []
    for values, spread in zip(arrays, spreads):
        block = values.shape[1:] if spread else values.shape
        shapes.append(jax.ShapeDtypeStruct((count,) + tuple(block), values.dtype))
    return pl.pallas_call(
        functools.partial(exchange_kernel, axis, count, tuple(spreads)),
        out_shape=tuple(shapes),
        in_specs=[pl.BlockSpec(memory_space=pltpu.VMEM)] * len(arrays),
        out_specs=tuple(pl.BlockSpec(memory_space=pltpu.VMEM) for _ in arrays),
        scratch_shapes=[
            pltpu.SemaphoreType.DMA((len(arrays), count)),
            pltpu.SemaphoreType.DMA((len(arrays), count)),
        ],
        compiler_params=pltpu.CompilerParams(collective_id=ident, has_side_effects=True),
    )(*arrays)


def exchange(values, axis, count, spread, ident):
    return exchange_many((values,), (spread,), axis, count, ident)[0]


def greet(peers):
    barrier = pltpu.get_barrier_semaphore()
    for axis, peer in peers:
        pl.semaphore_signal(barrier, inc=1, device_id={axis: peer}, device_id_type=MESH_IDS)
    pl.semaphore_wait(barrier, len(peers))


def peers_of(axis, count):
    me = lax.axis_index(axis)
    return me, [(offset, lax.rem(me + offset, count)) for offset in range(1, count)]


def send_all(axis, peers, src_of, dst, send_sems, recv_sems, phase):
    copies = []
    for offset, peer in peers:
        copy = pltpu.make_async_remote_copy(
            src_ref=src_of(peer),
            dst_ref=dst,
            send_sem=send_sems.at[phase, offset],
            recv_sem=recv_sems.at[phase, offset],
            device_id={axis: peer},
            device_id_type=MESH_IDS,
        )
        copy.start()
        copies.append(copy)
    for copy in copies:
        copy.wait()


def residual_kernel(count, parts_ref, hidden_ref, out_ref, summed, send_sems, recv_sems):
    me, peers = peers_of("head", count)
    cols = out_ref.shape[1] // count
    mine = pl.ds(pl.multiple_of(me * cols, cols), cols)
    greet([("head", peer) for _, peer in peers])
    summed[me] = parts_ref[:, mine]
    send_all(
        "head", peers, lambda peer: parts_ref.at[:, pl.ds(peer * cols, cols)], summed.at[me], send_sems, recv_sems, 0
    )
    out_ref[:, mine] = (hidden_ref[:, mine].astype(jnp.float32) + jnp.sum(summed[...], axis=0)).astype(
        out_ref.dtype
    )
    send_all("head", peers, lambda peer: out_ref.at[:, mine], out_ref.at[:, mine], send_sems, recv_sems, 1)


def residual_exchange(parts, hidden, count, ident):
    rows, width = parts.shape
    return pl.pallas_call(
        functools.partial(residual_kernel, count),
        out_shape=jax.ShapeDtypeStruct((rows, width), jnp.bfloat16),
        in_specs=[pl.BlockSpec(memory_space=pltpu.VMEM)] * 2,
        out_specs=pl.BlockSpec(memory_space=pltpu.VMEM),
        scratch_shapes=[
            pltpu.VMEM((count, rows, width // count), jnp.float32),
            pltpu.SemaphoreType.DMA((2, count)),
            pltpu.SemaphoreType.DMA((2, count)),
        ],
        compiler_params=pltpu.CompilerParams(collective_id=ident, has_side_effects=True),
    )(parts, hidden)


def rope(values, cos_ref, sin_ref, swap):
    swapped = jnp.dot(values, swap, precision=lax.Precision.HIGHEST, preferred_element_type=jnp.float32)
    return values * cos_ref[...] + swapped * sin_ref[...]


def query_kernel(
    count, pool_pages, page_size, hidden_ref, attn_gain_ref, w_query_ref, query_gain_ref, w_gate_ref, w_value_ref,
    w_key_ref, key_gain_ref, cos_ref, sin_ref, table_ref, lengths_ref, order_ref, out_ref, query_ref, gate_ref,
    value_ref, key_ref, owned_ref, filled_ref, page_query_ref, slot_scratch, send_sems, recv_sems,
):
    me, peers = peers_of("req", count)
    barrier = pltpu.get_barrier_semaphore()
    for _, peer in peers:
        pl.semaphore_signal(barrier, inc=1, device_id={"req": peer}, device_id_type=MESH_IDS)
    head_width = cos_ref.shape[1]
    lanes_in = lax.broadcasted_iota(jnp.int32, (head_width, head_width), 0)
    lanes_out = lax.broadcasted_iota(jnp.int32, (head_width, head_width), 1)
    swap = jnp.where(
        lanes_in == lax.rem(lanes_out + head_width // 2, head_width),
        jnp.where(lanes_out < head_width // 2, -1.0, 1.0),
        0.0,
    ).astype(jnp.float32)
    hidden = hidden_ref[...].astype(jnp.float32)
    normed = (hidden * rms_inv(hidden) * attn_gain_ref[...]).astype(jnp.bfloat16)
    queries = jnp.dot(normed, w_query_ref[...], preferred_element_type=jnp.float32)
    for pair in range(queries.shape[1] // head_width):
        lanes = slice(pair * head_width, (pair + 1) * head_width)
        query = queries[:, lanes]
        query = query * rms_inv(query) * query_gain_ref[...]
        query_ref[:, lanes] = rope(query, cos_ref, sin_ref, swap).astype(query_ref.dtype)
    pl.semaphore_wait(barrier, len(peers))
    copies = []
    for offset, peer in peers:
        copy = pltpu.make_async_remote_copy(
            src_ref=query_ref,
            dst_ref=out_ref.at[me],
            send_sem=send_sems.at[offset],
            recv_sem=recv_sems.at[offset],
            device_id={"req": peer},
            device_id_type=MESH_IDS,
        )
        copy.start()
        copies.append(copy)
    out_ref[me] = query_ref[...]
    gate_ref[...] = jnp.dot(normed, w_gate_ref[...], preferred_element_type=jnp.float32)
    value_ref[...] = jnp.dot(normed, w_value_ref[...], preferred_element_type=jnp.float32).astype(value_ref.dtype)
    keys = jnp.dot(normed, w_key_ref[...], preferred_element_type=jnp.float32)
    for kv in range(keys.shape[1] // head_width):
        lanes = slice(kv * head_width, (kv + 1) * head_width)
        key = keys[:, lanes]
        key = key * rms_inv(key) * key_gain_ref[...]
        key_ref[:, lanes] = rope(key, cos_ref, sin_ref, swap).astype(key_ref.dtype)
    slots, requests = table_ref.shape
    slot_ids = lax.broadcasted_iota(jnp.int32, (slots, requests), 0)
    lengths = lengths_ref[...]
    local_ids = table_ref[...] - me * pool_pages
    usable = (slot_ids < (lengths + page_size - 1) // page_size) & (local_ids >= 0) & (local_ids < pool_pages)
    keyed = jnp.where(usable, local_ids, pool_pages)
    slot_f = slot_ids.astype(jnp.float32)

    def one_page(page, carry):
        hit = keyed == page
        owned_ref[pl.ds(page, 1), :] = jnp.max(jnp.where(hit, 1.0, 0.0), axis=0, keepdims=True)
        slot_scratch[pl.ds(page, 1), :] = jnp.sum(jnp.where(hit, slot_f, 0.0), axis=0, keepdims=True)
        return carry

    lax.fori_loop(0, pool_pages, one_page, 0)
    owned_requests = owned_ref[...]
    owner_slot = jnp.sum(slot_scratch[...], axis=1, keepdims=True)
    owner_length = jnp.sum(owned_requests * lengths.astype(jnp.float32), axis=1, keepdims=True)
    filled = jnp.clip(owner_length - owner_slot * page_size, 0.0, float(page_size))
    filled = jnp.where(jnp.max(owned_requests, axis=1, keepdims=True) > 0.5, filled, 0.0)
    tokens = lax.broadcasted_iota(jnp.int32, filled_ref.shape, 1).astype(jnp.float32)
    filled_ref[...] = jnp.where(tokens < filled, 1.0, 0.0)
    dealing = (lax.broadcasted_iota(jnp.int32, (requests, requests), 0) == order_ref[...]).astype(jnp.bfloat16)
    owned_rows = jnp.dot(owned_requests.astype(jnp.bfloat16), dealing, preferred_element_type=jnp.float32)
    owned_ref[...] = jnp.where(owned_rows > 0.5, 1.0, 0.0)
    for copy in copies:
        copy.wait()
    rows = query_ref.shape[0]
    page_query_ref[...] = jnp.dot(
        owned_ref[...].astype(jnp.bfloat16),
        out_ref[...].reshape(count * rows, query_ref.shape[1]),
        preferred_element_type=jnp.float32,
    ).astype(page_query_ref.dtype)


def query_exchange(
    hidden, attn_gain, w_query, query_gain, w_gate, w_value, w_key, key_gain, cosine, sine, table, lengths, order,
    pool_pages, page_size, count, ident,
):
    rows = hidden.shape[0]
    requests = table.shape[1]
    return pl.pallas_call(
        functools.partial(query_kernel, count, pool_pages, page_size),
        out_shape=(
            jax.ShapeDtypeStruct((count, rows, w_query.shape[1]), jnp.bfloat16),
            jax.ShapeDtypeStruct((rows, w_query.shape[1]), jnp.bfloat16),
            jax.ShapeDtypeStruct((rows, w_gate.shape[1]), jnp.float32),
            jax.ShapeDtypeStruct((rows, w_value.shape[1]), jnp.bfloat16),
            jax.ShapeDtypeStruct((rows, w_key.shape[1]), jnp.bfloat16),
            jax.ShapeDtypeStruct((pool_pages, requests), jnp.float32),
            jax.ShapeDtypeStruct((pool_pages, page_size), jnp.float32),
            jax.ShapeDtypeStruct((pool_pages, w_query.shape[1]), jnp.bfloat16),
        ),
        in_specs=[pl.BlockSpec(memory_space=pltpu.VMEM)] * 13,
        out_specs=tuple(pl.BlockSpec(memory_space=pltpu.VMEM) for _ in range(8)),
        scratch_shapes=[
            pltpu.VMEM((pool_pages, requests), jnp.float32),
            pltpu.SemaphoreType.DMA((count,)),
            pltpu.SemaphoreType.DMA((count,)),
        ],
        compiler_params=pltpu.CompilerParams(collective_id=ident, has_side_effects=True),
    )(hidden, attn_gain, w_query, query_gain, w_gate, w_value, w_key, key_gain, cosine, sine, table, lengths, order)


def attend_kernel(
    req_count, head_count, group_size, scale_factor, num_ref, stats_ref, query_ref, key_ref, value_ref, gate_ref,
    w_out_ref, hidden_ref, out_ref, got_num, got_stats, projected, summed, send_sems, recv_sems,
):
    req_me, req_peers = peers_of("req", req_count)
    head_me, head_peers = peers_of("head", head_count)
    rows, width = out_ref.shape
    cols = width // head_count
    pairs = stats_ref.shape[1] // 2
    head_width = query_ref.shape[1] // pairs
    mine = pl.ds(pl.multiple_of(head_me * cols, cols), cols)
    greet([("req", peer) for _, peer in req_peers] + [("head", peer) for _, peer in head_peers])
    got_num[req_me] = num_ref[req_me]
    got_stats[req_me] = stats_ref[req_me]
    copies = []
    for offset, peer in req_peers:
        for which, (src_ref, dst_ref) in enumerate(((num_ref, got_num), (stats_ref, got_stats))):
            copy = pltpu.make_async_remote_copy(
                src_ref=src_ref.at[peer],
                dst_ref=dst_ref.at[req_me],
                send_sem=send_sems.at[which, offset],
                recv_sem=recv_sems.at[which, offset],
                device_id={"req": peer},
                device_id_type=MESH_IDS,
            )
            copy.start()
            copies.append(copy)
    for copy in copies:
        copy.wait()
    eye = (
        lax.broadcasted_iota(jnp.int32, (rows, rows), 0) == lax.broadcasted_iota(jnp.int32, (rows, rows), 1)
    ).astype(jnp.float32)
    flip = (((1,), (1,)), ((), ()))
    heads = []
    for pair in range(pairs):
        kv = pair // group_size
        lanes = slice(pair * head_width, (pair + 1) * head_width)
        kv_lanes = slice(kv * head_width, (kv + 1) * head_width)
        shifts = lax.dot_general(
            eye, got_stats[:, pair, :], flip, precision=lax.Precision.HIGHEST, preferred_element_type=jnp.float32
        )
        totals = lax.dot_general(
            eye,
            got_stats[:, pairs + pair, :],
            flip,
            precision=lax.Precision.HIGHEST,
            preferred_element_type=jnp.float32,
        )
        query = query_ref[:, lanes].astype(jnp.float32)
        self_score = jnp.sum(query * key_ref[:, kv_lanes].astype(jnp.float32), axis=1, keepdims=True) * scale_factor
        self_shift = LOG_TWO * jnp.ceil(self_score / LOG_TWO)
        shift = jnp.maximum(jnp.max(shifts, axis=1, keepdims=True), self_shift)
        factor = jnp.exp(shifts - shift)
        self_weight = jnp.exp(self_score - shift)
        total = jnp.sum(totals * factor, axis=1, keepdims=True) + self_weight
        acc = self_weight.astype(jnp.bfloat16).astype(jnp.float32) * value_ref[:, kv_lanes].astype(jnp.float32)
        for source in range(req_count):
            acc = acc + factor[:, source : source + 1] * got_num[source, :, lanes].astype(jnp.float32)
        heads.append(acc / total)
    heads_out = jnp.concatenate(heads, axis=1)
    gate = gate_ref[...]
    attended = (heads_out * (1.0 / (1.0 + jnp.exp(-gate)))).astype(jnp.bfloat16)
    projected[...] = jnp.dot(attended, w_out_ref[...], preferred_element_type=jnp.float32)
    summed[head_me] = projected[:, mine]
    send_all(
        "head", head_peers, lambda peer: projected.at[:, pl.ds(peer * cols, cols)], summed.at[head_me],
        send_sems, recv_sems, 2,
    )
    out_ref[:, mine] = (hidden_ref[:, mine].astype(jnp.float32) + jnp.sum(summed[...], axis=0)).astype(
        out_ref.dtype
    )
    send_all("head", head_peers, lambda peer: out_ref.at[:, mine], out_ref.at[:, mine], send_sems, recv_sems, 3)


def attend_exchange(
    num, stats, queries, keys, values, gate, w_out, hidden, head_count, group_size, scale_factor, ident
):
    req_count = num.shape[0]
    rows, width = hidden.shape
    most = max(head_count, req_count)
    return pl.pallas_call(
        functools.partial(attend_kernel, req_count, head_count, group_size, scale_factor),
        out_shape=jax.ShapeDtypeStruct((rows, width), jnp.bfloat16),
        in_specs=[pl.BlockSpec(memory_space=pltpu.VMEM)] * 8,
        out_specs=pl.BlockSpec(memory_space=pltpu.VMEM),
        scratch_shapes=[
            pltpu.VMEM(num.shape, num.dtype),
            pltpu.VMEM(stats.shape, stats.dtype),
            pltpu.VMEM((rows, width), jnp.float32),
            pltpu.VMEM((head_count, rows, width // head_count), jnp.float32),
            pltpu.SemaphoreType.DMA((4, most)),
            pltpu.SemaphoreType.DMA((4, most)),
        ],
        compiler_params=pltpu.CompilerParams(collective_id=ident, has_side_effects=True),
    )(num, stats, queries, keys, values, gate, w_out, hidden)


def tail_kernel(
    head_count, req_count, mixed_ref, gain_ref, w_gate_ref, w_up_ref, w_down_ref, order_ref, out_ref, parts_ref,
    summed, results, send_sems, recv_sems,
):
    head_me, head_peers = peers_of("head", head_count)
    req_me, req_peers = peers_of("req", req_count)
    rows, width = out_ref.shape
    cols = width // head_count
    mine = pl.ds(pl.multiple_of(head_me * cols, cols), cols)
    barrier = pltpu.get_barrier_semaphore()
    everyone = [("head", peer) for _, peer in head_peers] + [("req", peer) for _, peer in req_peers]
    for axis, peer in everyone:
        pl.semaphore_signal(barrier, inc=1, device_id={axis: peer}, device_id_type=MESH_IDS)
    mixed = mixed_ref[...].astype(jnp.float32)
    normed = (mixed * rms_inv(mixed) * gain_ref[...]).astype(jnp.bfloat16)
    gate_part = jnp.dot(normed, w_gate_ref[...], preferred_element_type=jnp.float32)
    up_part = jnp.dot(normed, w_up_ref[...], preferred_element_type=jnp.float32)
    inner_act = (gate_part / (1.0 + jnp.exp(-gate_part)) * up_part).astype(jnp.bfloat16)
    parts_ref[...] = jnp.dot(inner_act, w_down_ref[...], preferred_element_type=jnp.float32)
    pl.semaphore_wait(barrier, len(everyone))
    summed[head_me] = parts_ref[:, mine]
    send_all(
        "head",
        head_peers,
        lambda peer: parts_ref.at[:, pl.ds(peer * cols, cols)],
        summed.at[head_me],
        send_sems,
        recv_sems,
        0,
    )
    results[req_me] = (mixed_ref[:, mine].astype(jnp.float32) + jnp.sum(summed[...], axis=0)).astype(
        results.dtype
    )
    send_all("req", req_peers, lambda peer: results.at[req_me], results.at[req_me], send_sems, recv_sems, 1)
    wanted = req_me * rows + lax.broadcasted_iota(jnp.int32, (rows, req_count * rows), 0)
    picker = (order_ref[...] == wanted).astype(jnp.bfloat16)
    out_ref[:, mine] = jnp.dot(
        picker, results[...].reshape(req_count * rows, cols), preferred_element_type=jnp.float32
    ).astype(out_ref.dtype)
    send_all("head", head_peers, lambda peer: out_ref.at[:, mine], out_ref.at[:, mine], send_sems, recv_sems, 2)


def tail_exchange(mixed, gain, w_gate, w_up, w_down, order, head_count, req_count, ident):
    rows, width = mixed.shape
    most = max(head_count, req_count)
    return pl.pallas_call(
        functools.partial(tail_kernel, head_count, req_count),
        out_shape=jax.ShapeDtypeStruct((rows, width), jnp.bfloat16),
        in_specs=[pl.BlockSpec(memory_space=pltpu.VMEM)] * 6,
        out_specs=pl.BlockSpec(memory_space=pltpu.VMEM),
        scratch_shapes=[
            pltpu.VMEM((rows, width), jnp.float32),
            pltpu.VMEM((head_count, rows, width // head_count), jnp.float32),
            pltpu.VMEM((req_count, rows, width // head_count), jnp.bfloat16),
            pltpu.SemaphoreType.DMA((3, most)),
            pltpu.SemaphoreType.DMA((3, most)),
        ],
        compiler_params=pltpu.CompilerParams(collective_id=ident, has_side_effects=True),
    )(mixed, gain, w_gate, w_up, w_down, order)


def body(
    req_count,
    head_count,
    hidden,
    deal_order,
    lengths,
    page_table,
    key_cache,
    value_cache,
    attn_gain,
    w_query,
    w_key,
    w_value,
    w_gate,
    w_out,
    query_gain,
    key_gain,
    mlp_gain,
    mlp_gate,
    mlp_up,
    mlp_down,
):
    local_rows, model_width = hidden.shape
    req_index = lax.axis_index("req")
    head_index = lax.axis_index("head")
    all_rows = local_rows * req_count
    head_width = query_gain.shape[0]
    pool_pages, page_size, local_kv = key_cache.shape[:3]
    group_size = w_query.shape[1] // (local_kv * head_width)
    head_cols = local_kv * group_size * head_width
    pairs = local_kv * group_size
    chunk = model_width // head_count
    scale_factor = 1.0 / math.sqrt(head_width)
    first_own = req_index * local_rows

    with jax.named_scope("rotary_tables"):
        request_ids = jnp.arange(all_rows, dtype=jnp.int32)
        own_rows = first_own + jnp.arange(local_rows, dtype=jnp.int32)
        own_requests = jnp.sum(jnp.where(own_rows[:, None] == request_ids[None, :], deal_order[None, :], 0), axis=1)
        own_pick = own_requests[:, None] == request_ids[None, :]
        position = jnp.sum(jnp.where(own_pick, lengths[None, :], 0), axis=1).astype(jnp.float32)
        half = head_width // 2
        lane_ids = jnp.arange(head_width, dtype=jnp.int32) % half
        frequency = ROPE_BASE ** (-(lane_ids.astype(jnp.float32) * (2.0 / head_width)))
        angles = position[:, None] * frequency[None, :]
        cosine = jnp.cos(angles)
        sine = jnp.sin(angles)

    outs = query_exchange(
        hidden,
        attn_gain.reshape(1, model_width),
        w_query,
        query_gain.reshape(1, head_width),
        w_gate,
        w_value,
        w_key,
        key_gain.reshape(1, head_width),
        cosine,
        sine,
        page_table.T,
        lengths.reshape(1, all_rows),
        deal_order.reshape(1, all_rows),
        pool_pages,
        page_size,
        req_count,
        0,
    )
    _, own_queries, gate_logits, new_values, new_keys, owned_f, live_tokens, page_queries = outs
    owned = owned_f > 0.5
    page_queries = page_queries.reshape(pool_pages, local_kv, group_size, head_width)
    new_values = new_values.reshape(local_rows, local_kv, head_width)
    new_keys = new_keys.reshape(local_rows, local_kv, head_width)

    with jax.named_scope("page_attention"):
        scores = (
            jnp.einsum("pkgd,ptkd->pkgt", page_queries, key_cache, preferred_element_type=jnp.float32)
            * scale_factor
        )
        live_mask = live_tokens[:, None, None, :] > 0.5
        scores = jnp.where(live_mask, scores, LOW_SCORE)
        page_peaks = jnp.max(scores, axis=-1)
        owned_b = owned[:, :, None, None]
        row_peaks = jnp.max(jnp.where(owned_b, page_peaks[:, None], LOW_SCORE), axis=0)
        row_shift = LOG_TWO * jnp.ceil(row_peaks / LOG_TWO)
        page_shift = jnp.max(jnp.where(owned_b, row_shift[None], LOW_SCORE), axis=1)
        weights = jnp.where(live_mask, jnp.exp(scores - page_shift[..., None]), 0.0)
        page_totals = jnp.sum(weights, axis=-1)
        page_numerators = jnp.einsum(
            "pkgt,ptkd->pkgd",
            weights.astype(jnp.bfloat16),
            value_cache,
            preferred_element_type=jnp.float32,
        )
        row_totals = jnp.sum(jnp.where(owned_b, page_totals[:, None], 0.0), axis=0).reshape(all_rows, pairs)
        row_numerators = jnp.dot(
            owned_f.T.astype(jnp.bfloat16),
            page_numerators.reshape(pool_pages, head_cols).astype(jnp.bfloat16),
            preferred_element_type=jnp.float32,
        )
        numerator_message = row_numerators.astype(jnp.bfloat16).reshape(req_count, local_rows, head_cols)
        stats_message = jnp.concatenate(
            [row_shift.reshape(req_count, local_rows, pairs), row_totals.reshape(req_count, local_rows, pairs)],
            axis=2,
        ).transpose(0, 2, 1)

    mixed_rows = attend_exchange(
        numerator_message,
        stats_message,
        own_queries,
        new_keys.reshape(local_rows, local_kv * head_width),
        new_values.reshape(local_rows, local_kv * head_width),
        gate_logits,
        w_out,
        hidden,
        head_count,
        group_size,
        scale_factor,
        1,
    )

    return tail_exchange(
        mixed_rows,
        mlp_gain.reshape(1, model_width),
        mlp_gate,
        mlp_up,
        mlp_down,
        deal_order.reshape(1, all_rows),
        head_count,
        req_count,
        3,
    )


def solution(mesh):
    return jax.shard_map(
        functools.partial(body, mesh.shape["req"], mesh.shape["head"]),
        mesh=mesh,
        in_specs=(
            P("req", None),
            P(),
            P(),
            P(),
            P("req", None, "head", None),
            P("req", None, "head", None),
            P(),
            P(None, "head"),
            P(None, "head"),
            P(None, "head"),
            P(None, "head"),
            P("head", None),
            P(),
            P(),
            P(),
            P(None, "head"),
            P(None, "head"),
            P("head", None),
        ),
        out_specs=P("req", None),
        check_vma=False,
    )
```

```python
import functools
import math

import jax
import jax.numpy as jnp
from jax import lax
from jax.experimental import pallas as pl
from jax.experimental.pallas import tpu as pltpu
from jax.sharding import PartitionSpec as P

EPSILON = 1e-06
ROPE_BASE = 1000000.0
LOW_SCORE = -1e30
LOG_TWO = math.log(2.0)
MESH_IDS = pl.DeviceIdType.MESH


def rms_inv(values):
    return lax.rsqrt(jnp.mean(values * values, axis=-1, keepdims=True) + EPSILON)


def rotate(values, position):
    half_dim = values.shape[-1] // 2
    exponent = jnp.arange(half_dim, dtype=jnp.float32) * (2.0 / values.shape[-1])
    frequency = ROPE_BASE ** (-exponent)
    angles = position[:, None] * frequency[None, :]
    ones_tail = (1,) * (values.ndim - 2)
    angles = angles.reshape((angles.shape[0],) + ones_tail + (half_dim,))
    cosine = jnp.cos(angles)
    sine_vals = jnp.sin(angles)
    front_half = values[..., :half_dim]
    back_half = values[..., half_dim:]
    return jnp.concatenate(
        [front_half * cosine - back_half * sine_vals, back_half * cosine + front_half * sine_vals],
        axis=-1,
    )


def norm_rotate(values, gain_vec, position):
    return rotate(values * rms_inv(values) * gain_vec, position)


def exchange_kernel(axis, count, spreads, *refs):
    arrays = len(spreads)
    sources, outputs = refs[:arrays], refs[arrays : 2 * arrays]
    send_sems, recv_sems = refs[2 * arrays], refs[2 * arrays + 1]
    me = lax.axis_index(axis)
    barrier = pltpu.get_barrier_semaphore()
    for offset in range(1, count):
        peer = lax.rem(me + offset, count)
        pl.semaphore_signal(barrier, inc=1, device_id={axis: peer}, device_id_type=MESH_IDS)
    pl.semaphore_wait(barrier, count - 1)
    copies = []
    for offset in range(1, count):
        peer = lax.rem(me + offset, count)
        for which in range(arrays):
            src_ref, out_ref = sources[which], outputs[which]
            copy = pltpu.make_async_remote_copy(
                src_ref=src_ref.at[peer] if spreads[which] else src_ref,
                dst_ref=out_ref.at[me],
                send_sem=send_sems.at[which, offset],
                recv_sem=recv_sems.at[which, offset],
                device_id={axis: peer},
                device_id_type=MESH_IDS,
            )
            copy.start()
            copies.append(copy)
    for which in range(arrays):
        src_ref, out_ref = sources[which], outputs[which]
        out_ref[me] = src_ref[me] if spreads[which] else src_ref[...]
    for copy in copies:
        copy.wait()


def exchange_many(arrays, spreads, axis, count, ident):
    shapes = []
    for values, spread in zip(arrays, spreads):
        block = values.shape[1:] if spread else values.shape
        shapes.append(jax.ShapeDtypeStruct((count,) + tuple(block), values.dtype))
    return pl.pallas_call(
        functools.partial(exchange_kernel, axis, count, tuple(spreads)),
        out_shape=tuple(shapes),
        in_specs=[pl.BlockSpec(memory_space=pltpu.VMEM)] * len(arrays),
        out_specs=tuple(pl.BlockSpec(memory_space=pltpu.VMEM) for _ in arrays),
        scratch_shapes=[
            pltpu.SemaphoreType.DMA((len(arrays), count)),
            pltpu.SemaphoreType.DMA((len(arrays), count)),
        ],
        compiler_params=pltpu.CompilerParams(collective_id=ident, has_side_effects=True),
    )(*arrays)


def exchange(values, axis, count, spread, ident):
    return exchange_many((values,), (spread,), axis, count, ident)[0]


def greet(peers):
    barrier = pltpu.get_barrier_semaphore()
    for axis, peer in peers:
        pl.semaphore_signal(barrier, inc=1, device_id={axis: peer}, device_id_type=MESH_IDS)
    pl.semaphore_wait(barrier, len(peers))


def peers_of(axis, count):
    me = lax.axis_index(axis)
    return me, [(offset, lax.rem(me + offset, count)) for offset in range(1, count)]


def send_all(axis, peers, src_of, dst, send_sems, recv_sems, phase):
    copies = []
    for offset, peer in peers:
        copy = pltpu.make_async_remote_copy(
            src_ref=src_of(peer),
            dst_ref=dst,
            send_sem=send_sems.at[phase, offset],
            recv_sem=recv_sems.at[phase, offset],
            device_id={axis: peer},
            device_id_type=MESH_IDS,
        )
        copy.start()
        copies.append(copy)
    for copy in copies:
        copy.wait()


def residual_kernel(count, parts_ref, hidden_ref, out_ref, summed, send_sems, recv_sems):
    me, peers = peers_of("head", count)
    cols = out_ref.shape[1] // count
    mine = pl.ds(pl.multiple_of(me * cols, cols), cols)
    greet([("head", peer) for _, peer in peers])
    summed[me] = parts_ref[:, mine]
    send_all(
        "head", peers, lambda peer: parts_ref.at[:, pl.ds(peer * cols, cols)], summed.at[me], send_sems, recv_sems, 0
    )
    out_ref[:, mine] = (hidden_ref[:, mine].astype(jnp.float32) + jnp.sum(summed[...], axis=0)).astype(
        out_ref.dtype
    )
    send_all("head", peers, lambda peer: out_ref.at[:, mine], out_ref.at[:, mine], send_sems, recv_sems, 1)


def residual_exchange(parts, hidden, count, ident):
    rows, width = parts.shape
    return pl.pallas_call(
        functools.partial(residual_kernel, count),
        out_shape=jax.ShapeDtypeStruct((rows, width), jnp.bfloat16),
        in_specs=[pl.BlockSpec(memory_space=pltpu.VMEM)] * 2,
        out_specs=pl.BlockSpec(memory_space=pltpu.VMEM),
        scratch_shapes=[
            pltpu.VMEM((count, rows, width // count), jnp.float32),
            pltpu.SemaphoreType.DMA((2, count)),
            pltpu.SemaphoreType.DMA((2, count)),
        ],
        compiler_params=pltpu.CompilerParams(collective_id=ident, has_side_effects=True),
    )(parts, hidden)


def rope(values, cosine, sine, swap):
    swapped = jnp.dot(values, swap, precision=lax.Precision.HIGHEST, preferred_element_type=jnp.float32)
    return values * cosine + swapped * sine


def query_kernel(
    count, pool_pages, page_size, hidden_ref, attn_gain_ref, w_query_ref, query_gain_ref, w_gate_ref, w_value_ref,
    w_key_ref, key_gain_ref, frequency_ref, table_ref, lengths_ref, order_ref, out_ref, query_ref, gate_ref,
    value_ref, key_ref, owned_ref, filled_ref, page_query_ref, slot_scratch, send_sems, recv_sems,
):
    me, peers = peers_of("req", count)
    barrier = pltpu.get_barrier_semaphore()
    for _, peer in peers:
        pl.semaphore_signal(barrier, inc=1, device_id={"req": peer}, device_id_type=MESH_IDS)
    head_width = frequency_ref.shape[1]
    rows = query_ref.shape[0]
    requests = order_ref.shape[1]
    request_ids = lax.broadcasted_iota(jnp.int32, (rows, requests), 1)
    own_rows = me * rows + lax.broadcasted_iota(jnp.int32, (rows, requests), 0)
    own_requests = jnp.sum(jnp.where(request_ids == own_rows, order_ref[...], 0), axis=1, keepdims=True)
    position = jnp.sum(jnp.where(request_ids == own_requests, lengths_ref[...], 0), axis=1, keepdims=True)
    angles = position.astype(jnp.float32) * frequency_ref[...]
    cos_ref = jnp.cos(angles)
    sin_ref = jnp.sin(angles)
    lanes_in = lax.broadcasted_iota(jnp.int32, (head_width, head_width), 0)
    lanes_out = lax.broadcasted_iota(jnp.int32, (head_width, head_width), 1)
    swap = jnp.where(
        lanes_in == lax.rem(lanes_out + head_width // 2, head_width),
        jnp.where(lanes_out < head_width // 2, -1.0, 1.0),
        0.0,
    ).astype(jnp.float32)
    hidden = hidden_ref[...].astype(jnp.float32)
    normed = (hidden * rms_inv(hidden) * attn_gain_ref[...]).astype(jnp.bfloat16)
    queries = jnp.dot(normed, w_query_ref[...], preferred_element_type=jnp.float32)
    for pair in range(queries.shape[1] // head_width):
        lanes = slice(pair * head_width, (pair + 1) * head_width)
        query = queries[:, lanes]
        query = query * rms_inv(query) * query_gain_ref[...]
        query_ref[:, lanes] = rope(query, cos_ref, sin_ref, swap).astype(query_ref.dtype)
    pl.semaphore_wait(barrier, len(peers))
    copies = []
    for offset, peer in peers:
        copy = pltpu.make_async_remote_copy(
            src_ref=query_ref,
            dst_ref=out_ref.at[me],
            send_sem=send_sems.at[offset],
            recv_sem=recv_sems.at[offset],
            device_id={"req": peer},
            device_id_type=MESH_IDS,
        )
        copy.start()
        copies.append(copy)
    out_ref[me] = query_ref[...]
    gate_ref[...] = jnp.dot(normed, w_gate_ref[...], preferred_element_type=jnp.float32)
    value_ref[...] = jnp.dot(normed, w_value_ref[...], preferred_element_type=jnp.float32).astype(value_ref.dtype)
    keys = jnp.dot(normed, w_key_ref[...], preferred_element_type=jnp.float32)
    for kv in range(keys.shape[1] // head_width):
        lanes = slice(kv * head_width, (kv + 1) * head_width)
        key = keys[:, lanes]
        key = key * rms_inv(key) * key_gain_ref[...]
        key_ref[:, lanes] = rope(key, cos_ref, sin_ref, swap).astype(key_ref.dtype)
    slots, requests = table_ref.shape
    slot_ids = lax.broadcasted_iota(jnp.int32, (slots, requests), 0)
    lengths = lengths_ref[...]
    local_ids = table_ref[...] - me * pool_pages
    usable = (slot_ids < (lengths + page_size - 1) // page_size) & (local_ids >= 0) & (local_ids < pool_pages)
    keyed = jnp.where(usable, local_ids, pool_pages)
    slot_f = slot_ids.astype(jnp.float32)

    def one_page(page, carry):
        hit = keyed == page
        owned_ref[pl.ds(page, 1), :] = jnp.max(jnp.where(hit, 1.0, 0.0), axis=0, keepdims=True)
        slot_scratch[pl.ds(page, 1), :] = jnp.sum(jnp.where(hit, slot_f, 0.0), axis=0, keepdims=True)
        return carry

    lax.fori_loop(0, pool_pages, one_page, 0)
    owned_requests = owned_ref[...]
    owner_slot = jnp.sum(slot_scratch[...], axis=1, keepdims=True)
    owner_length = jnp.sum(owned_requests * lengths.astype(jnp.float32), axis=1, keepdims=True)
    filled = jnp.clip(owner_length - owner_slot * page_size, 0.0, float(page_size))
    filled = jnp.where(jnp.max(owned_requests, axis=1, keepdims=True) > 0.5, filled, 0.0)
    tokens = lax.broadcasted_iota(jnp.int32, filled_ref.shape, 1).astype(jnp.float32)
    filled_ref[...] = jnp.where(tokens < filled, 1.0, 0.0)
    dealing = (lax.broadcasted_iota(jnp.int32, (requests, requests), 0) == order_ref[...]).astype(jnp.bfloat16)
    owned_rows = jnp.dot(owned_requests.astype(jnp.bfloat16), dealing, preferred_element_type=jnp.float32)
    owned_ref[...] = jnp.where(owned_rows > 0.5, 1.0, 0.0)
    for copy in copies:
        copy.wait()
    rows = query_ref.shape[0]
    page_query_ref[...] = jnp.dot(
        owned_ref[...].astype(jnp.bfloat16),
        out_ref[...].reshape(count * rows, query_ref.shape[1]),
        preferred_element_type=jnp.float32,
    ).astype(page_query_ref.dtype)


def query_exchange(
    hidden, attn_gain, w_query, query_gain, w_gate, w_value, w_key, key_gain, frequency, table, lengths, order,
    pool_pages, page_size, count, ident,
):
    rows = hidden.shape[0]
    requests = table.shape[1]
    return pl.pallas_call(
        functools.partial(query_kernel, count, pool_pages, page_size),
        out_shape=(
            jax.ShapeDtypeStruct((count, rows, w_query.shape[1]), jnp.bfloat16),
            jax.ShapeDtypeStruct((rows, w_query.shape[1]), jnp.bfloat16),
            jax.ShapeDtypeStruct((rows, w_gate.shape[1]), jnp.float32),
            jax.ShapeDtypeStruct((rows, w_value.shape[1]), jnp.bfloat16),
            jax.ShapeDtypeStruct((rows, w_key.shape[1]), jnp.bfloat16),
            jax.ShapeDtypeStruct((pool_pages, requests), jnp.float32),
            jax.ShapeDtypeStruct((pool_pages, page_size), jnp.float32),
            jax.ShapeDtypeStruct((pool_pages, w_query.shape[1]), jnp.bfloat16),
        ),
        in_specs=[pl.BlockSpec(memory_space=pltpu.VMEM)] * 12,
        out_specs=tuple(pl.BlockSpec(memory_space=pltpu.VMEM) for _ in range(8)),
        scratch_shapes=[
            pltpu.VMEM((pool_pages, requests), jnp.float32),
            pltpu.SemaphoreType.DMA((count,)),
            pltpu.SemaphoreType.DMA((count,)),
        ],
        compiler_params=pltpu.CompilerParams(collective_id=ident, has_side_effects=True),
    )(hidden, attn_gain, w_query, query_gain, w_gate, w_value, w_key, key_gain, frequency, table, lengths, order)


def attend_kernel(
    req_count, head_count, group_size, scale_factor, num_ref, stats_ref, query_ref, key_ref, value_ref, gate_ref,
    w_out_ref, hidden_ref, out_ref, got_num, got_stats, projected, summed, send_sems, recv_sems,
):
    req_me, req_peers = peers_of("req", req_count)
    head_me, head_peers = peers_of("head", head_count)
    rows, width = out_ref.shape
    cols = width // head_count
    pairs = stats_ref.shape[1] // 2
    head_width = query_ref.shape[1] // pairs
    mine = pl.ds(pl.multiple_of(head_me * cols, cols), cols)
    greet([("req", peer) for _, peer in req_peers] + [("head", peer) for _, peer in head_peers])
    got_num[req_me] = num_ref[req_me]
    got_stats[req_me] = stats_ref[req_me]
    copies = []
    for offset, peer in req_peers:
        for which, (src_ref, dst_ref) in enumerate(((num_ref, got_num), (stats_ref, got_stats))):
            copy = pltpu.make_async_remote_copy(
                src_ref=src_ref.at[peer],
                dst_ref=dst_ref.at[req_me],
                send_sem=send_sems.at[which, offset],
                recv_sem=recv_sems.at[which, offset],
                device_id={"req": peer},
                device_id_type=MESH_IDS,
            )
            copy.start()
            copies.append(copy)
    for copy in copies:
        copy.wait()
    eye = (
        lax.broadcasted_iota(jnp.int32, (rows, rows), 0) == lax.broadcasted_iota(jnp.int32, (rows, rows), 1)
    ).astype(jnp.float32)
    flip = (((1,), (1,)), ((), ()))
    heads = []
    for pair in range(pairs):
        kv = pair // group_size
        lanes = slice(pair * head_width, (pair + 1) * head_width)
        kv_lanes = slice(kv * head_width, (kv + 1) * head_width)
        shifts = lax.dot_general(
            eye, got_stats[:, pair, :], flip, precision=lax.Precision.HIGHEST, preferred_element_type=jnp.float32
        )
        totals = lax.dot_general(
            eye,
            got_stats[:, pairs + pair, :],
            flip,
            precision=lax.Precision.HIGHEST,
            preferred_element_type=jnp.float32,
        )
        query = query_ref[:, lanes].astype(jnp.float32)
        self_score = jnp.sum(query * key_ref[:, kv_lanes].astype(jnp.float32), axis=1, keepdims=True) * scale_factor
        self_shift = LOG_TWO * jnp.ceil(self_score / LOG_TWO)
        shift = jnp.maximum(jnp.max(shifts, axis=1, keepdims=True), self_shift)
        factor = jnp.exp(shifts - shift)
        self_weight = jnp.exp(self_score - shift)
        total = jnp.sum(totals * factor, axis=1, keepdims=True) + self_weight
        acc = self_weight.astype(jnp.bfloat16).astype(jnp.float32) * value_ref[:, kv_lanes].astype(jnp.float32)
        for source in range(req_count):
            acc = acc + factor[:, source : source + 1] * got_num[source, :, lanes].astype(jnp.float32)
        heads.append(acc / total)
    heads_out = jnp.concatenate(heads, axis=1)
    gate = gate_ref[...]
    attended = (heads_out * (1.0 / (1.0 + jnp.exp(-gate)))).astype(jnp.bfloat16)
    projected[...] = jnp.dot(attended, w_out_ref[...], preferred_element_type=jnp.float32)
    summed[head_me] = projected[:, mine]
    send_all(
        "head", head_peers, lambda peer: projected.at[:, pl.ds(peer * cols, cols)], summed.at[head_me],
        send_sems, recv_sems, 2,
    )
    out_ref[:, mine] = (hidden_ref[:, mine].astype(jnp.float32) + jnp.sum(summed[...], axis=0)).astype(
        out_ref.dtype
    )
    send_all("head", head_peers, lambda peer: out_ref.at[:, mine], out_ref.at[:, mine], send_sems, recv_sems, 3)


def attend_exchange(
    num, stats, queries, keys, values, gate, w_out, hidden, head_count, group_size, scale_factor, ident
):
    req_count = num.shape[0]
    rows, width = hidden.shape
    most = max(head_count, req_count)
    return pl.pallas_call(
        functools.partial(attend_kernel, req_count, head_count, group_size, scale_factor),
        out_shape=jax.ShapeDtypeStruct((rows, width), jnp.bfloat16),
        in_specs=[pl.BlockSpec(memory_space=pltpu.VMEM)] * 8,
        out_specs=pl.BlockSpec(memory_space=pltpu.VMEM),
        scratch_shapes=[
            pltpu.VMEM(num.shape, num.dtype),
            pltpu.VMEM(stats.shape, stats.dtype),
            pltpu.VMEM((rows, width), jnp.float32),
            pltpu.VMEM((head_count, rows, width // head_count), jnp.float32),
            pltpu.SemaphoreType.DMA((4, most)),
            pltpu.SemaphoreType.DMA((4, most)),
        ],
        compiler_params=pltpu.CompilerParams(collective_id=ident, has_side_effects=True),
    )(num, stats, queries, keys, values, gate, w_out, hidden)


def tail_kernel(
    head_count, req_count, mixed_ref, gain_ref, w_gate_ref, w_up_ref, w_down_ref, order_ref, out_ref, parts_ref,
    summed, results, send_sems, recv_sems,
):
    head_me, head_peers = peers_of("head", head_count)
    req_me, req_peers = peers_of("req", req_count)
    rows, width = out_ref.shape
    cols = width // head_count
    mine = pl.ds(pl.multiple_of(head_me * cols, cols), cols)
    barrier = pltpu.get_barrier_semaphore()
    everyone = [("head", peer) for _, peer in head_peers] + [("req", peer) for _, peer in req_peers]
    for axis, peer in everyone:
        pl.semaphore_signal(barrier, inc=1, device_id={axis: peer}, device_id_type=MESH_IDS)
    mixed = mixed_ref[...].astype(jnp.float32)
    normed = (mixed * rms_inv(mixed) * gain_ref[...]).astype(jnp.bfloat16)
    gate_part = jnp.dot(normed, w_gate_ref[...], preferred_element_type=jnp.float32)
    up_part = jnp.dot(normed, w_up_ref[...], preferred_element_type=jnp.float32)
    inner_act = (gate_part / (1.0 + jnp.exp(-gate_part)) * up_part).astype(jnp.bfloat16)
    parts_ref[...] = jnp.dot(inner_act, w_down_ref[...], preferred_element_type=jnp.float32)
    pl.semaphore_wait(barrier, len(everyone))
    summed[head_me] = parts_ref[:, mine]
    send_all(
        "head",
        head_peers,
        lambda peer: parts_ref.at[:, pl.ds(peer * cols, cols)],
        summed.at[head_me],
        send_sems,
        recv_sems,
        0,
    )
    results[req_me] = (mixed_ref[:, mine].astype(jnp.float32) + jnp.sum(summed[...], axis=0)).astype(
        results.dtype
    )
    send_all("req", req_peers, lambda peer: results.at[req_me], results.at[req_me], send_sems, recv_sems, 1)
    wanted = req_me * rows + lax.broadcasted_iota(jnp.int32, (rows, req_count * rows), 0)
    picker = (order_ref[...] == wanted).astype(jnp.bfloat16)
    out_ref[:, mine] = jnp.dot(
        picker, results[...].reshape(req_count * rows, cols), preferred_element_type=jnp.float32
    ).astype(out_ref.dtype)
    send_all("head", head_peers, lambda peer: out_ref.at[:, mine], out_ref.at[:, mine], send_sems, recv_sems, 2)


def tail_exchange(mixed, gain, w_gate, w_up, w_down, order, head_count, req_count, ident):
    rows, width = mixed.shape
    most = max(head_count, req_count)
    return pl.pallas_call(
        functools.partial(tail_kernel, head_count, req_count),
        out_shape=jax.ShapeDtypeStruct((rows, width), jnp.bfloat16),
        in_specs=[pl.BlockSpec(memory_space=pltpu.VMEM)] * 6,
        out_specs=pl.BlockSpec(memory_space=pltpu.VMEM),
        scratch_shapes=[
            pltpu.VMEM((rows, width), jnp.float32),
            pltpu.VMEM((head_count, rows, width // head_count), jnp.float32),
            pltpu.VMEM((req_count, rows, width // head_count), jnp.bfloat16),
            pltpu.SemaphoreType.DMA((3, most)),
            pltpu.SemaphoreType.DMA((3, most)),
        ],
        compiler_params=pltpu.CompilerParams(collective_id=ident, has_side_effects=True),
    )(mixed, gain, w_gate, w_up, w_down, order)


def body(
    req_count,
    head_count,
    hidden,
    deal_order,
    lengths,
    page_table,
    key_cache,
    value_cache,
    attn_gain,
    w_query,
    w_key,
    w_value,
    w_gate,
    w_out,
    query_gain,
    key_gain,
    mlp_gain,
    mlp_gate,
    mlp_up,
    mlp_down,
):
    local_rows, model_width = hidden.shape
    req_index = lax.axis_index("req")
    head_index = lax.axis_index("head")
    all_rows = local_rows * req_count
    head_width = query_gain.shape[0]
    pool_pages, page_size, local_kv = key_cache.shape[:3]
    group_size = w_query.shape[1] // (local_kv * head_width)
    head_cols = local_kv * group_size * head_width
    pairs = local_kv * group_size
    chunk = model_width // head_count
    scale_factor = 1.0 / math.sqrt(head_width)
    first_own = req_index * local_rows

    with jax.named_scope("rotary_tables"):
        half = head_width // 2
        lane_ids = jnp.arange(head_width, dtype=jnp.int32) % half
        frequency = ROPE_BASE ** (-(lane_ids.astype(jnp.float32) * (2.0 / head_width)))

    outs = query_exchange(
        hidden,
        attn_gain.reshape(1, model_width),
        w_query,
        query_gain.reshape(1, head_width),
        w_gate,
        w_value,
        w_key,
        key_gain.reshape(1, head_width),
        frequency.reshape(1, head_width),
        page_table.T,
        lengths.reshape(1, all_rows),
        deal_order.reshape(1, all_rows),
        pool_pages,
        page_size,
        req_count,
        0,
    )
    _, own_queries, gate_logits, new_values, new_keys, owned_f, live_tokens, page_queries = outs
    owned = owned_f > 0.5
    page_queries = page_queries.reshape(pool_pages, local_kv, group_size, head_width)
    new_values = new_values.reshape(local_rows, local_kv, head_width)
    new_keys = new_keys.reshape(local_rows, local_kv, head_width)

    with jax.named_scope("page_attention"):
        scores = (
            jnp.einsum("pkgd,ptkd->pkgt", page_queries, key_cache, preferred_element_type=jnp.float32)
            * scale_factor
        )
        live_mask = live_tokens[:, None, None, :] > 0.5
        scores = jnp.where(live_mask, scores, LOW_SCORE)
        page_peaks = jnp.max(scores, axis=-1)
        owned_b = owned[:, :, None, None]
        row_peaks = jnp.max(jnp.where(owned_b, page_peaks[:, None], LOW_SCORE), axis=0)
        row_shift = LOG_TWO * jnp.ceil(row_peaks / LOG_TWO)
        page_shift = jnp.max(jnp.where(owned_b, row_shift[None], LOW_SCORE), axis=1)
        weights = jnp.where(live_mask, jnp.exp(scores - page_shift[..., None]), 0.0)
        page_totals = jnp.sum(weights, axis=-1)
        page_numerators = jnp.einsum(
            "pkgt,ptkd->pkgd",
            weights.astype(jnp.bfloat16),
            value_cache,
            preferred_element_type=jnp.float32,
        )
        row_totals = jnp.sum(jnp.where(owned_b, page_totals[:, None], 0.0), axis=0).reshape(all_rows, pairs)
        row_numerators = jnp.dot(
            owned_f.T.astype(jnp.bfloat16),
            page_numerators.reshape(pool_pages, head_cols).astype(jnp.bfloat16),
            preferred_element_type=jnp.float32,
        )
        numerator_message = row_numerators.astype(jnp.bfloat16).reshape(req_count, local_rows, head_cols)
        stats_message = jnp.concatenate(
            [row_shift.reshape(req_count, local_rows, pairs), row_totals.reshape(req_count, local_rows, pairs)],
            axis=2,
        ).transpose(0, 2, 1)

    mixed_rows = attend_exchange(
        numerator_message,
        stats_message,
        own_queries,
        new_keys.reshape(local_rows, local_kv * head_width),
        new_values.reshape(local_rows, local_kv * head_width),
        gate_logits,
        w_out,
        hidden,
        head_count,
        group_size,
        scale_factor,
        1,
    )

    return tail_exchange(
        mixed_rows,
        mlp_gain.reshape(1, model_width),
        mlp_gate,
        mlp_up,
        mlp_down,
        deal_order.reshape(1, all_rows),
        head_count,
        req_count,
        3,
    )


def solution(mesh):
    return jax.shard_map(
        functools.partial(body, mesh.shape["req"], mesh.shape["head"]),
        mesh=mesh,
        in_specs=(
            P("req", None),
            P(),
            P(),
            P(),
            P("req", None, "head", None),
            P("req", None, "head", None),
            P(),
            P(None, "head"),
            P(None, "head"),
            P(None, "head"),
            P(None, "head"),
            P("head", None),
            P(),
            P(),
            P(),
            P(None, "head"),
            P(None, "head"),
            P("head", None),
        ),
        out_specs=P("req", None),
        check_vma=False,
    )
```

```python
import functools
import math

import jax
import jax.numpy as jnp
from jax import lax
from jax.experimental import pallas as pl
from jax.experimental.pallas import tpu as pltpu
from jax.sharding import PartitionSpec as P

EPSILON = 1e-06
ROPE_BASE = 1000000.0
LOW_SCORE = -1e30
LOG_TWO = math.log(2.0)
MESH_IDS = pl.DeviceIdType.MESH


def rms_inv(values):
    return lax.rsqrt(jnp.mean(values * values, axis=-1, keepdims=True) + EPSILON)


def rotate(values, position):
    half_dim = values.shape[-1] // 2
    exponent = jnp.arange(half_dim, dtype=jnp.float32) * (2.0 / values.shape[-1])
    frequency = ROPE_BASE ** (-exponent)
    angles = position[:, None] * frequency[None, :]
    ones_tail = (1,) * (values.ndim - 2)
    angles = angles.reshape((angles.shape[0],) + ones_tail + (half_dim,))
    cosine = jnp.cos(angles)
    sine_vals = jnp.sin(angles)
    front_half = values[..., :half_dim]
    back_half = values[..., half_dim:]
    return jnp.concatenate(
        [front_half * cosine - back_half * sine_vals, back_half * cosine + front_half * sine_vals],
        axis=-1,
    )


def norm_rotate(values, gain_vec, position):
    return rotate(values * rms_inv(values) * gain_vec, position)


def exchange_kernel(axis, count, spreads, *refs):
    arrays = len(spreads)
    sources, outputs = refs[:arrays], refs[arrays : 2 * arrays]
    send_sems, recv_sems = refs[2 * arrays], refs[2 * arrays + 1]
    me = lax.axis_index(axis)
    barrier = pltpu.get_barrier_semaphore()
    for offset in range(1, count):
        peer = lax.rem(me + offset, count)
        pl.semaphore_signal(barrier, inc=1, device_id={axis: peer}, device_id_type=MESH_IDS)
    pl.semaphore_wait(barrier, count - 1)
    copies = []
    for offset in range(1, count):
        peer = lax.rem(me + offset, count)
        for which in range(arrays):
            src_ref, out_ref = sources[which], outputs[which]
            copy = pltpu.make_async_remote_copy(
                src_ref=src_ref.at[peer] if spreads[which] else src_ref,
                dst_ref=out_ref.at[me],
                send_sem=send_sems.at[which, offset],
                recv_sem=recv_sems.at[which, offset],
                device_id={axis: peer},
                device_id_type=MESH_IDS,
            )
            copy.start()
            copies.append(copy)
    for which in range(arrays):
        src_ref, out_ref = sources[which], outputs[which]
        out_ref[me] = src_ref[me] if spreads[which] else src_ref[...]
    for copy in copies:
        copy.wait()


def exchange_many(arrays, spreads, axis, count, ident):
    shapes = []
    for values, spread in zip(arrays, spreads):
        block = values.shape[1:] if spread else values.shape
        shapes.append(jax.ShapeDtypeStruct((count,) + tuple(block), values.dtype))
    return pl.pallas_call(
        functools.partial(exchange_kernel, axis, count, tuple(spreads)),
        out_shape=tuple(shapes),
        in_specs=[pl.BlockSpec(memory_space=pltpu.VMEM)] * len(arrays),
        out_specs=tuple(pl.BlockSpec(memory_space=pltpu.VMEM) for _ in arrays),
        scratch_shapes=[
            pltpu.SemaphoreType.DMA((len(arrays), count)),
            pltpu.SemaphoreType.DMA((len(arrays), count)),
        ],
        compiler_params=pltpu.CompilerParams(collective_id=ident, has_side_effects=True),
    )(*arrays)


def exchange(values, axis, count, spread, ident):
    return exchange_many((values,), (spread,), axis, count, ident)[0]


def greet(peers):
    barrier = pltpu.get_barrier_semaphore()
    for axis, peer in peers:
        pl.semaphore_signal(barrier, inc=1, device_id={axis: peer}, device_id_type=MESH_IDS)
    pl.semaphore_wait(barrier, len(peers))


def peers_of(axis, count):
    me = lax.axis_index(axis)
    return me, [(offset, lax.rem(me + offset, count)) for offset in range(1, count)]


def send_all(axis, peers, src_of, dst, send_sems, recv_sems, phase):
    copies = []
    for offset, peer in peers:
        copy = pltpu.make_async_remote_copy(
            src_ref=src_of(peer),
            dst_ref=dst,
            send_sem=send_sems.at[phase, offset],
            recv_sem=recv_sems.at[phase, offset],
            device_id={axis: peer},
            device_id_type=MESH_IDS,
        )
        copy.start()
        copies.append(copy)
    for copy in copies:
        copy.wait()


def residual_kernel(count, parts_ref, hidden_ref, out_ref, summed, send_sems, recv_sems):
    me, peers = peers_of("head", count)
    cols = out_ref.shape[1] // count
    mine = pl.ds(pl.multiple_of(me * cols, cols), cols)
    greet([("head", peer) for _, peer in peers])
    summed[me] = parts_ref[:, mine]
    send_all(
        "head", peers, lambda peer: parts_ref.at[:, pl.ds(peer * cols, cols)], summed.at[me], send_sems, recv_sems, 0
    )
    out_ref[:, mine] = (hidden_ref[:, mine].astype(jnp.float32) + jnp.sum(summed[...], axis=0)).astype(
        out_ref.dtype
    )
    send_all("head", peers, lambda peer: out_ref.at[:, mine], out_ref.at[:, mine], send_sems, recv_sems, 1)


def residual_exchange(parts, hidden, count, ident):
    rows, width = parts.shape
    return pl.pallas_call(
        functools.partial(residual_kernel, count),
        out_shape=jax.ShapeDtypeStruct((rows, width), jnp.bfloat16),
        in_specs=[pl.BlockSpec(memory_space=pltpu.VMEM)] * 2,
        out_specs=pl.BlockSpec(memory_space=pltpu.VMEM),
        scratch_shapes=[
            pltpu.VMEM((count, rows, width // count), jnp.float32),
            pltpu.SemaphoreType.DMA((2, count)),
            pltpu.SemaphoreType.DMA((2, count)),
        ],
        compiler_params=pltpu.CompilerParams(collective_id=ident, has_side_effects=True),
    )(parts, hidden)


def rope(values, cosine, sine, swap):
    swapped = jnp.dot(values, swap, precision=lax.Precision.HIGHEST, preferred_element_type=jnp.float32)
    return values * cosine + swapped * sine


def query_kernel(
    count, pool_pages, page_size, hidden_ref, attn_gain_ref, w_query_ref, query_gain_ref, w_gate_ref, w_value_ref,
    w_key_ref, key_gain_ref, frequency_ref, table_ref, lengths_ref, order_ref, out_ref, query_ref, gate_ref,
    value_ref, key_ref, owned_ref, filled_ref, page_query_ref, slot_scratch, send_sems, recv_sems,
):
    me, peers = peers_of("req", count)
    barrier = pltpu.get_barrier_semaphore()
    for _, peer in peers:
        pl.semaphore_signal(barrier, inc=1, device_id={"req": peer}, device_id_type=MESH_IDS)
    head_width = frequency_ref.shape[1]
    rows = query_ref.shape[0]
    requests = order_ref.shape[1]
    request_ids = lax.broadcasted_iota(jnp.int32, (rows, requests), 1)
    own_rows = me * rows + lax.broadcasted_iota(jnp.int32, (rows, requests), 0)
    own_requests = jnp.sum(jnp.where(request_ids == own_rows, order_ref[...], 0), axis=1, keepdims=True)
    position = jnp.sum(jnp.where(request_ids == own_requests, lengths_ref[...], 0), axis=1, keepdims=True)
    angles = position.astype(jnp.float32) * frequency_ref[...]
    cos_ref = jnp.cos(angles)
    sin_ref = jnp.sin(angles)
    lanes_in = lax.broadcasted_iota(jnp.int32, (head_width, head_width), 0)
    lanes_out = lax.broadcasted_iota(jnp.int32, (head_width, head_width), 1)
    swap = jnp.where(
        lanes_in == lax.rem(lanes_out + head_width // 2, head_width),
        jnp.where(lanes_out < head_width // 2, -1.0, 1.0),
        0.0,
    ).astype(jnp.float32)
    hidden = hidden_ref[...].astype(jnp.float32)
    normed = (hidden * rms_inv(hidden) * attn_gain_ref[...]).astype(jnp.bfloat16)
    queries = jnp.dot(normed, w_query_ref[...], preferred_element_type=jnp.float32)
    for pair in range(queries.shape[1] // head_width):
        lanes = slice(pair * head_width, (pair + 1) * head_width)
        query = queries[:, lanes]
        query = query * rms_inv(query) * query_gain_ref[...]
        query_ref[:, lanes] = rope(query, cos_ref, sin_ref, swap).astype(query_ref.dtype)
    pl.semaphore_wait(barrier, len(peers))
    copies = []
    for offset, peer in peers:
        copy = pltpu.make_async_remote_copy(
            src_ref=query_ref,
            dst_ref=out_ref.at[me],
            send_sem=send_sems.at[offset],
            recv_sem=recv_sems.at[offset],
            device_id={"req": peer},
            device_id_type=MESH_IDS,
        )
        copy.start()
        copies.append(copy)
    out_ref[me] = query_ref[...]
    gate_ref[...] = jnp.dot(normed, w_gate_ref[...], preferred_element_type=jnp.float32)
    value_ref[...] = jnp.dot(normed, w_value_ref[...], preferred_element_type=jnp.float32).astype(value_ref.dtype)
    keys = jnp.dot(normed, w_key_ref[...], preferred_element_type=jnp.float32)
    for kv in range(keys.shape[1] // head_width):
        lanes = slice(kv * head_width, (kv + 1) * head_width)
        key = keys[:, lanes]
        key = key * rms_inv(key) * key_gain_ref[...]
        key_ref[:, lanes] = rope(key, cos_ref, sin_ref, swap).astype(key_ref.dtype)
    slots, requests = table_ref.shape
    slot_ids = lax.broadcasted_iota(jnp.int32, (slots, requests), 0)
    lengths = lengths_ref[...]
    local_ids = table_ref[...] - me * pool_pages
    usable = (slot_ids < (lengths + page_size - 1) // page_size) & (local_ids >= 0) & (local_ids < pool_pages)
    keyed = jnp.where(usable, local_ids, pool_pages)
    slot_f = slot_ids.astype(jnp.float32)

    def one_page(page, carry):
        hit = keyed == page
        owned_ref[pl.ds(page, 1), :] = jnp.max(jnp.where(hit, 1.0, 0.0), axis=0, keepdims=True)
        slot_scratch[pl.ds(page, 1), :] = jnp.sum(jnp.where(hit, slot_f, 0.0), axis=0, keepdims=True)
        return carry

    lax.fori_loop(0, pool_pages, one_page, 0)
    owned_requests = owned_ref[...]
    owner_slot = jnp.sum(slot_scratch[...], axis=1, keepdims=True)
    owner_length = jnp.sum(owned_requests * lengths.astype(jnp.float32), axis=1, keepdims=True)
    filled = jnp.clip(owner_length - owner_slot * page_size, 0.0, float(page_size))
    filled = jnp.where(jnp.max(owned_requests, axis=1, keepdims=True) > 0.5, filled, 0.0)
    tokens = lax.broadcasted_iota(jnp.int32, filled_ref.shape, 1).astype(jnp.float32)
    filled_ref[...] = jnp.where(tokens < filled, 1.0, 0.0)
    dealing = (lax.broadcasted_iota(jnp.int32, (requests, requests), 0) == order_ref[...]).astype(jnp.bfloat16)
    owned_rows = jnp.dot(owned_requests.astype(jnp.bfloat16), dealing, preferred_element_type=jnp.float32)
    owned_ref[...] = jnp.where(owned_rows > 0.5, 1.0, 0.0)
    for copy in copies:
        copy.wait()
    rows = query_ref.shape[0]
    page_query_ref[...] = jnp.dot(
        owned_ref[...].astype(jnp.bfloat16),
        out_ref[...].reshape(count * rows, query_ref.shape[1]),
        preferred_element_type=jnp.float32,
    ).astype(page_query_ref.dtype)


def query_exchange(
    hidden, attn_gain, w_query, query_gain, w_gate, w_value, w_key, key_gain, frequency, table, lengths, order,
    pool_pages, page_size, count, ident,
):
    rows = hidden.shape[0]
    requests = table.shape[1]
    return pl.pallas_call(
        functools.partial(query_kernel, count, pool_pages, page_size),
        out_shape=(
            jax.ShapeDtypeStruct((count, rows, w_query.shape[1]), jnp.bfloat16),
            jax.ShapeDtypeStruct((rows, w_query.shape[1]), jnp.bfloat16),
            jax.ShapeDtypeStruct((rows, w_gate.shape[1]), jnp.float32),
            jax.ShapeDtypeStruct((rows, w_value.shape[1]), jnp.bfloat16),
            jax.ShapeDtypeStruct((rows, w_key.shape[1]), jnp.bfloat16),
            jax.ShapeDtypeStruct((pool_pages, requests), jnp.float32),
            jax.ShapeDtypeStruct((pool_pages, page_size), jnp.float32),
            jax.ShapeDtypeStruct((pool_pages, w_query.shape[1]), jnp.bfloat16),
        ),
        in_specs=[pl.BlockSpec(memory_space=pltpu.VMEM)] * 12,
        out_specs=tuple(pl.BlockSpec(memory_space=pltpu.VMEM) for _ in range(8)),
        scratch_shapes=[
            pltpu.VMEM((pool_pages, requests), jnp.float32),
            pltpu.SemaphoreType.DMA((count,)),
            pltpu.SemaphoreType.DMA((count,)),
        ],
        compiler_params=pltpu.CompilerParams(collective_id=ident, has_side_effects=True),
    )(hidden, attn_gain, w_query, query_gain, w_gate, w_value, w_key, key_gain, frequency, table, lengths, order)


def attend_kernel(
    req_count, head_count, group_size, scale_factor, num_ref, stats_ref, query_ref, key_ref, value_ref, gate_ref,
    w_out_ref, hidden_ref, out_ref, got_num, got_stats, projected, summed, send_sems, recv_sems,
):
    req_me, req_peers = peers_of("req", req_count)
    head_me, head_peers = peers_of("head", head_count)
    rows, width = out_ref.shape
    cols = width // head_count
    pairs = stats_ref.shape[1] // 2
    head_width = query_ref.shape[1] // pairs
    mine = pl.ds(pl.multiple_of(head_me * cols, cols), cols)
    greet([("req", peer) for _, peer in req_peers] + [("head", peer) for _, peer in head_peers])
    got_num[req_me] = num_ref[req_me]
    got_stats[req_me] = stats_ref[req_me]
    copies = []
    for offset, peer in req_peers:
        for which, (src_ref, dst_ref) in enumerate(((num_ref, got_num), (stats_ref, got_stats))):
            copy = pltpu.make_async_remote_copy(
                src_ref=src_ref.at[peer],
                dst_ref=dst_ref.at[req_me],
                send_sem=send_sems.at[which, offset],
                recv_sem=recv_sems.at[which, offset],
                device_id={"req": peer},
                device_id_type=MESH_IDS,
            )
            copy.start()
            copies.append(copy)
    for copy in copies:
        copy.wait()
    eye = (
        lax.broadcasted_iota(jnp.int32, (rows, rows), 0) == lax.broadcasted_iota(jnp.int32, (rows, rows), 1)
    ).astype(jnp.float32)
    flip = (((1,), (1,)), ((), ()))
    heads = []
    for pair in range(pairs):
        kv = pair // group_size
        lanes = slice(pair * head_width, (pair + 1) * head_width)
        kv_lanes = slice(kv * head_width, (kv + 1) * head_width)
        shifts = lax.dot_general(
            eye, got_stats[:, pair, :], flip, precision=lax.Precision.HIGHEST, preferred_element_type=jnp.float32
        )
        totals = lax.dot_general(
            eye,
            got_stats[:, pairs + pair, :],
            flip,
            precision=lax.Precision.HIGHEST,
            preferred_element_type=jnp.float32,
        )
        query = query_ref[:, lanes].astype(jnp.float32)
        self_score = jnp.sum(query * key_ref[:, kv_lanes].astype(jnp.float32), axis=1, keepdims=True) * scale_factor
        self_shift = LOG_TWO * jnp.ceil(self_score / LOG_TWO)
        shift = jnp.maximum(jnp.max(shifts, axis=1, keepdims=True), self_shift)
        factor = jnp.exp(shifts - shift)
        self_weight = jnp.exp(self_score - shift)
        total = jnp.sum(totals * factor, axis=1, keepdims=True) + self_weight
        acc = self_weight.astype(jnp.bfloat16).astype(jnp.float32) * value_ref[:, kv_lanes].astype(jnp.float32)
        for source in range(req_count):
            acc = acc + factor[:, source : source + 1] * got_num[source, :, lanes].astype(jnp.float32)
        heads.append(acc / total)
    heads_out = jnp.concatenate(heads, axis=1)
    gate = gate_ref[...]
    attended = (heads_out * (1.0 / (1.0 + jnp.exp(-gate)))).astype(jnp.bfloat16)
    projected[...] = jnp.dot(attended, w_out_ref[...], preferred_element_type=jnp.float32)
    summed[head_me] = projected[:, mine]
    send_all(
        "head", head_peers, lambda peer: projected.at[:, pl.ds(peer * cols, cols)], summed.at[head_me],
        send_sems, recv_sems, 2,
    )
    out_ref[:, mine] = (hidden_ref[:, mine].astype(jnp.float32) + jnp.sum(summed[...], axis=0)).astype(
        out_ref.dtype
    )
    send_all("head", head_peers, lambda peer: out_ref.at[:, mine], out_ref.at[:, mine], send_sems, recv_sems, 3)


def attend_exchange(
    num, stats, queries, keys, values, gate, w_out, hidden, head_count, group_size, scale_factor, ident
):
    req_count = num.shape[0]
    rows, width = hidden.shape
    most = max(head_count, req_count)
    return pl.pallas_call(
        functools.partial(attend_kernel, req_count, head_count, group_size, scale_factor),
        out_shape=jax.ShapeDtypeStruct((rows, width), jnp.bfloat16),
        in_specs=[pl.BlockSpec(memory_space=pltpu.VMEM)] * 8,
        out_specs=pl.BlockSpec(memory_space=pltpu.VMEM),
        scratch_shapes=[
            pltpu.VMEM(num.shape, num.dtype),
            pltpu.VMEM(stats.shape, stats.dtype),
            pltpu.VMEM((rows, width), jnp.float32),
            pltpu.VMEM((head_count, rows, width // head_count), jnp.float32),
            pltpu.SemaphoreType.DMA((4, most)),
            pltpu.SemaphoreType.DMA((4, most)),
        ],
        compiler_params=pltpu.CompilerParams(collective_id=ident, has_side_effects=True),
    )(num, stats, queries, keys, values, gate, w_out, hidden)


def tail_kernel(
    head_count, req_count, mixed_ref, gain_ref, w_gate_ref, w_up_ref, w_down_ref, order_ref, out_ref, parts_ref,
    summed, results, send_sems, recv_sems,
):
    head_me, head_peers = peers_of("head", head_count)
    req_me, req_peers = peers_of("req", req_count)
    rows, width = out_ref.shape
    cols = width // head_count
    mine = pl.ds(pl.multiple_of(head_me * cols, cols), cols)
    barrier = pltpu.get_barrier_semaphore()
    everyone = [("head", peer) for _, peer in head_peers] + [("req", peer) for _, peer in req_peers]
    for axis, peer in everyone:
        pl.semaphore_signal(barrier, inc=1, device_id={axis: peer}, device_id_type=MESH_IDS)
    mixed = mixed_ref[...].astype(jnp.float32)
    normed = (mixed * rms_inv(mixed) * gain_ref[...]).astype(jnp.bfloat16)
    gate_part = jnp.dot(normed, w_gate_ref[...], preferred_element_type=jnp.float32)
    up_part = jnp.dot(normed, w_up_ref[...], preferred_element_type=jnp.float32)
    inner_act = (gate_part / (1.0 + jnp.exp(-gate_part)) * up_part).astype(jnp.bfloat16)
    parts_ref[...] = jnp.dot(inner_act, w_down_ref[...], preferred_element_type=jnp.float32)
    pl.semaphore_wait(barrier, len(everyone))
    summed[head_me] = parts_ref[:, mine]
    send_all(
        "head",
        head_peers,
        lambda peer: parts_ref.at[:, pl.ds(peer * cols, cols)],
        summed.at[head_me],
        send_sems,
        recv_sems,
        0,
    )
    results[req_me] = (mixed_ref[:, mine].astype(jnp.float32) + jnp.sum(summed[...], axis=0)).astype(
        results.dtype
    )
    send_all("req", req_peers, lambda peer: results.at[req_me], results.at[req_me], send_sems, recv_sems, 1)
    wanted = req_me * rows + lax.broadcasted_iota(jnp.int32, (rows, req_count * rows), 0)
    picker = (order_ref[...] == wanted).astype(jnp.bfloat16)
    out_ref[:, mine] = jnp.dot(
        picker, results[...].reshape(req_count * rows, cols), preferred_element_type=jnp.float32
    ).astype(out_ref.dtype)
    send_all("head", head_peers, lambda peer: out_ref.at[:, mine], out_ref.at[:, mine], send_sems, recv_sems, 2)


def tail_exchange(mixed, gain, w_gate, w_up, w_down, order, head_count, req_count, ident):
    rows, width = mixed.shape
    most = max(head_count, req_count)
    return pl.pallas_call(
        functools.partial(tail_kernel, head_count, req_count),
        out_shape=jax.ShapeDtypeStruct((rows, width), jnp.bfloat16),
        in_specs=[pl.BlockSpec(memory_space=pltpu.VMEM)] * 6,
        out_specs=pl.BlockSpec(memory_space=pltpu.VMEM),
        scratch_shapes=[
            pltpu.VMEM((rows, width), jnp.float32),
            pltpu.VMEM((head_count, rows, width // head_count), jnp.float32),
            pltpu.VMEM((req_count, rows, width // head_count), jnp.bfloat16),
            pltpu.SemaphoreType.DMA((3, most)),
            pltpu.SemaphoreType.DMA((3, most)),
        ],
        compiler_params=pltpu.CompilerParams(collective_id=ident, has_side_effects=True),
    )(mixed, gain, w_gate, w_up, w_down, order)


def body(
    req_count,
    head_count,
    hidden,
    deal_order,
    lengths,
    page_table,
    key_cache,
    value_cache,
    attn_gain,
    w_query,
    w_key,
    w_value,
    w_gate,
    w_out,
    query_gain,
    key_gain,
    mlp_gain,
    mlp_gate,
    mlp_up,
    mlp_down,
):
    local_rows, model_width = hidden.shape
    req_index = lax.axis_index("req")
    head_index = lax.axis_index("head")
    all_rows = local_rows * req_count
    head_width = query_gain.shape[0]
    pool_pages, page_size, local_kv = key_cache.shape[:3]
    group_size = w_query.shape[1] // (local_kv * head_width)
    head_cols = local_kv * group_size * head_width
    pairs = local_kv * group_size
    chunk = model_width // head_count
    scale_factor = 1.0 / math.sqrt(head_width)
    first_own = req_index * local_rows

    with jax.named_scope("rotary_tables"):
        half = head_width // 2
        lane_ids = jnp.arange(head_width, dtype=jnp.int32) % half
        frequency = ROPE_BASE ** (-(lane_ids.astype(jnp.float32) * (2.0 / head_width)))

    outs = query_exchange(
        hidden,
        attn_gain.reshape(1, model_width),
        w_query,
        query_gain.reshape(1, head_width),
        w_gate,
        w_value,
        w_key,
        key_gain.reshape(1, head_width),
        frequency.reshape(1, head_width),
        page_table.T,
        lengths.reshape(1, all_rows),
        deal_order.reshape(1, all_rows),
        pool_pages,
        page_size,
        req_count,
        0,
    )
    _, own_queries, gate_logits, new_values, new_keys, owned_f, live_tokens, page_queries = outs
    page_queries = page_queries.reshape(pool_pages, local_kv, group_size, head_width)
    new_values = new_values.reshape(local_rows, local_kv, head_width)
    new_keys = new_keys.reshape(local_rows, local_kv, head_width)

    with jax.named_scope("page_attention"):
        scores = (
            jnp.einsum("pkgd,ptkd->pkgt", page_queries, key_cache, preferred_element_type=jnp.float32)
            * scale_factor
        )
        scores = jnp.where(live_tokens[:, None, None, :] > 0.5, scores, LOW_SCORE)
        page_peaks = jnp.max(scores, axis=-1)
        row_peaks = jnp.max(jnp.where(owned_f[:, :, None, None] > 0.5, page_peaks[:, None], LOW_SCORE), axis=0)
        row_shift = LOG_TWO * jnp.ceil(row_peaks / LOG_TWO)
        page_shift = jnp.max(jnp.where(owned_f[:, :, None, None] > 0.5, row_shift[None], LOW_SCORE), axis=1)
        weights = live_tokens[:, None, None, :] * jnp.exp(scores - page_shift[..., None])
        page_totals = jnp.sum(weights, axis=-1)
        page_numerators = jnp.einsum(
            "pkgt,ptkd->pkgd",
            weights.astype(jnp.bfloat16),
            value_cache,
            preferred_element_type=jnp.float32,
        )
        row_totals = jnp.sum(owned_f[:, :, None, None] * page_totals[:, None], axis=0).reshape(all_rows, pairs)
        row_numerators = jnp.dot(
            owned_f.T.astype(jnp.bfloat16),
            page_numerators.reshape(pool_pages, head_cols).astype(jnp.bfloat16),
            preferred_element_type=jnp.float32,
        )
        numerator_message = row_numerators.astype(jnp.bfloat16).reshape(req_count, local_rows, head_cols)
        stats_message = jnp.concatenate(
            [row_shift.reshape(req_count, local_rows, pairs), row_totals.reshape(req_count, local_rows, pairs)],
            axis=2,
        ).transpose(0, 2, 1)

    mixed_rows = attend_exchange(
        numerator_message,
        stats_message,
        own_queries,
        new_keys.reshape(local_rows, local_kv * head_width),
        new_values.reshape(local_rows, local_kv * head_width),
        gate_logits,
        w_out,
        hidden,
        head_count,
        group_size,
        scale_factor,
        1,
    )

    return tail_exchange(
        mixed_rows,
        mlp_gain.reshape(1, model_width),
        mlp_gate,
        mlp_up,
        mlp_down,
        deal_order.reshape(1, all_rows),
        head_count,
        req_count,
        3,
    )


def solution(mesh):
    return jax.shard_map(
        functools.partial(body, mesh.shape["req"], mesh.shape["head"]),
        mesh=mesh,
        in_specs=(
            P("req", None),
            P(),
            P(),
            P(),
            P("req", None, "head", None),
            P("req", None, "head", None),
            P(),
            P(None, "head"),
            P(None, "head"),
            P(None, "head"),
            P(None, "head"),
            P("head", None),
            P(),
            P(),
            P(),
            P(None, "head"),
            P(None, "head"),
            P("head", None),
        ),
        out_specs=P("req", None),
        check_vma=False,
    )
```

```python
import functools
import math

import jax
import jax.numpy as jnp
from jax import lax
from jax.experimental import pallas as pl
from jax.experimental.pallas import tpu as pltpu
from jax.sharding import PartitionSpec as P

EPSILON = 1e-06
ROPE_BASE = 1000000.0
LOW_SCORE = -1e30
LOG_TWO = math.log(2.0)
MESH_IDS = pl.DeviceIdType.MESH


def rms_inv(values):
    return lax.rsqrt(jnp.mean(values * values, axis=-1, keepdims=True) + EPSILON)


def rotate(values, position):
    half_dim = values.shape[-1] // 2
    exponent = jnp.arange(half_dim, dtype=jnp.float32) * (2.0 / values.shape[-1])
    frequency = ROPE_BASE ** (-exponent)
    angles = position[:, None] * frequency[None, :]
    ones_tail = (1,) * (values.ndim - 2)
    angles = angles.reshape((angles.shape[0],) + ones_tail + (half_dim,))
    cosine = jnp.cos(angles)
    sine_vals = jnp.sin(angles)
    front_half = values[..., :half_dim]
    back_half = values[..., half_dim:]
    return jnp.concatenate(
        [front_half * cosine - back_half * sine_vals, back_half * cosine + front_half * sine_vals],
        axis=-1,
    )


def norm_rotate(values, gain_vec, position):
    return rotate(values * rms_inv(values) * gain_vec, position)


def exchange_kernel(axis, count, spreads, *refs):
    arrays = len(spreads)
    sources, outputs = refs[:arrays], refs[arrays : 2 * arrays]
    send_sems, recv_sems = refs[2 * arrays], refs[2 * arrays + 1]
    me = lax.axis_index(axis)
    barrier = pltpu.get_barrier_semaphore()
    for offset in range(1, count):
        peer = lax.rem(me + offset, count)
        pl.semaphore_signal(barrier, inc=1, device_id={axis: peer}, device_id_type=MESH_IDS)
    pl.semaphore_wait(barrier, count - 1)
    copies = []
    for offset in range(1, count):
        peer = lax.rem(me + offset, count)
        for which in range(arrays):
            src_ref, out_ref = sources[which], outputs[which]
            copy = pltpu.make_async_remote_copy(
                src_ref=src_ref.at[peer] if spreads[which] else src_ref,
                dst_ref=out_ref.at[me],
                send_sem=send_sems.at[which, offset],
                recv_sem=recv_sems.at[which, offset],
                device_id={axis: peer},
                device_id_type=MESH_IDS,
            )
            copy.start()
            copies.append(copy)
    for which in range(arrays):
        src_ref, out_ref = sources[which], outputs[which]
        out_ref[me] = src_ref[me] if spreads[which] else src_ref[...]
    for copy in copies:
        copy.wait()


def exchange_many(arrays, spreads, axis, count, ident):
    shapes = []
    for values, spread in zip(arrays, spreads):
        block = values.shape[1:] if spread else values.shape
        shapes.append(jax.ShapeDtypeStruct((count,) + tuple(block), values.dtype))
    return pl.pallas_call(
        functools.partial(exchange_kernel, axis, count, tuple(spreads)),
        out_shape=tuple(shapes),
        in_specs=[pl.BlockSpec(memory_space=pltpu.VMEM)] * len(arrays),
        out_specs=tuple(pl.BlockSpec(memory_space=pltpu.VMEM) for _ in arrays),
        scratch_shapes=[
            pltpu.SemaphoreType.DMA((len(arrays), count)),
            pltpu.SemaphoreType.DMA((len(arrays), count)),
        ],
        compiler_params=pltpu.CompilerParams(collective_id=ident, has_side_effects=True),
    )(*arrays)


def exchange(values, axis, count, spread, ident):
    return exchange_many((values,), (spread,), axis, count, ident)[0]


def greet(peers):
    barrier = pltpu.get_barrier_semaphore()
    for axis, peer in peers:
        pl.semaphore_signal(barrier, inc=1, device_id={axis: peer}, device_id_type=MESH_IDS)
    pl.semaphore_wait(barrier, len(peers))


def peers_of(axis, count):
    me = lax.axis_index(axis)
    return me, [(offset, lax.rem(me + offset, count)) for offset in range(1, count)]


def send_all(axis, peers, src_of, dst, send_sems, recv_sems, phase):
    copies = []
    for offset, peer in peers:
        copy = pltpu.make_async_remote_copy(
            src_ref=src_of(peer),
            dst_ref=dst,
            send_sem=send_sems.at[phase, offset],
            recv_sem=recv_sems.at[phase, offset],
            device_id={axis: peer},
            device_id_type=MESH_IDS,
        )
        copy.start()
        copies.append(copy)
    for copy in copies:
        copy.wait()


def residual_kernel(count, parts_ref, hidden_ref, out_ref, summed, send_sems, recv_sems):
    me, peers = peers_of("head", count)
    cols = out_ref.shape[1] // count
    mine = pl.ds(pl.multiple_of(me * cols, cols), cols)
    greet([("head", peer) for _, peer in peers])
    summed[me] = parts_ref[:, mine]
    send_all(
        "head", peers, lambda peer: parts_ref.at[:, pl.ds(peer * cols, cols)], summed.at[me], send_sems, recv_sems, 0
    )
    out_ref[:, mine] = (hidden_ref[:, mine].astype(jnp.float32) + jnp.sum(summed[...], axis=0)).astype(
        out_ref.dtype
    )
    send_all("head", peers, lambda peer: out_ref.at[:, mine], out_ref.at[:, mine], send_sems, recv_sems, 1)


def residual_exchange(parts, hidden, count, ident):
    rows, width = parts.shape
    return pl.pallas_call(
        functools.partial(residual_kernel, count),
        out_shape=jax.ShapeDtypeStruct((rows, width), jnp.bfloat16),
        in_specs=[pl.BlockSpec(memory_space=pltpu.VMEM)] * 2,
        out_specs=pl.BlockSpec(memory_space=pltpu.VMEM),
        scratch_shapes=[
            pltpu.VMEM((count, rows, width // count), jnp.float32),
            pltpu.SemaphoreType.DMA((2, count)),
            pltpu.SemaphoreType.DMA((2, count)),
        ],
        compiler_params=pltpu.CompilerParams(collective_id=ident, has_side_effects=True),
    )(parts, hidden)


def rope(values, cosine, sine, swap):
    swapped = jnp.dot(values, swap, precision=lax.Precision.HIGHEST, preferred_element_type=jnp.float32)
    return values * cosine + swapped * sine


def query_kernel(
    count, pool_pages, page_size, hidden_ref, attn_gain_ref, w_query_ref, query_gain_ref, w_gate_ref, w_value_ref,
    w_key_ref, key_gain_ref, frequency_ref, table_ref, lengths_ref, order_ref, out_ref, query_ref, gate_ref,
    value_ref, key_ref, owned_ref, filled_ref, page_query_ref, slot_scratch, send_sems, recv_sems,
):
    me, peers = peers_of("req", count)
    barrier = pltpu.get_barrier_semaphore()
    for _, peer in peers:
        pl.semaphore_signal(barrier, inc=1, device_id={"req": peer}, device_id_type=MESH_IDS)
    head_width = frequency_ref.shape[1]
    rows = query_ref.shape[0]
    requests = order_ref.shape[1]
    request_ids = lax.broadcasted_iota(jnp.int32, (rows, requests), 1)
    own_rows = me * rows + lax.broadcasted_iota(jnp.int32, (rows, requests), 0)
    own_requests = jnp.sum(jnp.where(request_ids == own_rows, order_ref[...], 0), axis=1, keepdims=True)
    position = jnp.sum(jnp.where(request_ids == own_requests, lengths_ref[...], 0), axis=1, keepdims=True)
    angles = position.astype(jnp.float32) * frequency_ref[...]
    cos_ref = jnp.cos(angles)
    sin_ref = jnp.sin(angles)
    lanes_in = lax.broadcasted_iota(jnp.int32, (head_width, head_width), 0)
    lanes_out = lax.broadcasted_iota(jnp.int32, (head_width, head_width), 1)
    swap = jnp.where(
        lanes_in == lax.rem(lanes_out + head_width // 2, head_width),
        jnp.where(lanes_out < head_width // 2, -1.0, 1.0),
        0.0,
    ).astype(jnp.float32)
    hidden = hidden_ref[...].astype(jnp.float32)
    normed = (hidden * rms_inv(hidden) * attn_gain_ref[...]).astype(jnp.bfloat16)
    queries = jnp.dot(normed, w_query_ref[...], preferred_element_type=jnp.float32)
    for pair in range(queries.shape[1] // head_width):
        lanes = slice(pair * head_width, (pair + 1) * head_width)
        query = queries[:, lanes]
        query = query * rms_inv(query) * query_gain_ref[...]
        query_ref[:, lanes] = rope(query, cos_ref, sin_ref, swap).astype(query_ref.dtype)
    pl.semaphore_wait(barrier, len(peers))
    copies = []
    for offset, peer in peers:
        copy = pltpu.make_async_remote_copy(
            src_ref=query_ref,
            dst_ref=out_ref.at[me],
            send_sem=send_sems.at[offset],
            recv_sem=recv_sems.at[offset],
            device_id={"req": peer},
            device_id_type=MESH_IDS,
        )
        copy.start()
        copies.append(copy)
    out_ref[me] = query_ref[...]
    gate_ref[...] = jnp.dot(normed, w_gate_ref[...], preferred_element_type=jnp.float32)
    value_ref[...] = jnp.dot(normed, w_value_ref[...], preferred_element_type=jnp.float32).astype(value_ref.dtype)
    keys = jnp.dot(normed, w_key_ref[...], preferred_element_type=jnp.float32)
    for kv in range(keys.shape[1] // head_width):
        lanes = slice(kv * head_width, (kv + 1) * head_width)
        key = keys[:, lanes]
        key = key * rms_inv(key) * key_gain_ref[...]
        key_ref[:, lanes] = rope(key, cos_ref, sin_ref, swap).astype(key_ref.dtype)
    slots, requests = table_ref.shape
    slot_ids = lax.broadcasted_iota(jnp.int32, (slots, requests), 0)
    lengths = lengths_ref[...]
    local_ids = table_ref[...] - me * pool_pages
    usable = (slot_ids < (lengths + page_size - 1) // page_size) & (local_ids >= 0) & (local_ids < pool_pages)
    keyed = jnp.where(usable, local_ids, pool_pages)
    slot_f = slot_ids.astype(jnp.float32)

    def one_page(page, carry):
        hit = keyed == page
        owned_ref[pl.ds(page, 1), :] = jnp.max(jnp.where(hit, 1.0, 0.0), axis=0, keepdims=True)
        slot_scratch[pl.ds(page, 1), :] = jnp.sum(jnp.where(hit, slot_f, 0.0), axis=0, keepdims=True)
        return carry

    lax.fori_loop(0, pool_pages, one_page, 0)
    owned_requests = owned_ref[...]
    owner_slot = jnp.sum(slot_scratch[...], axis=1, keepdims=True)
    owner_length = jnp.sum(owned_requests * lengths.astype(jnp.float32), axis=1, keepdims=True)
    filled = jnp.clip(owner_length - owner_slot * page_size, 0.0, float(page_size))
    filled = jnp.where(jnp.max(owned_requests, axis=1, keepdims=True) > 0.5, filled, 0.0)
    tokens = lax.broadcasted_iota(jnp.int32, filled_ref.shape, 1).astype(jnp.float32)
    filled_ref[...] = jnp.where(tokens < filled, 1.0, 0.0)
    dealing = (lax.broadcasted_iota(jnp.int32, (requests, requests), 0) == order_ref[...]).astype(jnp.bfloat16)
    owned_rows = jnp.dot(owned_requests.astype(jnp.bfloat16), dealing, preferred_element_type=jnp.float32)
    owned_ref[...] = jnp.where(owned_rows > 0.5, 1.0, 0.0)
    for copy in copies:
        copy.wait()
    rows = query_ref.shape[0]
    page_queries = jnp.dot(
        owned_ref[...].astype(jnp.bfloat16),
        out_ref[...].reshape(count * rows, query_ref.shape[1]),
        preferred_element_type=jnp.float32,
    ).astype(page_query_ref.dtype)
    for pair in range(page_query_ref.shape[1]):
        page_query_ref[:, pair, :] = page_queries[:, pair * head_width : (pair + 1) * head_width]


def query_exchange(
    hidden, attn_gain, w_query, query_gain, w_gate, w_value, w_key, key_gain, frequency, table, lengths, order,
    pool_pages, page_size, count, ident,
):
    rows = hidden.shape[0]
    requests = table.shape[1]
    return pl.pallas_call(
        functools.partial(query_kernel, count, pool_pages, page_size),
        out_shape=(
            jax.ShapeDtypeStruct((count, rows, w_query.shape[1]), jnp.bfloat16),
            jax.ShapeDtypeStruct((rows, w_query.shape[1]), jnp.bfloat16),
            jax.ShapeDtypeStruct((rows, w_gate.shape[1]), jnp.float32),
            jax.ShapeDtypeStruct((rows, w_value.shape[1]), jnp.bfloat16),
            jax.ShapeDtypeStruct((rows, w_key.shape[1]), jnp.bfloat16),
            jax.ShapeDtypeStruct((pool_pages, requests), jnp.float32),
            jax.ShapeDtypeStruct((pool_pages, page_size), jnp.float32),
            jax.ShapeDtypeStruct((pool_pages, w_query.shape[1] // key_gain.shape[1], key_gain.shape[1]), jnp.bfloat16),
        ),
        in_specs=[pl.BlockSpec(memory_space=pltpu.VMEM)] * 12,
        out_specs=tuple(pl.BlockSpec(memory_space=pltpu.VMEM) for _ in range(8)),
        scratch_shapes=[
            pltpu.VMEM((pool_pages, requests), jnp.float32),
            pltpu.SemaphoreType.DMA((count,)),
            pltpu.SemaphoreType.DMA((count,)),
        ],
        compiler_params=pltpu.CompilerParams(collective_id=ident, has_side_effects=True),
    )(hidden, attn_gain, w_query, query_gain, w_gate, w_value, w_key, key_gain, frequency, table, lengths, order)


def attend_kernel(
    req_count, head_count, group_size, scale_factor, num_ref, stats_ref, query_ref, key_ref, value_ref, gate_ref,
    w_out_ref, hidden_ref, out_ref, got_num, got_stats, projected, summed, send_sems, recv_sems,
):
    req_me, req_peers = peers_of("req", req_count)
    head_me, head_peers = peers_of("head", head_count)
    rows, width = out_ref.shape
    cols = width // head_count
    pairs = stats_ref.shape[1] // 2
    head_width = query_ref.shape[1] // pairs
    mine = pl.ds(pl.multiple_of(head_me * cols, cols), cols)
    greet([("req", peer) for _, peer in req_peers] + [("head", peer) for _, peer in head_peers])
    got_num[req_me] = num_ref[req_me]
    got_stats[req_me] = stats_ref[req_me]
    copies = []
    for offset, peer in req_peers:
        for which, (src_ref, dst_ref) in enumerate(((num_ref, got_num), (stats_ref, got_stats))):
            copy = pltpu.make_async_remote_copy(
                src_ref=src_ref.at[peer],
                dst_ref=dst_ref.at[req_me],
                send_sem=send_sems.at[which, offset],
                recv_sem=recv_sems.at[which, offset],
                device_id={"req": peer},
                device_id_type=MESH_IDS,
            )
            copy.start()
            copies.append(copy)
    for copy in copies:
        copy.wait()
    eye = (
        lax.broadcasted_iota(jnp.int32, (rows, rows), 0) == lax.broadcasted_iota(jnp.int32, (rows, rows), 1)
    ).astype(jnp.float32)
    flip = (((1,), (1,)), ((), ()))
    heads = []
    for pair in range(pairs):
        kv = pair // group_size
        lanes = slice(pair * head_width, (pair + 1) * head_width)
        kv_lanes = slice(kv * head_width, (kv + 1) * head_width)
        shifts = lax.dot_general(
            eye, got_stats[:, pair, :], flip, precision=lax.Precision.HIGHEST, preferred_element_type=jnp.float32
        )
        totals = lax.dot_general(
            eye,
            got_stats[:, pairs + pair, :],
            flip,
            precision=lax.Precision.HIGHEST,
            preferred_element_type=jnp.float32,
        )
        query = query_ref[:, lanes].astype(jnp.float32)
        self_score = jnp.sum(query * key_ref[:, kv_lanes].astype(jnp.float32), axis=1, keepdims=True) * scale_factor
        self_shift = LOG_TWO * jnp.ceil(self_score / LOG_TWO)
        shift = jnp.maximum(jnp.max(shifts, axis=1, keepdims=True), self_shift)
        factor = jnp.exp(shifts - shift)
        self_weight = jnp.exp(self_score - shift)
        total = jnp.sum(totals * factor, axis=1, keepdims=True) + self_weight
        acc = self_weight.astype(jnp.bfloat16).astype(jnp.float32) * value_ref[:, kv_lanes].astype(jnp.float32)
        for source in range(req_count):
            acc = acc + factor[:, source : source + 1] * got_num[source, :, lanes].astype(jnp.float32)
        heads.append(acc / total)
    heads_out = jnp.concatenate(heads, axis=1)
    gate = gate_ref[...]
    attended = (heads_out * (1.0 / (1.0 + jnp.exp(-gate)))).astype(jnp.bfloat16)
    projected[...] = jnp.dot(attended, w_out_ref[...], preferred_element_type=jnp.float32)
    summed[head_me] = projected[:, mine]
    send_all(
        "head", head_peers, lambda peer: projected.at[:, pl.ds(peer * cols, cols)], summed.at[head_me],
        send_sems, recv_sems, 2,
    )
    out_ref[:, mine] = (hidden_ref[:, mine].astype(jnp.float32) + jnp.sum(summed[...], axis=0)).astype(
        out_ref.dtype
    )
    send_all("head", head_peers, lambda peer: out_ref.at[:, mine], out_ref.at[:, mine], send_sems, recv_sems, 3)


def attend_exchange(
    num, stats, queries, keys, values, gate, w_out, hidden, head_count, group_size, scale_factor, ident
):
    req_count = num.shape[0]
    rows, width = hidden.shape
    most = max(head_count, req_count)
    return pl.pallas_call(
        functools.partial(attend_kernel, req_count, head_count, group_size, scale_factor),
        out_shape=jax.ShapeDtypeStruct((rows, width), jnp.bfloat16),
        in_specs=[pl.BlockSpec(memory_space=pltpu.VMEM)] * 8,
        out_specs=pl.BlockSpec(memory_space=pltpu.VMEM),
        scratch_shapes=[
            pltpu.VMEM(num.shape, num.dtype),
            pltpu.VMEM(stats.shape, stats.dtype),
            pltpu.VMEM((rows, width), jnp.float32),
            pltpu.VMEM((head_count, rows, width // head_count), jnp.float32),
            pltpu.SemaphoreType.DMA((4, most)),
            pltpu.SemaphoreType.DMA((4, most)),
        ],
        compiler_params=pltpu.CompilerParams(collective_id=ident, has_side_effects=True),
    )(num, stats, queries, keys, values, gate, w_out, hidden)


def tail_kernel(
    head_count, req_count, mixed_ref, gain_ref, w_gate_ref, w_up_ref, w_down_ref, order_ref, out_ref, parts_ref,
    summed, results, send_sems, recv_sems,
):
    head_me, head_peers = peers_of("head", head_count)
    req_me, req_peers = peers_of("req", req_count)
    rows, width = out_ref.shape
    cols = width // head_count
    mine = pl.ds(pl.multiple_of(head_me * cols, cols), cols)
    barrier = pltpu.get_barrier_semaphore()
    everyone = [("head", peer) for _, peer in head_peers] + [("req", peer) for _, peer in req_peers]
    for axis, peer in everyone:
        pl.semaphore_signal(barrier, inc=1, device_id={axis: peer}, device_id_type=MESH_IDS)
    mixed = mixed_ref[...].astype(jnp.float32)
    normed = (mixed * rms_inv(mixed) * gain_ref[...]).astype(jnp.bfloat16)
    gate_part = jnp.dot(normed, w_gate_ref[...], preferred_element_type=jnp.float32)
    up_part = jnp.dot(normed, w_up_ref[...], preferred_element_type=jnp.float32)
    inner_act = (gate_part / (1.0 + jnp.exp(-gate_part)) * up_part).astype(jnp.bfloat16)
    parts_ref[...] = jnp.dot(inner_act, w_down_ref[...], preferred_element_type=jnp.float32)
    pl.semaphore_wait(barrier, len(everyone))
    summed[head_me] = parts_ref[:, mine]
    send_all(
        "head",
        head_peers,
        lambda peer: parts_ref.at[:, pl.ds(peer * cols, cols)],
        summed.at[head_me],
        send_sems,
        recv_sems,
        0,
    )
    results[req_me] = (mixed_ref[:, mine].astype(jnp.float32) + jnp.sum(summed[...], axis=0)).astype(
        results.dtype
    )
    send_all("req", req_peers, lambda peer: results.at[req_me], results.at[req_me], send_sems, recv_sems, 1)
    wanted = req_me * rows + lax.broadcasted_iota(jnp.int32, (rows, req_count * rows), 0)
    picker = (order_ref[...] == wanted).astype(jnp.bfloat16)
    out_ref[:, mine] = jnp.dot(
        picker, results[...].reshape(req_count * rows, cols), preferred_element_type=jnp.float32
    ).astype(out_ref.dtype)
    send_all("head", head_peers, lambda peer: out_ref.at[:, mine], out_ref.at[:, mine], send_sems, recv_sems, 2)


def tail_exchange(mixed, gain, w_gate, w_up, w_down, order, head_count, req_count, ident):
    rows, width = mixed.shape
    most = max(head_count, req_count)
    return pl.pallas_call(
        functools.partial(tail_kernel, head_count, req_count),
        out_shape=jax.ShapeDtypeStruct((rows, width), jnp.bfloat16),
        in_specs=[pl.BlockSpec(memory_space=pltpu.VMEM)] * 6,
        out_specs=pl.BlockSpec(memory_space=pltpu.VMEM),
        scratch_shapes=[
            pltpu.VMEM((rows, width), jnp.float32),
            pltpu.VMEM((head_count, rows, width // head_count), jnp.float32),
            pltpu.VMEM((req_count, rows, width // head_count), jnp.bfloat16),
            pltpu.SemaphoreType.DMA((3, most)),
            pltpu.SemaphoreType.DMA((3, most)),
        ],
        compiler_params=pltpu.CompilerParams(collective_id=ident, has_side_effects=True),
    )(mixed, gain, w_gate, w_up, w_down, order)


def body(
    req_count,
    head_count,
    hidden,
    deal_order,
    lengths,
    page_table,
    key_cache,
    value_cache,
    attn_gain,
    w_query,
    w_key,
    w_value,
    w_gate,
    w_out,
    query_gain,
    key_gain,
    mlp_gain,
    mlp_gate,
    mlp_up,
    mlp_down,
):
    local_rows, model_width = hidden.shape
    req_index = lax.axis_index("req")
    head_index = lax.axis_index("head")
    all_rows = local_rows * req_count
    head_width = query_gain.shape[0]
    pool_pages, page_size, local_kv = key_cache.shape[:3]
    group_size = w_query.shape[1] // (local_kv * head_width)
    head_cols = local_kv * group_size * head_width
    pairs = local_kv * group_size
    chunk = model_width // head_count
    scale_factor = 1.0 / math.sqrt(head_width)
    first_own = req_index * local_rows

    with jax.named_scope("rotary_tables"):
        half = head_width // 2
        lane_ids = jnp.arange(head_width, dtype=jnp.int32) % half
        frequency = ROPE_BASE ** (-(lane_ids.astype(jnp.float32) * (2.0 / head_width)))

    outs = query_exchange(
        hidden,
        attn_gain.reshape(1, model_width),
        w_query,
        query_gain.reshape(1, head_width),
        w_gate,
        w_value,
        w_key,
        key_gain.reshape(1, head_width),
        frequency.reshape(1, head_width),
        page_table.T,
        lengths.reshape(1, all_rows),
        deal_order.reshape(1, all_rows),
        pool_pages,
        page_size,
        req_count,
        0,
    )
    _, own_queries, gate_logits, new_values, new_keys, owned_f, live_tokens, page_queries = outs
    page_queries = page_queries.reshape(pool_pages, local_kv, group_size, head_width)
    new_values = new_values.reshape(local_rows, local_kv, head_width)
    new_keys = new_keys.reshape(local_rows, local_kv, head_width)

    with jax.named_scope("page_attention"):
        scores = (
            jnp.einsum("pkgd,ptkd->pkgt", page_queries, key_cache, preferred_element_type=jnp.float32)
            * scale_factor
        )
        scores = jnp.where(live_tokens[:, None, None, :] > 0.5, scores, LOW_SCORE)
        page_peaks = jnp.max(scores, axis=-1)
        row_peaks = jnp.max(jnp.where(owned_f[:, :, None, None] > 0.5, page_peaks[:, None], LOW_SCORE), axis=0)
        row_shift = LOG_TWO * jnp.ceil(row_peaks / LOG_TWO)
        page_shift = jnp.max(jnp.where(owned_f[:, :, None, None] > 0.5, row_shift[None], LOW_SCORE), axis=1)
        weights = live_tokens[:, None, None, :] * jnp.exp(scores - page_shift[..., None])
        page_totals = jnp.sum(weights, axis=-1)
        page_numerators = jnp.einsum(
            "pkgt,ptkd->pkgd",
            weights.astype(jnp.bfloat16),
            value_cache,
            preferred_element_type=jnp.float32,
        )
        row_totals = jnp.sum(owned_f[:, :, None, None] * page_totals[:, None], axis=0).reshape(all_rows, pairs)
        row_numerators = jnp.dot(
            owned_f.T.astype(jnp.bfloat16),
            page_numerators.reshape(pool_pages, head_cols).astype(jnp.bfloat16),
            preferred_element_type=jnp.float32,
        )
        numerator_message = row_numerators.astype(jnp.bfloat16).reshape(req_count, local_rows, head_cols)
        stats_message = jnp.concatenate(
            [row_shift.reshape(req_count, local_rows, pairs), row_totals.reshape(req_count, local_rows, pairs)],
            axis=2,
        ).transpose(0, 2, 1)

    mixed_rows = attend_exchange(
        numerator_message,
        stats_message,
        own_queries,
        new_keys.reshape(local_rows, local_kv * head_width),
        new_values.reshape(local_rows, local_kv * head_width),
        gate_logits,
        w_out,
        hidden,
        head_count,
        group_size,
        scale_factor,
        1,
    )

    return tail_exchange(
        mixed_rows,
        mlp_gain.reshape(1, model_width),
        mlp_gate,
        mlp_up,
        mlp_down,
        deal_order.reshape(1, all_rows),
        head_count,
        req_count,
        3,
    )


def solution(mesh):
    return jax.shard_map(
        functools.partial(body, mesh.shape["req"], mesh.shape["head"]),
        mesh=mesh,
        in_specs=(
            P("req", None),
            P(),
            P(),
            P(),
            P("req", None, "head", None),
            P("req", None, "head", None),
            P(),
            P(None, "head"),
            P(None, "head"),
            P(None, "head"),
            P(None, "head"),
            P("head", None),
            P(),
            P(),
            P(),
            P(None, "head"),
            P(None, "head"),
            P("head", None),
        ),
        out_specs=P("req", None),
        check_vma=False,
    )
```

```python
import functools
import math

import jax
import jax.numpy as jnp
from jax import lax
from jax.experimental import pallas as pl
from jax.experimental.pallas import tpu as pltpu
from jax.sharding import PartitionSpec as P

EPSILON = 1e-06
ROPE_BASE = 1000000.0
LOW_SCORE = -1e30
LOG_TWO = math.log(2.0)
MESH_IDS = pl.DeviceIdType.MESH


def rms_inv(values):
    return lax.rsqrt(jnp.mean(values * values, axis=-1, keepdims=True) + EPSILON)


def rotate(values, position):
    half_dim = values.shape[-1] // 2
    exponent = jnp.arange(half_dim, dtype=jnp.float32) * (2.0 / values.shape[-1])
    frequency = ROPE_BASE ** (-exponent)
    angles = position[:, None] * frequency[None, :]
    ones_tail = (1,) * (values.ndim - 2)
    angles = angles.reshape((angles.shape[0],) + ones_tail + (half_dim,))
    cosine = jnp.cos(angles)
    sine_vals = jnp.sin(angles)
    front_half = values[..., :half_dim]
    back_half = values[..., half_dim:]
    return jnp.concatenate(
        [front_half * cosine - back_half * sine_vals, back_half * cosine + front_half * sine_vals],
        axis=-1,
    )


def norm_rotate(values, gain_vec, position):
    return rotate(values * rms_inv(values) * gain_vec, position)


def exchange_kernel(axis, count, spreads, *refs):
    arrays = len(spreads)
    sources, outputs = refs[:arrays], refs[arrays : 2 * arrays]
    send_sems, recv_sems = refs[2 * arrays], refs[2 * arrays + 1]
    me = lax.axis_index(axis)
    barrier = pltpu.get_barrier_semaphore()
    for offset in range(1, count):
        peer = lax.rem(me + offset, count)
        pl.semaphore_signal(barrier, inc=1, device_id={axis: peer}, device_id_type=MESH_IDS)
    pl.semaphore_wait(barrier, count - 1)
    copies = []
    for offset in range(1, count):
        peer = lax.rem(me + offset, count)
        for which in range(arrays):
            src_ref, out_ref = sources[which], outputs[which]
            copy = pltpu.make_async_remote_copy(
                src_ref=src_ref.at[peer] if spreads[which] else src_ref,
                dst_ref=out_ref.at[me],
                send_sem=send_sems.at[which, offset],
                recv_sem=recv_sems.at[which, offset],
                device_id={axis: peer},
                device_id_type=MESH_IDS,
            )
            copy.start()
            copies.append(copy)
    for which in range(arrays):
        src_ref, out_ref = sources[which], outputs[which]
        out_ref[me] = src_ref[me] if spreads[which] else src_ref[...]
    for copy in copies:
        copy.wait()


def exchange_many(arrays, spreads, axis, count, ident):
    shapes = []
    for values, spread in zip(arrays, spreads):
        block = values.shape[1:] if spread else values.shape
        shapes.append(jax.ShapeDtypeStruct((count,) + tuple(block), values.dtype))
    return pl.pallas_call(
        functools.partial(exchange_kernel, axis, count, tuple(spreads)),
        out_shape=tuple(shapes),
        in_specs=[pl.BlockSpec(memory_space=pltpu.VMEM)] * len(arrays),
        out_specs=tuple(pl.BlockSpec(memory_space=pltpu.VMEM) for _ in arrays),
        scratch_shapes=[
            pltpu.SemaphoreType.DMA((len(arrays), count)),
            pltpu.SemaphoreType.DMA((len(arrays), count)),
        ],
        compiler_params=pltpu.CompilerParams(collective_id=ident, has_side_effects=True),
    )(*arrays)


def exchange(values, axis, count, spread, ident):
    return exchange_many((values,), (spread,), axis, count, ident)[0]


def greet(peers):
    barrier = pltpu.get_barrier_semaphore()
    for axis, peer in peers:
        pl.semaphore_signal(barrier, inc=1, device_id={axis: peer}, device_id_type=MESH_IDS)
    pl.semaphore_wait(barrier, len(peers))


def peers_of(axis, count):
    me = lax.axis_index(axis)
    return me, [(offset, lax.rem(me + offset, count)) for offset in range(1, count)]


def send_all(axis, peers, src_of, dst, send_sems, recv_sems, phase):
    copies = []
    for offset, peer in peers:
        copy = pltpu.make_async_remote_copy(
            src_ref=src_of(peer),
            dst_ref=dst,
            send_sem=send_sems.at[phase, offset],
            recv_sem=recv_sems.at[phase, offset],
            device_id={axis: peer},
            device_id_type=MESH_IDS,
        )
        copy.start()
        copies.append(copy)
    for copy in copies:
        copy.wait()


def residual_kernel(count, parts_ref, hidden_ref, out_ref, summed, send_sems, recv_sems):
    me, peers = peers_of("head", count)
    cols = out_ref.shape[1] // count
    mine = pl.ds(pl.multiple_of(me * cols, cols), cols)
    greet([("head", peer) for _, peer in peers])
    summed[me] = parts_ref[:, mine]
    send_all(
        "head", peers, lambda peer: parts_ref.at[:, pl.ds(peer * cols, cols)], summed.at[me], send_sems, recv_sems, 0
    )
    out_ref[:, mine] = (hidden_ref[:, mine].astype(jnp.float32) + jnp.sum(summed[...], axis=0)).astype(
        out_ref.dtype
    )
    send_all("head", peers, lambda peer: out_ref.at[:, mine], out_ref.at[:, mine], send_sems, recv_sems, 1)


def residual_exchange(parts, hidden, count, ident):
    rows, width = parts.shape
    return pl.pallas_call(
        functools.partial(residual_kernel, count),
        out_shape=jax.ShapeDtypeStruct((rows, width), jnp.bfloat16),
        in_specs=[pl.BlockSpec(memory_space=pltpu.VMEM)] * 2,
        out_specs=pl.BlockSpec(memory_space=pltpu.VMEM),
        scratch_shapes=[
            pltpu.VMEM((count, rows, width // count), jnp.float32),
            pltpu.SemaphoreType.DMA((2, count)),
            pltpu.SemaphoreType.DMA((2, count)),
        ],
        compiler_params=pltpu.CompilerParams(collective_id=ident, has_side_effects=True),
    )(parts, hidden)


def rope(values, cosine, sine, swap):
    swapped = jnp.dot(values, swap, precision=lax.Precision.HIGHEST, preferred_element_type=jnp.float32)
    return values * cosine + swapped * sine


def query_kernel(
    count, pool_pages, page_size, hidden_ref, attn_gain_ref, w_query_ref, query_gain_ref, w_gate_ref, w_value_ref,
    w_key_ref, key_gain_ref, frequency_ref, table_ref, lengths_ref, order_ref, out_ref, query_ref, gate_ref,
    value_ref, key_ref, owned_ref, filled_ref, page_query_ref, slot_scratch, send_sems, recv_sems,
):
    me, peers = peers_of("req", count)
    barrier = pltpu.get_barrier_semaphore()
    for _, peer in peers:
        pl.semaphore_signal(barrier, inc=1, device_id={"req": peer}, device_id_type=MESH_IDS)
    head_width = frequency_ref.shape[1]
    rows = query_ref.shape[0]
    requests = order_ref.shape[1]
    request_ids = lax.broadcasted_iota(jnp.int32, (rows, requests), 1)
    own_rows = me * rows + lax.broadcasted_iota(jnp.int32, (rows, requests), 0)
    own_requests = jnp.sum(jnp.where(request_ids == own_rows, order_ref[...], 0), axis=1, keepdims=True)
    position = jnp.sum(jnp.where(request_ids == own_requests, lengths_ref[...], 0), axis=1, keepdims=True)
    angles = position.astype(jnp.float32) * frequency_ref[...]
    cos_ref = jnp.cos(angles)
    sin_ref = jnp.sin(angles)
    lanes_in = lax.broadcasted_iota(jnp.int32, (head_width, head_width), 0)
    lanes_out = lax.broadcasted_iota(jnp.int32, (head_width, head_width), 1)
    swap = jnp.where(
        lanes_in == lax.rem(lanes_out + head_width // 2, head_width),
        jnp.where(lanes_out < head_width // 2, -1.0, 1.0),
        0.0,
    ).astype(jnp.float32)
    hidden = hidden_ref[...].astype(jnp.float32)
    normed = (hidden * rms_inv(hidden) * attn_gain_ref[...]).astype(jnp.bfloat16)
    queries = jnp.dot(normed, w_query_ref[...], preferred_element_type=jnp.float32)
    for pair in range(queries.shape[1] // head_width):
        lanes = slice(pair * head_width, (pair + 1) * head_width)
        query = queries[:, lanes]
        query = query * rms_inv(query) * query_gain_ref[...]
        query_ref[:, lanes] = rope(query, cos_ref, sin_ref, swap).astype(query_ref.dtype)
    pl.semaphore_wait(barrier, len(peers))
    copies = []
    for offset, peer in peers:
        copy = pltpu.make_async_remote_copy(
            src_ref=query_ref,
            dst_ref=out_ref.at[me],
            send_sem=send_sems.at[offset],
            recv_sem=recv_sems.at[offset],
            device_id={"req": peer},
            device_id_type=MESH_IDS,
        )
        copy.start()
        copies.append(copy)
    out_ref[me] = query_ref[...]
    gate_ref[...] = jnp.dot(normed, w_gate_ref[...], preferred_element_type=jnp.float32)
    value_ref[...] = jnp.dot(normed, w_value_ref[...], preferred_element_type=jnp.float32).astype(value_ref.dtype)
    keys = jnp.dot(normed, w_key_ref[...], preferred_element_type=jnp.float32)
    for kv in range(keys.shape[1] // head_width):
        lanes = slice(kv * head_width, (kv + 1) * head_width)
        key = keys[:, lanes]
        key = key * rms_inv(key) * key_gain_ref[...]
        key_ref[:, lanes] = rope(key, cos_ref, sin_ref, swap).astype(key_ref.dtype)
    slots, requests = table_ref.shape
    slot_ids = lax.broadcasted_iota(jnp.int32, (slots, requests), 0)
    lengths = lengths_ref[...]
    local_ids = table_ref[...] - me * pool_pages
    usable = (slot_ids < (lengths + page_size - 1) // page_size) & (local_ids >= 0) & (local_ids < pool_pages)
    keyed = jnp.where(usable, local_ids, pool_pages)
    slot_f = slot_ids.astype(jnp.float32)

    def one_page(page, carry):
        hit = keyed == page
        owned_ref[pl.ds(page, 1), :] = jnp.max(jnp.where(hit, 1.0, 0.0), axis=0, keepdims=True)
        slot_scratch[pl.ds(page, 1), :] = jnp.sum(jnp.where(hit, slot_f, 0.0), axis=0, keepdims=True)
        return carry

    lax.fori_loop(0, pool_pages, one_page, 0)
    owned_requests = owned_ref[...]
    owner_slot = jnp.sum(slot_scratch[...], axis=1, keepdims=True)
    owner_length = jnp.sum(owned_requests * lengths.astype(jnp.float32), axis=1, keepdims=True)
    filled = jnp.clip(owner_length - owner_slot * page_size, 0.0, float(page_size))
    filled = jnp.where(jnp.max(owned_requests, axis=1, keepdims=True) > 0.5, filled, 0.0)
    tokens = lax.broadcasted_iota(jnp.int32, filled_ref.shape, 1).astype(jnp.float32)
    filled_ref[...] = jnp.where(tokens < filled, 1.0, 0.0)
    dealing = (lax.broadcasted_iota(jnp.int32, (requests, requests), 0) == order_ref[...]).astype(jnp.bfloat16)
    owned_rows = jnp.dot(owned_requests.astype(jnp.bfloat16), dealing, preferred_element_type=jnp.float32)
    owned_ref[...] = jnp.where(owned_rows > 0.5, 1.0, 0.0)
    for copy in copies:
        copy.wait()
    rows = query_ref.shape[0]
    page_query_ref[...] = jnp.dot(
        owned_ref[...].astype(jnp.bfloat16),
        out_ref[...].reshape(count * rows, query_ref.shape[1]),
        preferred_element_type=jnp.float32,
    ).astype(page_query_ref.dtype)


def query_exchange(
    hidden, attn_gain, w_query, query_gain, w_gate, w_value, w_key, key_gain, frequency, table, lengths, order,
    pool_pages, page_size, count, ident,
):
    rows = hidden.shape[0]
    requests = table.shape[1]
    return pl.pallas_call(
        functools.partial(query_kernel, count, pool_pages, page_size),
        out_shape=(
            jax.ShapeDtypeStruct((count, rows, w_query.shape[1]), jnp.bfloat16),
            jax.ShapeDtypeStruct((rows, w_query.shape[1]), jnp.bfloat16),
            jax.ShapeDtypeStruct((rows, w_gate.shape[1]), jnp.float32),
            jax.ShapeDtypeStruct((rows, w_value.shape[1]), jnp.bfloat16),
            jax.ShapeDtypeStruct((rows, w_key.shape[1]), jnp.bfloat16),
            jax.ShapeDtypeStruct((pool_pages, requests), jnp.float32),
            jax.ShapeDtypeStruct((pool_pages, page_size), jnp.float32),
            jax.ShapeDtypeStruct((pool_pages, w_query.shape[1]), jnp.bfloat16),
        ),
        in_specs=[pl.BlockSpec(memory_space=pltpu.VMEM)] * 12,
        out_specs=tuple(pl.BlockSpec(memory_space=pltpu.VMEM) for _ in range(8)),
        scratch_shapes=[
            pltpu.VMEM((pool_pages, requests), jnp.float32),
            pltpu.SemaphoreType.DMA((count,)),
            pltpu.SemaphoreType.DMA((count,)),
        ],
        compiler_params=pltpu.CompilerParams(collective_id=ident, has_side_effects=True),
    )(hidden, attn_gain, w_query, query_gain, w_gate, w_value, w_key, key_gain, frequency, table, lengths, order)


def attend_kernel(
    req_count, head_count, group_size, scale_factor, num_ref, stats_ref, query_ref, key_ref, value_ref, gate_ref,
    w_out_ref, hidden_ref, out_ref, got_num, got_stats, projected, summed, send_sems, recv_sems,
):
    req_me, req_peers = peers_of("req", req_count)
    head_me, head_peers = peers_of("head", head_count)
    rows, width = out_ref.shape
    cols = width // head_count
    pairs = stats_ref.shape[1] // 2
    head_width = query_ref.shape[1] // pairs
    mine = pl.ds(pl.multiple_of(head_me * cols, cols), cols)
    barrier = pltpu.get_barrier_semaphore()
    everyone = [("req", peer) for _, peer in req_peers] + [("head", peer) for _, peer in head_peers]
    for axis, peer in everyone:
        pl.semaphore_signal(barrier, inc=1, device_id={axis: peer}, device_id_type=MESH_IDS)
    self_scores = []
    for pair in range(pairs):
        kv = pair // group_size
        query = query_ref[:, pair * head_width : (pair + 1) * head_width].astype(jnp.float32)
        key = key_ref[:, kv * head_width : (kv + 1) * head_width].astype(jnp.float32)
        self_scores.append(jnp.sum(query * key, axis=1, keepdims=True) * scale_factor)
    gate = gate_ref[...]
    gate_scale = 1.0 / (1.0 + jnp.exp(-gate))
    pl.semaphore_wait(barrier, len(everyone))
    got_num[req_me] = num_ref[req_me]
    got_stats[req_me] = stats_ref[req_me]
    copies = []
    for offset, peer in req_peers:
        for which, (src_ref, dst_ref) in enumerate(((num_ref, got_num), (stats_ref, got_stats))):
            copy = pltpu.make_async_remote_copy(
                src_ref=src_ref.at[peer],
                dst_ref=dst_ref.at[req_me],
                send_sem=send_sems.at[which, offset],
                recv_sem=recv_sems.at[which, offset],
                device_id={"req": peer},
                device_id_type=MESH_IDS,
            )
            copy.start()
            copies.append(copy)
    for copy in copies:
        copy.wait()
    eye = (
        lax.broadcasted_iota(jnp.int32, (rows, rows), 0) == lax.broadcasted_iota(jnp.int32, (rows, rows), 1)
    ).astype(jnp.float32)
    flip = (((1,), (1,)), ((), ()))
    heads = []
    for pair in range(pairs):
        kv = pair // group_size
        lanes = slice(pair * head_width, (pair + 1) * head_width)
        kv_lanes = slice(kv * head_width, (kv + 1) * head_width)
        shifts = lax.dot_general(
            eye, got_stats[:, pair, :], flip, precision=lax.Precision.HIGHEST, preferred_element_type=jnp.float32
        )
        totals = lax.dot_general(
            eye,
            got_stats[:, pairs + pair, :],
            flip,
            precision=lax.Precision.HIGHEST,
            preferred_element_type=jnp.float32,
        )
        self_score = self_scores[pair]
        self_shift = LOG_TWO * jnp.ceil(self_score / LOG_TWO)
        shift = jnp.maximum(jnp.max(shifts, axis=1, keepdims=True), self_shift)
        factor = jnp.exp(shifts - shift)
        self_weight = jnp.exp(self_score - shift)
        total = jnp.sum(totals * factor, axis=1, keepdims=True) + self_weight
        acc = self_weight.astype(jnp.bfloat16).astype(jnp.float32) * value_ref[:, kv_lanes].astype(jnp.float32)
        for source in range(req_count):
            acc = acc + factor[:, source : source + 1] * got_num[source, :, lanes].astype(jnp.float32)
        heads.append(acc / total)
    heads_out = jnp.concatenate(heads, axis=1)
    attended = (heads_out * gate_scale).astype(jnp.bfloat16)
    projected[...] = jnp.dot(attended, w_out_ref[...], preferred_element_type=jnp.float32)
    summed[head_me] = projected[:, mine]
    send_all(
        "head", head_peers, lambda peer: projected.at[:, pl.ds(peer * cols, cols)], summed.at[head_me],
        send_sems, recv_sems, 2,
    )
    out_ref[:, mine] = (hidden_ref[:, mine].astype(jnp.float32) + jnp.sum(summed[...], axis=0)).astype(
        out_ref.dtype
    )
    send_all("head", head_peers, lambda peer: out_ref.at[:, mine], out_ref.at[:, mine], send_sems, recv_sems, 3)


def attend_exchange(
    num, stats, queries, keys, values, gate, w_out, hidden, head_count, group_size, scale_factor, ident
):
    req_count = num.shape[0]
    rows, width = hidden.shape
    most = max(head_count, req_count)
    return pl.pallas_call(
        functools.partial(attend_kernel, req_count, head_count, group_size, scale_factor),
        out_shape=jax.ShapeDtypeStruct((rows, width), jnp.bfloat16),
        in_specs=[pl.BlockSpec(memory_space=pltpu.VMEM)] * 8,
        out_specs=pl.BlockSpec(memory_space=pltpu.VMEM),
        scratch_shapes=[
            pltpu.VMEM(num.shape, num.dtype),
            pltpu.VMEM(stats.shape, stats.dtype),
            pltpu.VMEM((rows, width), jnp.float32),
            pltpu.VMEM((head_count, rows, width // head_count), jnp.float32),
            pltpu.SemaphoreType.DMA((4, most)),
            pltpu.SemaphoreType.DMA((4, most)),
        ],
        compiler_params=pltpu.CompilerParams(collective_id=ident, has_side_effects=True),
    )(num, stats, queries, keys, values, gate, w_out, hidden)


def tail_kernel(
    head_count, req_count, mixed_ref, gain_ref, w_gate_ref, w_up_ref, w_down_ref, order_ref, out_ref, parts_ref,
    summed, results, send_sems, recv_sems,
):
    head_me, head_peers = peers_of("head", head_count)
    req_me, req_peers = peers_of("req", req_count)
    rows, width = out_ref.shape
    cols = width // head_count
    mine = pl.ds(pl.multiple_of(head_me * cols, cols), cols)
    barrier = pltpu.get_barrier_semaphore()
    everyone = [("head", peer) for _, peer in head_peers] + [("req", peer) for _, peer in req_peers]
    for axis, peer in everyone:
        pl.semaphore_signal(barrier, inc=1, device_id={axis: peer}, device_id_type=MESH_IDS)
    mixed = mixed_ref[...].astype(jnp.float32)
    normed = (mixed * rms_inv(mixed) * gain_ref[...]).astype(jnp.bfloat16)
    gate_part = jnp.dot(normed, w_gate_ref[...], preferred_element_type=jnp.float32)
    up_part = jnp.dot(normed, w_up_ref[...], preferred_element_type=jnp.float32)
    inner_act = (gate_part / (1.0 + jnp.exp(-gate_part)) * up_part).astype(jnp.bfloat16)
    parts_ref[...] = jnp.dot(inner_act, w_down_ref[...], preferred_element_type=jnp.float32)
    pl.semaphore_wait(barrier, len(everyone))
    summed[head_me] = parts_ref[:, mine]
    send_all(
        "head",
        head_peers,
        lambda peer: parts_ref.at[:, pl.ds(peer * cols, cols)],
        summed.at[head_me],
        send_sems,
        recv_sems,
        0,
    )
    results[req_me] = (mixed_ref[:, mine].astype(jnp.float32) + jnp.sum(summed[...], axis=0)).astype(
        results.dtype
    )
    send_all("req", req_peers, lambda peer: results.at[req_me], results.at[req_me], send_sems, recv_sems, 1)
    wanted = req_me * rows + lax.broadcasted_iota(jnp.int32, (rows, req_count * rows), 0)
    picker = (order_ref[...] == wanted).astype(jnp.bfloat16)
    out_ref[:, mine] = jnp.dot(
        picker, results[...].reshape(req_count * rows, cols), preferred_element_type=jnp.float32
    ).astype(out_ref.dtype)
    send_all("head", head_peers, lambda peer: out_ref.at[:, mine], out_ref.at[:, mine], send_sems, recv_sems, 2)


def tail_exchange(mixed, gain, w_gate, w_up, w_down, order, head_count, req_count, ident):
    rows, width = mixed.shape
    most = max(head_count, req_count)
    return pl.pallas_call(
        functools.partial(tail_kernel, head_count, req_count),
        out_shape=jax.ShapeDtypeStruct((rows, width), jnp.bfloat16),
        in_specs=[pl.BlockSpec(memory_space=pltpu.VMEM)] * 6,
        out_specs=pl.BlockSpec(memory_space=pltpu.VMEM),
        scratch_shapes=[
            pltpu.VMEM((rows, width), jnp.float32),
            pltpu.VMEM((head_count, rows, width // head_count), jnp.float32),
            pltpu.VMEM((req_count, rows, width // head_count), jnp.bfloat16),
            pltpu.SemaphoreType.DMA((3, most)),
            pltpu.SemaphoreType.DMA((3, most)),
        ],
        compiler_params=pltpu.CompilerParams(collective_id=ident, has_side_effects=True),
    )(mixed, gain, w_gate, w_up, w_down, order)


def body(
    req_count,
    head_count,
    hidden,
    deal_order,
    lengths,
    page_table,
    key_cache,
    value_cache,
    attn_gain,
    w_query,
    w_key,
    w_value,
    w_gate,
    w_out,
    query_gain,
    key_gain,
    mlp_gain,
    mlp_gate,
    mlp_up,
    mlp_down,
):
    local_rows, model_width = hidden.shape
    req_index = lax.axis_index("req")
    head_index = lax.axis_index("head")
    all_rows = local_rows * req_count
    head_width = query_gain.shape[0]
    pool_pages, page_size, local_kv = key_cache.shape[:3]
    group_size = w_query.shape[1] // (local_kv * head_width)
    head_cols = local_kv * group_size * head_width
    pairs = local_kv * group_size
    chunk = model_width // head_count
    scale_factor = 1.0 / math.sqrt(head_width)
    first_own = req_index * local_rows

    with jax.named_scope("rotary_tables"):
        half = head_width // 2
        lane_ids = jnp.arange(head_width, dtype=jnp.int32) % half
        frequency = ROPE_BASE ** (-(lane_ids.astype(jnp.float32) * (2.0 / head_width)))

    outs = query_exchange(
        hidden,
        attn_gain.reshape(1, model_width),
        w_query,
        query_gain.reshape(1, head_width),
        w_gate,
        w_value,
        w_key,
        key_gain.reshape(1, head_width),
        frequency.reshape(1, head_width),
        page_table.T,
        lengths.reshape(1, all_rows),
        deal_order.reshape(1, all_rows),
        pool_pages,
        page_size,
        req_count,
        0,
    )
    _, own_queries, gate_logits, new_values, new_keys, owned_f, live_tokens, page_queries = outs
    page_queries = page_queries.reshape(pool_pages, local_kv, group_size, head_width)
    new_values = new_values.reshape(local_rows, local_kv, head_width)
    new_keys = new_keys.reshape(local_rows, local_kv, head_width)

    with jax.named_scope("page_attention"):
        scores = (
            jnp.einsum("pkgd,ptkd->pkgt", page_queries, key_cache, preferred_element_type=jnp.float32)
            * scale_factor
        )
        scores = jnp.where(live_tokens[:, None, None, :] > 0.5, scores, LOW_SCORE)
        page_peaks = jnp.max(scores, axis=-1)
        row_peaks = jnp.max(jnp.where(owned_f[:, :, None, None] > 0.5, page_peaks[:, None], LOW_SCORE), axis=0)
        row_shift = LOG_TWO * jnp.ceil(row_peaks / LOG_TWO)
        page_shift = jnp.max(jnp.where(owned_f[:, :, None, None] > 0.5, row_shift[None], LOW_SCORE), axis=1)
        weights = live_tokens[:, None, None, :] * jnp.exp(scores - page_shift[..., None])
        page_totals = jnp.sum(weights, axis=-1)
        page_numerators = jnp.einsum(
            "pkgt,ptkd->pkgd",
            weights.astype(jnp.bfloat16),
            value_cache,
            preferred_element_type=jnp.float32,
        )
        row_totals = jnp.sum(owned_f[:, :, None, None] * page_totals[:, None], axis=0).reshape(all_rows, pairs)
        row_numerators = jnp.dot(
            owned_f.T.astype(jnp.bfloat16),
            page_numerators.reshape(pool_pages, head_cols).astype(jnp.bfloat16),
            preferred_element_type=jnp.float32,
        )
        numerator_message = row_numerators.astype(jnp.bfloat16).reshape(req_count, local_rows, head_cols)
        stats_message = jnp.concatenate(
            [row_shift.reshape(req_count, local_rows, pairs), row_totals.reshape(req_count, local_rows, pairs)],
            axis=2,
        ).transpose(0, 2, 1)

    mixed_rows = attend_exchange(
        numerator_message,
        stats_message,
        own_queries,
        new_keys.reshape(local_rows, local_kv * head_width),
        new_values.reshape(local_rows, local_kv * head_width),
        gate_logits,
        w_out,
        hidden,
        head_count,
        group_size,
        scale_factor,
        1,
    )

    return tail_exchange(
        mixed_rows,
        mlp_gain.reshape(1, model_width),
        mlp_gate,
        mlp_up,
        mlp_down,
        deal_order.reshape(1, all_rows),
        head_count,
        req_count,
        3,
    )


def solution(mesh):
    return jax.shard_map(
        functools.partial(body, mesh.shape["req"], mesh.shape["head"]),
        mesh=mesh,
        in_specs=(
            P("req", None),
            P(),
            P(),
            P(),
            P("req", None, "head", None),
            P("req", None, "head", None),
            P(),
            P(None, "head"),
            P(None, "head"),
            P(None, "head"),
            P(None, "head"),
            P("head", None),
            P(),
            P(),
            P(),
            P(None, "head"),
            P(None, "head"),
            P("head", None),
        ),
        out_specs=P("req", None),
        check_vma=False,
    )
```

```python
import functools
import math

import jax
import jax.numpy as jnp
from jax import lax
from jax.experimental import pallas as pl
from jax.experimental.pallas import tpu as pltpu
from jax.sharding import PartitionSpec as P

EPSILON = 1e-06
ROPE_BASE = 1000000.0
LOW_SCORE = -1e30
LOG_TWO = math.log(2.0)
MESH_IDS = pl.DeviceIdType.MESH


def rms_inv(values):
    return lax.rsqrt(jnp.mean(values * values, axis=-1, keepdims=True) + EPSILON)


def rotate(values, position):
    half_dim = values.shape[-1] // 2
    exponent = jnp.arange(half_dim, dtype=jnp.float32) * (2.0 / values.shape[-1])
    frequency = ROPE_BASE ** (-exponent)
    angles = position[:, None] * frequency[None, :]
    ones_tail = (1,) * (values.ndim - 2)
    angles = angles.reshape((angles.shape[0],) + ones_tail + (half_dim,))
    cosine = jnp.cos(angles)
    sine_vals = jnp.sin(angles)
    front_half = values[..., :half_dim]
    back_half = values[..., half_dim:]
    return jnp.concatenate(
        [front_half * cosine - back_half * sine_vals, back_half * cosine + front_half * sine_vals],
        axis=-1,
    )


def norm_rotate(values, gain_vec, position):
    return rotate(values * rms_inv(values) * gain_vec, position)


def exchange_kernel(axis, count, spreads, *refs):
    arrays = len(spreads)
    sources, outputs = refs[:arrays], refs[arrays : 2 * arrays]
    send_sems, recv_sems = refs[2 * arrays], refs[2 * arrays + 1]
    me = lax.axis_index(axis)
    barrier = pltpu.get_barrier_semaphore()
    for offset in range(1, count):
        peer = lax.rem(me + offset, count)
        pl.semaphore_signal(barrier, inc=1, device_id={axis: peer}, device_id_type=MESH_IDS)
    pl.semaphore_wait(barrier, count - 1)
    copies = []
    for offset in range(1, count):
        peer = lax.rem(me + offset, count)
        for which in range(arrays):
            src_ref, out_ref = sources[which], outputs[which]
            copy = pltpu.make_async_remote_copy(
                src_ref=src_ref.at[peer] if spreads[which] else src_ref,
                dst_ref=out_ref.at[me],
                send_sem=send_sems.at[which, offset],
                recv_sem=recv_sems.at[which, offset],
                device_id={axis: peer},
                device_id_type=MESH_IDS,
            )
            copy.start()
            copies.append(copy)
    for which in range(arrays):
        src_ref, out_ref = sources[which], outputs[which]
        out_ref[me] = src_ref[me] if spreads[which] else src_ref[...]
    for copy in copies:
        copy.wait()


def exchange_many(arrays, spreads, axis, count, ident):
    shapes = []
    for values, spread in zip(arrays, spreads):
        block = values.shape[1:] if spread else values.shape
        shapes.append(jax.ShapeDtypeStruct((count,) + tuple(block), values.dtype))
    return pl.pallas_call(
        functools.partial(exchange_kernel, axis, count, tuple(spreads)),
        out_shape=tuple(shapes),
        in_specs=[pl.BlockSpec(memory_space=pltpu.VMEM)] * len(arrays),
        out_specs=tuple(pl.BlockSpec(memory_space=pltpu.VMEM) for _ in arrays),
        scratch_shapes=[
            pltpu.SemaphoreType.DMA((len(arrays), count)),
            pltpu.SemaphoreType.DMA((len(arrays), count)),
        ],
        compiler_params=pltpu.CompilerParams(collective_id=ident, has_side_effects=True),
    )(*arrays)


def exchange(values, axis, count, spread, ident):
    return exchange_many((values,), (spread,), axis, count, ident)[0]


def greet(peers):
    barrier = pltpu.get_barrier_semaphore()
    for axis, peer in peers:
        pl.semaphore_signal(barrier, inc=1, device_id={axis: peer}, device_id_type=MESH_IDS)
    pl.semaphore_wait(barrier, len(peers))


def peers_of(axis, count):
    me = lax.axis_index(axis)
    return me, [(offset, lax.rem(me + offset, count)) for offset in range(1, count)]


def send_all(axis, peers, src_of, dst, send_sems, recv_sems, phase):
    copies = []
    for offset, peer in peers:
        copy = pltpu.make_async_remote_copy(
            src_ref=src_of(peer),
            dst_ref=dst,
            send_sem=send_sems.at[phase, offset],
            recv_sem=recv_sems.at[phase, offset],
            device_id={axis: peer},
            device_id_type=MESH_IDS,
        )
        copy.start()
        copies.append(copy)
    for copy in copies:
        copy.wait()


def residual_kernel(count, parts_ref, hidden_ref, out_ref, summed, send_sems, recv_sems):
    me, peers = peers_of("head", count)
    cols = out_ref.shape[1] // count
    mine = pl.ds(pl.multiple_of(me * cols, cols), cols)
    greet([("head", peer) for _, peer in peers])
    summed[me] = parts_ref[:, mine]
    send_all(
        "head", peers, lambda peer: parts_ref.at[:, pl.ds(peer * cols, cols)], summed.at[me], send_sems, recv_sems, 0
    )
    out_ref[:, mine] = (hidden_ref[:, mine].astype(jnp.float32) + jnp.sum(summed[...], axis=0)).astype(
        out_ref.dtype
    )
    send_all("head", peers, lambda peer: out_ref.at[:, mine], out_ref.at[:, mine], send_sems, recv_sems, 1)


def residual_exchange(parts, hidden, count, ident):
    rows, width = parts.shape
    return pl.pallas_call(
        functools.partial(residual_kernel, count),
        out_shape=jax.ShapeDtypeStruct((rows, width), jnp.bfloat16),
        in_specs=[pl.BlockSpec(memory_space=pltpu.VMEM)] * 2,
        out_specs=pl.BlockSpec(memory_space=pltpu.VMEM),
        scratch_shapes=[
            pltpu.VMEM((count, rows, width // count), jnp.float32),
            pltpu.SemaphoreType.DMA((2, count)),
            pltpu.SemaphoreType.DMA((2, count)),
        ],
        compiler_params=pltpu.CompilerParams(collective_id=ident, has_side_effects=True),
    )(parts, hidden)


def rope(values, cosine, sine, swap):
    swapped = jnp.dot(values, swap, precision=lax.Precision.HIGHEST, preferred_element_type=jnp.float32)
    return values * cosine + swapped * sine


def query_kernel(
    count, pool_pages, page_size, hidden_ref, attn_gain_ref, w_query_ref, query_gain_ref, w_gate_ref, w_value_ref,
    w_key_ref, key_gain_ref, frequency_ref, table_ref, lengths_ref, order_ref, out_ref, query_ref, gate_ref,
    value_ref, key_ref, owned_ref, filled_ref, page_query_ref, slot_scratch, send_sems, recv_sems,
):
    me, peers = peers_of("req", count)
    barrier = pltpu.get_barrier_semaphore()
    for _, peer in peers:
        pl.semaphore_signal(barrier, inc=1, device_id={"req": peer}, device_id_type=MESH_IDS)
    head_width = frequency_ref.shape[1]
    rows = query_ref.shape[0]
    requests = order_ref.shape[1]
    request_ids = lax.broadcasted_iota(jnp.int32, (rows, requests), 1)
    own_rows = me * rows + lax.broadcasted_iota(jnp.int32, (rows, requests), 0)
    own_requests = jnp.sum(jnp.where(request_ids == own_rows, order_ref[...], 0), axis=1, keepdims=True)
    position = jnp.sum(jnp.where(request_ids == own_requests, lengths_ref[...], 0), axis=1, keepdims=True)
    angles = position.astype(jnp.float32) * frequency_ref[...]
    cos_ref = jnp.cos(angles)
    sin_ref = jnp.sin(angles)
    lanes_in = lax.broadcasted_iota(jnp.int32, (head_width, head_width), 0)
    lanes_out = lax.broadcasted_iota(jnp.int32, (head_width, head_width), 1)
    swap = jnp.where(
        lanes_in == lax.rem(lanes_out + head_width // 2, head_width),
        jnp.where(lanes_out < head_width // 2, -1.0, 1.0),
        0.0,
    ).astype(jnp.float32)
    hidden = hidden_ref[...].astype(jnp.float32)
    normed = (hidden * rms_inv(hidden) * attn_gain_ref[...]).astype(jnp.bfloat16)
    queries = jnp.dot(normed, w_query_ref[...], preferred_element_type=jnp.float32)
    for pair in range(queries.shape[1] // head_width):
        lanes = slice(pair * head_width, (pair + 1) * head_width)
        query = queries[:, lanes]
        query = query * rms_inv(query) * query_gain_ref[...]
        query_ref[:, lanes] = rope(query, cos_ref, sin_ref, swap).astype(query_ref.dtype)
    pl.semaphore_wait(barrier, len(peers))
    copies = []
    for offset, peer in peers:
        copy = pltpu.make_async_remote_copy(
            src_ref=query_ref,
            dst_ref=out_ref.at[me],
            send_sem=send_sems.at[offset],
            recv_sem=recv_sems.at[offset],
            device_id={"req": peer},
            device_id_type=MESH_IDS,
        )
        copy.start()
        copies.append(copy)
    out_ref[me] = query_ref[...]
    gate_ref[...] = jnp.dot(normed, w_gate_ref[...], preferred_element_type=jnp.float32)
    value_ref[...] = jnp.dot(normed, w_value_ref[...], preferred_element_type=jnp.float32).astype(value_ref.dtype)
    keys = jnp.dot(normed, w_key_ref[...], preferred_element_type=jnp.float32)
    for kv in range(keys.shape[1] // head_width):
        lanes = slice(kv * head_width, (kv + 1) * head_width)
        key = keys[:, lanes]
        key = key * rms_inv(key) * key_gain_ref[...]
        key_ref[:, lanes] = rope(key, cos_ref, sin_ref, swap).astype(key_ref.dtype)
    slots, requests = table_ref.shape
    slot_ids = lax.broadcasted_iota(jnp.int32, (slots, requests), 0)
    lengths = lengths_ref[...]
    local_ids = table_ref[...] - me * pool_pages
    usable = (slot_ids < (lengths + page_size - 1) // page_size) & (local_ids >= 0) & (local_ids < pool_pages)
    keyed = jnp.where(usable, local_ids, pool_pages)
    slot_f = slot_ids.astype(jnp.float32)

    def one_page(page, carry):
        hit = keyed == page
        owned_ref[pl.ds(page, 1), :] = jnp.max(jnp.where(hit, 1.0, 0.0), axis=0, keepdims=True)
        slot_scratch[pl.ds(page, 1), :] = jnp.sum(jnp.where(hit, slot_f, 0.0), axis=0, keepdims=True)
        return carry

    lax.fori_loop(0, pool_pages, one_page, 0)
    owned_requests = owned_ref[...]
    owner_slot = jnp.sum(slot_scratch[...], axis=1, keepdims=True)
    owner_length = jnp.sum(owned_requests * lengths.astype(jnp.float32), axis=1, keepdims=True)
    filled = jnp.clip(owner_length - owner_slot * page_size, 0.0, float(page_size))
    filled = jnp.where(jnp.max(owned_requests, axis=1, keepdims=True) > 0.5, filled, 0.0)
    tokens = lax.broadcasted_iota(jnp.int32, filled_ref.shape, 1).astype(jnp.float32)
    filled_ref[...] = jnp.where(tokens < filled, 1.0, 0.0)
    dealing = (lax.broadcasted_iota(jnp.int32, (requests, requests), 0) == order_ref[...]).astype(jnp.bfloat16)
    owned_rows = jnp.dot(owned_requests.astype(jnp.bfloat16), dealing, preferred_element_type=jnp.float32)
    owned_ref[...] = jnp.where(owned_rows > 0.5, 1.0, 0.0)
    for copy in copies:
        copy.wait()
    rows = query_ref.shape[0]
    page_query_ref[...] = jnp.dot(
        owned_ref[...].astype(jnp.bfloat16),
        out_ref[...].reshape(count * rows, query_ref.shape[1]),
        preferred_element_type=jnp.float32,
    ).astype(page_query_ref.dtype)


def query_exchange(
    hidden, attn_gain, w_query, query_gain, w_gate, w_value, w_key, key_gain, frequency, table, lengths, order,
    pool_pages, page_size, count, ident,
):
    rows = hidden.shape[0]
    requests = table.shape[1]
    return pl.pallas_call(
        functools.partial(query_kernel, count, pool_pages, page_size),
        out_shape=(
            jax.ShapeDtypeStruct((count, rows, w_query.shape[1]), jnp.bfloat16),
            jax.ShapeDtypeStruct((rows, w_query.shape[1]), jnp.bfloat16),
            jax.ShapeDtypeStruct((rows, w_gate.shape[1]), jnp.float32),
            jax.ShapeDtypeStruct((rows, w_value.shape[1]), jnp.bfloat16),
            jax.ShapeDtypeStruct((rows, w_key.shape[1]), jnp.bfloat16),
            jax.ShapeDtypeStruct((pool_pages, requests), jnp.float32),
            jax.ShapeDtypeStruct((pool_pages, page_size), jnp.float32),
            jax.ShapeDtypeStruct((pool_pages, w_query.shape[1]), jnp.bfloat16),
        ),
        in_specs=[pl.BlockSpec(memory_space=pltpu.VMEM)] * 12,
        out_specs=tuple(pl.BlockSpec(memory_space=pltpu.VMEM) for _ in range(8)),
        scratch_shapes=[
            pltpu.VMEM((pool_pages, requests), jnp.float32),
            pltpu.SemaphoreType.DMA((count,)),
            pltpu.SemaphoreType.DMA((count,)),
        ],
        compiler_params=pltpu.CompilerParams(collective_id=ident, has_side_effects=True),
    )(hidden, attn_gain, w_query, query_gain, w_gate, w_value, w_key, key_gain, frequency, table, lengths, order)


def attend_kernel(
    req_count, head_count, group_size, scale_factor, num_ref, stats_ref, query_ref, key_ref, value_ref, gate_ref,
    w_out_ref, hidden_ref, out_ref, got_num, got_stats, projected, summed, send_sems, recv_sems,
):
    req_me, req_peers = peers_of("req", req_count)
    head_me, head_peers = peers_of("head", head_count)
    rows, width = out_ref.shape
    cols = width // head_count
    pairs = stats_ref.shape[1] // 2
    head_width = query_ref.shape[1] // pairs
    mine = pl.ds(pl.multiple_of(head_me * cols, cols), cols)
    greet([("req", peer) for _, peer in req_peers] + [("head", peer) for _, peer in head_peers])
    got_num[req_me] = num_ref[req_me]
    got_stats[req_me] = stats_ref[req_me]
    copies = []
    for offset, peer in req_peers:
        for which, (src_ref, dst_ref) in enumerate(((num_ref, got_num), (stats_ref, got_stats))):
            copy = pltpu.make_async_remote_copy(
                src_ref=src_ref.at[peer],
                dst_ref=dst_ref.at[req_me],
                send_sem=send_sems.at[which, offset],
                recv_sem=recv_sems.at[which, offset],
                device_id={"req": peer},
                device_id_type=MESH_IDS,
            )
            copy.start()
            copies.append(copy)
    for copy in copies:
        copy.wait()
    eye = (
        lax.broadcasted_iota(jnp.int32, (rows, rows), 0) == lax.broadcasted_iota(jnp.int32, (rows, rows), 1)
    ).astype(jnp.float32)
    flip = (((1,), (1,)), ((), ()))
    heads = []
    for pair in range(pairs):
        kv = pair // group_size
        lanes = slice(pair * head_width, (pair + 1) * head_width)
        kv_lanes = slice(kv * head_width, (kv + 1) * head_width)
        shifts = lax.dot_general(
            eye, got_stats[:, pair, :], flip, precision=lax.Precision.HIGHEST, preferred_element_type=jnp.float32
        )
        totals = lax.dot_general(
            eye,
            got_stats[:, pairs + pair, :],
            flip,
            precision=lax.Precision.HIGHEST,
            preferred_element_type=jnp.float32,
        )
        query = query_ref[:, lanes].astype(jnp.float32)
        self_score = jnp.sum(query * key_ref[:, kv_lanes].astype(jnp.float32), axis=1, keepdims=True) * scale_factor
        self_shift = LOG_TWO * jnp.ceil(self_score / LOG_TWO)
        shift = jnp.maximum(jnp.max(shifts, axis=1, keepdims=True), self_shift)
        factor = jnp.exp(shifts - shift)
        self_weight = jnp.exp(self_score - shift)
        total = jnp.sum(totals * factor, axis=1, keepdims=True) + self_weight
        acc = self_weight.astype(jnp.bfloat16).astype(jnp.float32) * value_ref[:, kv_lanes].astype(jnp.float32)
        for source in range(req_count):
            acc = acc + factor[:, source : source + 1] * got_num[source, :, lanes].astype(jnp.float32)
        heads.append(acc / total)
    heads_out = jnp.concatenate(heads, axis=1)
    gate = gate_ref[...]
    attended = (heads_out * (1.0 / (1.0 + jnp.exp(-gate)))).astype(jnp.bfloat16)
    projected[...] = jnp.dot(attended, w_out_ref[...], preferred_element_type=jnp.float32)
    summed[head_me] = projected[:, mine]
    send_all(
        "head", head_peers, lambda peer: projected.at[:, pl.ds(peer * cols, cols)], summed.at[head_me],
        send_sems, recv_sems, 2,
    )
    out_ref[:, mine] = (hidden_ref[:, mine].astype(jnp.float32) + jnp.sum(summed[...], axis=0)).astype(
        out_ref.dtype
    )
    send_all("head", head_peers, lambda peer: out_ref.at[:, mine], out_ref.at[:, mine], send_sems, recv_sems, 3)


def attend_exchange(
    num, stats, queries, keys, values, gate, w_out, hidden, head_count, group_size, scale_factor, ident
):
    req_count = num.shape[0]
    rows, width = hidden.shape
    most = max(head_count, req_count)
    return pl.pallas_call(
        functools.partial(attend_kernel, req_count, head_count, group_size, scale_factor),
        out_shape=jax.ShapeDtypeStruct((rows, width), jnp.bfloat16),
        in_specs=[pl.BlockSpec(memory_space=pltpu.VMEM)] * 8,
        out_specs=pl.BlockSpec(memory_space=pltpu.VMEM),
        scratch_shapes=[
            pltpu.VMEM(num.shape, num.dtype),
            pltpu.VMEM(stats.shape, stats.dtype),
            pltpu.VMEM((rows, width), jnp.float32),
            pltpu.VMEM((head_count, rows, width // head_count), jnp.float32),
            pltpu.SemaphoreType.DMA((4, most)),
            pltpu.SemaphoreType.DMA((4, most)),
        ],
        compiler_params=pltpu.CompilerParams(collective_id=ident, has_side_effects=True),
    )(num, stats, queries, keys, values, gate, w_out, hidden)


def tail_kernel(
    head_count, req_count, mixed_ref, gain_ref, w_gate_ref, w_up_ref, w_down_ref, order_ref, out_ref, parts_ref,
    summed, results, send_sems, recv_sems,
):
    head_me, head_peers = peers_of("head", head_count)
    req_me, req_peers = peers_of("req", req_count)
    rows, width = out_ref.shape
    cols = width // head_count
    mine = pl.ds(pl.multiple_of(head_me * cols, cols), cols)
    barrier = pltpu.get_barrier_semaphore()
    everyone = [("head", peer) for _, peer in head_peers] + [("req", peer) for _, peer in req_peers]
    for axis, peer in everyone:
        pl.semaphore_signal(barrier, inc=1, device_id={axis: peer}, device_id_type=MESH_IDS)
    mixed = mixed_ref[...].astype(jnp.float32)
    normed = (mixed * rms_inv(mixed) * gain_ref[...]).astype(jnp.bfloat16)
    gate_part = jnp.dot(normed, w_gate_ref[...], preferred_element_type=jnp.float32)
    up_part = jnp.dot(normed, w_up_ref[...], preferred_element_type=jnp.float32)
    inner_act = (gate_part / (1.0 + jnp.exp(-gate_part)) * up_part).astype(jnp.bfloat16)
    parts_ref[...] = jnp.dot(inner_act, w_down_ref[...], preferred_element_type=jnp.float32)
    summed[head_me] = parts_ref[:, mine]
    wanted = req_me * rows + lax.broadcasted_iota(jnp.int32, (rows, req_count * rows), 0)
    picker = (order_ref[...] == wanted).astype(jnp.bfloat16)
    pl.semaphore_wait(barrier, len(everyone))
    send_all(
        "head",
        head_peers,
        lambda peer: parts_ref.at[:, pl.ds(peer * cols, cols)],
        summed.at[head_me],
        send_sems,
        recv_sems,
        0,
    )
    results[req_me] = (mixed_ref[:, mine].astype(jnp.float32) + jnp.sum(summed[...], axis=0)).astype(
        results.dtype
    )
    send_all("req", req_peers, lambda peer: results.at[req_me], results.at[req_me], send_sems, recv_sems, 1)
    out_ref[:, mine] = jnp.dot(
        picker, results[...].reshape(req_count * rows, cols), preferred_element_type=jnp.float32
    ).astype(out_ref.dtype)
    send_all("head", head_peers, lambda peer: out_ref.at[:, mine], out_ref.at[:, mine], send_sems, recv_sems, 2)


def tail_exchange(mixed, gain, w_gate, w_up, w_down, order, head_count, req_count, ident):
    rows, width = mixed.shape
    most = max(head_count, req_count)
    return pl.pallas_call(
        functools.partial(tail_kernel, head_count, req_count),
        out_shape=jax.ShapeDtypeStruct((rows, width), jnp.bfloat16),
        in_specs=[pl.BlockSpec(memory_space=pltpu.VMEM)] * 6,
        out_specs=pl.BlockSpec(memory_space=pltpu.VMEM),
        scratch_shapes=[
            pltpu.VMEM((rows, width), jnp.float32),
            pltpu.VMEM((head_count, rows, width // head_count), jnp.float32),
            pltpu.VMEM((req_count, rows, width // head_count), jnp.bfloat16),
            pltpu.SemaphoreType.DMA((3, most)),
            pltpu.SemaphoreType.DMA((3, most)),
        ],
        compiler_params=pltpu.CompilerParams(collective_id=ident, has_side_effects=True),
    )(mixed, gain, w_gate, w_up, w_down, order)


def body(
    req_count,
    head_count,
    hidden,
    deal_order,
    lengths,
    page_table,
    key_cache,
    value_cache,
    attn_gain,
    w_query,
    w_key,
    w_value,
    w_gate,
    w_out,
    query_gain,
    key_gain,
    mlp_gain,
    mlp_gate,
    mlp_up,
    mlp_down,
):
    local_rows, model_width = hidden.shape
    req_index = lax.axis_index("req")
    head_index = lax.axis_index("head")
    all_rows = local_rows * req_count
    head_width = query_gain.shape[0]
    pool_pages, page_size, local_kv = key_cache.shape[:3]
    group_size = w_query.shape[1] // (local_kv * head_width)
    head_cols = local_kv * group_size * head_width
    pairs = local_kv * group_size
    chunk = model_width // head_count
    scale_factor = 1.0 / math.sqrt(head_width)
    first_own = req_index * local_rows

    with jax.named_scope("rotary_tables"):
        half = head_width // 2
        lane_ids = jnp.arange(head_width, dtype=jnp.int32) % half
        frequency = ROPE_BASE ** (-(lane_ids.astype(jnp.float32) * (2.0 / head_width)))

    outs = query_exchange(
        hidden,
        attn_gain.reshape(1, model_width),
        w_query,
        query_gain.reshape(1, head_width),
        w_gate,
        w_value,
        w_key,
        key_gain.reshape(1, head_width),
        frequency.reshape(1, head_width),
        page_table.T,
        lengths.reshape(1, all_rows),
        deal_order.reshape(1, all_rows),
        pool_pages,
        page_size,
        req_count,
        0,
    )
    _, own_queries, gate_logits, new_values, new_keys, owned_f, live_tokens, page_queries = outs
    page_queries = page_queries.reshape(pool_pages, local_kv, group_size, head_width)
    new_values = new_values.reshape(local_rows, local_kv, head_width)
    new_keys = new_keys.reshape(local_rows, local_kv, head_width)

    with jax.named_scope("page_attention"):
        scores = (
            jnp.einsum("pkgd,ptkd->pkgt", page_queries, key_cache, preferred_element_type=jnp.float32)
            * scale_factor
        )
        scores = jnp.where(live_tokens[:, None, None, :] > 0.5, scores, LOW_SCORE)
        page_peaks = jnp.max(scores, axis=-1)
        row_peaks = jnp.max(jnp.where(owned_f[:, :, None, None] > 0.5, page_peaks[:, None], LOW_SCORE), axis=0)
        row_shift = LOG_TWO * jnp.ceil(row_peaks / LOG_TWO)
        page_shift = jnp.max(jnp.where(owned_f[:, :, None, None] > 0.5, row_shift[None], LOW_SCORE), axis=1)
        weights = live_tokens[:, None, None, :] * jnp.exp(scores - page_shift[..., None])
        page_totals = jnp.sum(weights, axis=-1)
        page_numerators = jnp.einsum(
            "pkgt,ptkd->pkgd",
            weights.astype(jnp.bfloat16),
            value_cache,
            preferred_element_type=jnp.float32,
        )
        row_totals = jnp.sum(owned_f[:, :, None, None] * page_totals[:, None], axis=0).reshape(all_rows, pairs)
        row_numerators = jnp.dot(
            owned_f.T.astype(jnp.bfloat16),
            page_numerators.reshape(pool_pages, head_cols).astype(jnp.bfloat16),
            preferred_element_type=jnp.float32,
        )
        numerator_message = row_numerators.astype(jnp.bfloat16).reshape(req_count, local_rows, head_cols)
        stats_message = jnp.concatenate(
            [row_shift.reshape(req_count, local_rows, pairs), row_totals.reshape(req_count, local_rows, pairs)],
            axis=2,
        ).transpose(0, 2, 1)

    mixed_rows = attend_exchange(
        numerator_message,
        stats_message,
        own_queries,
        new_keys.reshape(local_rows, local_kv * head_width),
        new_values.reshape(local_rows, local_kv * head_width),
        gate_logits,
        w_out,
        hidden,
        head_count,
        group_size,
        scale_factor,
        1,
    )

    return tail_exchange(
        mixed_rows,
        mlp_gain.reshape(1, model_width),
        mlp_gate,
        mlp_up,
        mlp_down,
        deal_order.reshape(1, all_rows),
        head_count,
        req_count,
        3,
    )


def solution(mesh):
    return jax.shard_map(
        functools.partial(body, mesh.shape["req"], mesh.shape["head"]),
        mesh=mesh,
        in_specs=(
            P("req", None),
            P(),
            P(),
            P(),
            P("req", None, "head", None),
            P("req", None, "head", None),
            P(),
            P(None, "head"),
            P(None, "head"),
            P(None, "head"),
            P(None, "head"),
            P("head", None),
            P(),
            P(),
            P(),
            P(None, "head"),
            P(None, "head"),
            P("head", None),
        ),
        out_specs=P("req", None),
        check_vma=False,
    )
```
